128 devices in a mesh: row: 8 (over y_lo, z), col: 16 (over x, y_hi, core).
Axes of the slice: x: 4, y: 4 (y_hi: 2, y_lo: 2; y = y_hi * 2 + y_lo), z: 4, core: 2. Of those that a mesh axis runs over, the one named last changes fastest.
Arguments:
- queries: bfloat16 [16384, 512], P(('row', 'col')), may hold values from -6 to 6
- keys: bfloat16 [16384, 512], P(('row', 'col')), may hold values from -6 to 6
- fwd_table: bfloat16 [256, 16384], P(('row', 'col')), may hold values from 0.0099487305 to 1
- bwd_table: bfloat16 [256, 16384], P(('row', 'col')), may hold values from 0.0099487305 to 1
- step_weight: float32 [256], P(('row', 'col')), may hold values from 1000 to 6000
- block_order: int32 [512], replicated, may hold values from 0 to 511, each once
Outputs:
- query_grad: float32 [16384, 512], P(('row', 'col'))
- key_grad: float32 [16384, 512], P(('row', 'col'))
The draws below stay inside these ranges and needn't reach their ends.
Inputs may be any that keep to these rules, and one draw needn't show every extreme that they name: `block_order`: each value occurs exactly once.
All inputs are finite; a program needn't handle non-finite values.
Results may differ from the reference program's by a relative error of at most 0.01.
Values may be sent and summed in bfloat16 or wider, within the bound.
A program may use at most 192 MiB of HBM per device.

```python
import math
import jax
import jax.numpy as jnp
from jax import lax

HEADS = 8
HEAD = 64
STEPS = 256
GRAIN = 32
VERTS = 16384


def vertex_pair(key):
    width = HEADS * HEAD
    key_q = jax.random.fold_in(key, 101)
    key_k = jax.random.fold_in(key, 202)
    queries = jnp.clip(jax.random.normal(key_q, (VERTS, width), jnp.float32), -6.0, 6.0)
    keys = jnp.clip(jax.random.normal(key_k, (VERTS, width), jnp.float32), -6.0, 6.0)
    return (queries, keys)


def draw_queries(key, part):
    return vertex_pair(key)[0].astype(jnp.bfloat16)


def draw_keys(key, part):
    return vertex_pair(key)[1].astype(jnp.bfloat16)


def steps_of(stream_key, shape, pieces, smallest, largest):
    factor_of, own = 1.0, jax.random.fold_in(stream_key, 6)
    for dim, blocks in pieces:
        steps = jnp.exp(jax.random.uniform(jax.random.fold_in(own, dim), (blocks,), jnp.float32, smallest / len(pieces), largest / len(pieces)))
        factor_of = factor_of * jnp.repeat(steps, shape[dim] // blocks).reshape([-1 if axis == dim else 1 for axis in range(len(shape))])
    return factor_of


def setup_inputs(seed: int = 0) -> dict:
    key_of = jax.random.split(jax.random.key(seed), 7)
    return {
        "queries": draw_queries(jax.random.fold_in(key_of[6], 71), 0),
        "keys": draw_keys(jax.random.fold_in(key_of[6], 71), 0),
        "fwd_table": jnp.clip(jnp.exp(math.log(1.0) - 4.61031033 * jax.random.uniform(key_of[2], (STEPS, VERTS), jnp.float32) ** steps_of(key_of[2], (STEPS, VERTS), ((0, 128),), -0.2, 0.2)), 0.0099487305, 1.0).astype(jnp.bfloat16),
        "bwd_table": jnp.clip(jnp.exp(math.log(1.0) - 4.61031033 * jax.random.uniform(key_of[3], (STEPS, VERTS), jnp.float32) ** steps_of(key_of[3], (STEPS, VERTS), ((0, 128),), -0.2, 0.2)), 0.0099487305, 1.0).astype(jnp.bfloat16),
        "step_weight": jnp.clip(jnp.exp(math.log(6000.0) - 1.7917595 * jax.random.uniform(key_of[4], (STEPS,), jnp.float32) ** steps_of(key_of[4], (STEPS,), ((0, 128),), -0.2, 0.2)), 1000.0, 6000.0),
        "block_order": jax.random.permutation(key_of[5], VERTS // GRAIN).astype(jnp.int32),
    }


NEG = -1.0e30


def reference(queries, keys, fwd_table, bwd_table, step_weight, block_order):
    verts = queries.shape[0]
    width = queries.shape[1]
    scale = HEAD ** -0.5
    offsets = jnp.arange(GRAIN, dtype=jnp.int32)
    positions = ((block_order * GRAIN)[:, None] + offsets[None, :]).reshape(verts).astype(jnp.int32)
    scaled = (bwd_table.astype(jnp.float32) * step_weight[:, None]).astype(jnp.bfloat16)
    rows = 512 if verts % 512 == 0 else verts
    blocks = verts // rows

    def step(key_acc, index):
        start = (index * rows).astype(jnp.int32)
        fwd_rows = lax.dynamic_slice_in_dim(fwd_table, start, rows, 1)
        counts = lax.dot_general(fwd_rows, scaled, (((0,), (0,)), ((), ())), preferred_element_type=jnp.float32)
        q_rows = lax.dynamic_slice_in_dim(queries, start, rows, 0)
        pos_rows = lax.dynamic_slice_in_dim(positions, start, rows, 0)
        valid = pos_rows[:, None] <= positions[None, :]
        q_terms = []
        k_terms = []
        for head in range(HEADS):
            q_part = q_rows[:, head * HEAD:(head + 1) * HEAD]
            k_part = keys[:, head * HEAD:(head + 1) * HEAD]
            raw = lax.dot_general(q_part, k_part, (((1,), (1,)), ((), ())), preferred_element_type=jnp.float32) * scale
            scores = jnp.where(valid, raw, NEG)
            top = jnp.max(scores, axis=1, keepdims=True)
            weights = jnp.where(valid, jnp.exp(scores - top), 0.0)
            total = jnp.sum(weights, axis=1, keepdims=True)
            expected = jnp.sum(weights * counts, axis=1, keepdims=True)
            grad = ((weights / total) * (expected / total - counts) / HEADS).astype(jnp.bfloat16)
            q_terms.append(jnp.dot(grad, k_part, preferred_element_type=jnp.float32) * scale)
            k_terms.append(lax.dot_general(grad, q_part, (((0,), (0,)), ((), ())), preferred_element_type=jnp.float32) * scale)
        return key_acc + jnp.concatenate(k_terms, axis=1), jnp.concatenate(q_terms, axis=1)

    key_grad, q_blocks = lax.scan(step, jnp.zeros((verts, width), jnp.float32), jnp.arange(blocks, dtype=jnp.int32))
    return q_blocks.reshape(verts, width), key_grad
```

```python
import jax
import jax.numpy as jnp
from jax import lax
from jax.experimental import pallas as pl
from jax.experimental.pallas import tpu as pltpu
from jax.sharding import PartitionSpec as P

HEADS = 8
HEAD = 64
GRAIN = 32
SCALE = HEAD**-0.5
LOG_HEADS = 2.0794415416798357
NEG = -1e30
UB = 256
VC = 256
MESH = pl.DeviceIdType.MESH
VM = pl.BlockSpec(memory_space=pltpu.VMEM)
SM = pl.BlockSpec(memory_space=pltpu.SMEM)


def nn(a, b):
    return lax.dot_general(a, b, (((1,), (0,)), ((), ())), preferred_element_type=jnp.float32)


def nt(a, b):
    return lax.dot_general(a, b, (((1,), (1,)), ((), ())), preferred_element_type=jnp.float32)


def remote(src, dst, send, recv, peer):
    return pltpu.make_async_remote_copy(
        src_ref=src, dst_ref=dst, send_sem=send, recv_sem=recv, device_id=peer, device_id_type=MESH
    )


def enter(peers):
    barrier = pltpu.get_barrier_semaphore()
    for peer in peers:
        pl.semaphore_signal(barrier, inc=1, device_id=peer, device_id_type=MESH)
    pl.semaphore_wait(barrier, len(peers))


class Sends:
    def __init__(self, sems):
        self.sems = sems
        self.started = []

    def start(self, src, dst, recv, peer):
        copy = remote(src, dst, self.sems.at[len(self.started)], recv, peer)
        copy.start()
        self.started.append(copy)

    def drain(self):
        for copy in self.started:
            copy.wait_send()


def gather_kernel(q, k, sf, sb, qa, ka, fa, ba, send, recv_q, recv_f, recv_k, recv_b, in_f, in_b, own):
    row, col = lax.axis_index("row"), lax.axis_index("col")
    x, yh, core = col // 4, (col // 2) % 2, col % 2
    yl, z = row // 4, row % 4

    def at(r=None, c=None):
        return {"row": row if r is None else r, "col": col if c is None else c}

    def cslot(xx, yy, cc):
        return xx * 4 + yy * 2 + cc

    enter(
        [at(r=(row + d) % 8) for d in range(1, 8)] + [at(c=(col + d) % 16) for d in range(1, 16)]
    )
    sends = Sends(send)
    local = [
        pltpu.make_async_copy(q, qa.at[col], own.at[0]),
        pltpu.make_async_copy(k, ka.at[row], own.at[1]),
        pltpu.make_async_copy(sf.at[row], fa.at[:, col, row], own.at[2]),
        pltpu.make_async_copy(sb.at[:, col], ba.at[:, col, row], own.at[3]),
    ]
    for copy in local:
        copy.start()
    for d in range(1, 8):
        to = (row + d) % 8
        sends.start(sf.at[to], fa.at[:, col, row], in_f.at[row], at(r=to))
    for d in range(1, 16):
        to = (col + d) % 16
        sends.start(sb.at[:, to], ba.at[:, col, row], in_b.at[col], at(c=to))

    def q_part(slot, half=None):
        return qa.at[slot] if half is None else qa.at[slot, pl.ds(half * 64, 64)]

    def f_part(slot, half=None):
        return fa.at[:, slot] if half is None else fa.at[pl.ds(half * 8, 8), slot]

    def k_part(slot, half=None):
        return ka.at[slot] if half is None else ka.at[slot, pl.ds(half * 64, 64)]

    def b_part(slot, half=None):
        return ba.at[:, :, slot] if half is None else ba.at[pl.ds(half * 4, 4), :, slot]

    def src_slot(dx, dy, cc=None):
        return cslot((x + dx) % 4, (yh + dy) % 2, core if cc is None else cc)

    def tgt_slot(dz, dy):
        return ((yl + dy) % 2) * 4 + (z + dz) % 4

    def src_dev(dx, dy, dc=0):
        return at(c=cslot((x + dx) % 4, (yh + dy) % 2, (core + dc) % 2))

    def tgt_dev(dz, dy):
        return at(r=tgt_slot(dz, dy))

    source = (src_slot, src_dev, True)
    target = (tgt_slot, tgt_dev, False)
    streams = {
        "q": (q_part, recv_q, source),
        "f": (f_part, recv_f, source),
        "k": (k_part, recv_k, target),
        "b": (b_part, recv_b, target),
    }

    def push(kind, slot, peer, half=None):
        part, recv, _ = streams[kind]
        ref = part(slot, half)
        sends.start(ref, ref, recv.at[slot, 0 if half is None else half], peer)

    def arrived(kind, slot, half=None):
        part, recv, _ = streams[kind]
        ref = part(slot, half)
        remote(ref, ref, send.at[0], recv.at[slot, 0 if half is None else half], at()).wait_recv()

    def first(kind):
        slot_of, dev_of, pair = streams[kind][2]
        mine = slot_of(0, 0)
        push(kind, mine, dev_of(0, 1))
        push(kind, mine, dev_of(1, 0))
        push(kind, mine, dev_of(3, 0))
        if pair:
            push(kind, mine, dev_of(0, 0, 1))

    def second(kind):
        slot_of, dev_of, pair = streams[kind][2]
        other = slot_of(0, 1)
        arrived(kind, other)
        push(kind, other, dev_of(1, 0))
        push(kind, other, dev_of(3, 0))
        if pair:
            push(kind, other, dev_of(0, 0, 1))

    def relay(kind, dy):
        slot_of, dev_of, pair = streams[kind][2]
        for step, half in ((3, 0), (1, 1)):
            slot = slot_of(step, dy)
            arrived(kind, slot)
            push(kind, slot, dev_of(4 - step, 0), half)
            if pair:
                push(kind, slot, dev_of(0, 0, 1))

    def last(kind, dy):
        slot_of, dev_of, pair = streams[kind][2]
        slot = slot_of(2, dy)
        arrived(kind, slot, 0)
        arrived(kind, slot, 1)
        if pair:
            push(kind, slot, dev_of(0, 0, 1))

    local[0].wait()
    local[1].wait()
    first("q")
    first("k")
    local[2].wait()
    for d in range(1, 8):
        frm = (row + d) % 8
        ref = fa.at[:, col, frm]
        remote(ref, ref, send.at[0], in_f.at[frm], at()).wait_recv()
    first("f")
    local[3].wait()
    for d in range(1, 16):
        frm = (col + d) % 16
        ref = ba.at[:, frm, row]
        remote(ref, ref, send.at[0], in_b.at[frm], at()).wait_recv()
    first("b")
    second("k")
    second("q")
    relay("k", 0)
    relay("q", 0)
    second("b")
    second("f")
    relay("k", 1)
    relay("q", 1)
    relay("b", 0)
    relay("f", 0)
    relay("b", 1)
    relay("f", 1)
    for kind in ("k", "q", "b", "f"):
        last(kind, 0)
        last(kind, 1)
    for kind in ("q", "f"):
        for dx in range(4):
            for dy in range(2):
                arrived(kind, src_slot(dx, dy, 1 - core))
    sends.drain()


def gather(q, k, sf, sb):
    bf = jnp.bfloat16
    return pl.pallas_call(
        gather_kernel,
        in_specs=[VM] * 4,
        out_specs=[VM] * 4,
        out_shape=[
            jax.ShapeDtypeStruct((16, 128, 512), bf),
            jax.ShapeDtypeStruct((8, 128, 512), bf),
            jax.ShapeDtypeStruct((16, 16, 8, 2, 128), bf),
            jax.ShapeDtypeStruct((8, 16, 8, 2, 128), bf),
        ],
        scratch_shapes=[
            pltpu.SemaphoreType.DMA((100,)),
            pltpu.SemaphoreType.DMA((16, 2)),
            pltpu.SemaphoreType.DMA((16, 2)),
            pltpu.SemaphoreType.DMA((8, 2)),
            pltpu.SemaphoreType.DMA((8, 2)),
            pltpu.SemaphoreType.DMA((8,)),
            pltpu.SemaphoreType.DMA((16,)),
            pltpu.SemaphoreType.DMA((4,)),
        ],
        compiler_params=pltpu.CompilerParams(
            collective_id=0, has_side_effects=True, vmem_limit_bytes=40 << 20
        ),
        name="gather",
    )(q, k, sf, sb)


def merge_kernel(part, out, landed, mine, send, recv, recv2, own):
    row, col = lax.axis_index("row"), lax.axis_index("col")
    peers = [{"row": row, "col": (col + d) % 16} for d in range(1, 16)]
    enter(peers)
    sends = Sends(send)
    keep = pltpu.make_async_copy(part.at[col], landed.at[col], own.at[0])
    keep.start()
    for d, peer in enumerate(peers):
        sends.start(part.at[peer["col"]], landed.at[col], recv.at[col], peer)
    keep.wait()
    for peer in peers:
        ref = landed.at[peer["col"]]
        remote(ref, ref, send.at[0], recv.at[peer["col"]], peer).wait_recv()
    logs = landed[:, 0:8]
    top = jnp.max(logs, axis=0)
    weight = jnp.exp(logs - top[None])
    total = jnp.sum(weight, axis=0)
    mean = jnp.sum(weight * landed[:, 8:16], axis=0) / total
    mine[0:8, :] = top + jnp.log(total) + LOG_HEADS
    mine[8:16, :] = mean
    keep = pltpu.make_async_copy(mine, out.at[col], own.at[1])
    keep.start()
    for peer in peers:
        sends.start(mine, out.at[col], recv2.at[col], peer)
    keep.wait()
    for peer in peers:
        ref = out.at[peer["col"]]
        remote(ref, ref, send.at[0], recv2.at[peer["col"]], peer).wait_recv()
    sends.drain()


def merge(part):
    return pl.pallas_call(
        merge_kernel,
        in_specs=[VM],
        out_specs=VM,
        out_shape=jax.ShapeDtypeStruct((16, 16, 128), jnp.float32),
        scratch_shapes=[
            pltpu.VMEM((16, 16, 128), jnp.float32),
            pltpu.VMEM((16, 128), jnp.float32),
            pltpu.SemaphoreType.DMA((30,)),
            pltpu.SemaphoreType.DMA((16,)),
            pltpu.SemaphoreType.DMA((16,)),
            pltpu.SemaphoreType.DMA((2,)),
        ],
        compiler_params=pltpu.CompilerParams(collective_id=1, has_side_effects=True),
        name="merge",
    )(part)


def reduce_kernel(qp, kp, qo, ko, pair_in, pair_sum, ring_q, ring_k, out_q, out_k, last_q, last_k, send, recv):
    row, col = lax.axis_index("row"), lax.axis_index("col")
    x, yh, core = col // 4, (col // 2) % 2, col % 2
    yl, z = row // 4, row % 4

    def q_dev(xx, yy, cc):
        return {"row": row, "col": xx * 4 + yy * 2 + cc}

    def k_dev(yy, zz):
        return {"row": yy * 4 + zz, "col": col}

    sibling = q_dev(x, yh, 1 - core)
    ring_x = [(x + d) % 4 for d in range(1, 4)]
    ring_z = [(z + d) % 4 for d in range(1, 4)]
    enter(
        [sibling, q_dev(x, 1 - yh, core), k_dev(1 - yl, z)]
        + [q_dev(xx, yh, core) for xx in ring_x]
        + [k_dev(yl, zz) for zz in ring_z]
    )
    sends = Sends(send)
    for xx in ring_x + [x]:
        sends.start(
            qp.at[xx, :, 1 - core], pair_in.at[xx], recv.at[0, xx], sibling
        )
    for zz in ring_z:
        sends.start(kp.at[:, zz], ring_k.at[z], recv.at[1, z], k_dev(yl, zz))
    for xx in ring_x + [x]:
        ref = pair_in.at[xx]
        remote(ref, ref, send.at[0], recv.at[0, xx], sibling).wait_recv()
        pair_sum[xx] = (
            qp[xx, :, core].astype(jnp.float32) + pair_in[xx].astype(jnp.float32)
        ).astype(jnp.bfloat16)
    for xx in ring_x:
        sends.start(pair_sum.at[xx], ring_q.at[x], recv.at[2, x], q_dev(xx, yh, core))

    def ring_total(own, landed, row_of, ring, which, peer):
        for at in ring:
            ref = landed.at[at]
            remote(ref, ref, send.at[0], recv.at[which, at], peer).wait_recv()
        totals = []
        for half in range(2):
            total = own(half).astype(jnp.float32)
            for at in ring:
                total = total + landed[at, half].astype(jnp.float32)
            totals.append(total)
        return totals

    def finish(own, landed, ring, which, pos, stage, last, out, peer, slot):
        for at in ring:
            ref = landed.at[at]
            remote(ref, ref, send.at[0], recv.at[which, at], peer).wait_recv()
        total = own(1 - pos).astype(jnp.float32)
        for at in ring:
            total = total + landed[at, 1 - pos].astype(jnp.float32)
        stage[...] = total.astype(jnp.bfloat16)
        sends.start(stage, last, recv.at[3, slot], peer)
        total = own(pos).astype(jnp.float32)
        for at in ring:
            total = total + landed[at, pos].astype(jnp.float32)
        out[...] = total

    pair_y = q_dev(x, 1 - yh, core)
    pair_r = k_dev(1 - yl, z)
    finish(lambda y: kp[y, z], ring_k, ring_z, 1, yl, out_k, last_k, ko, pair_r, 0)
    finish(lambda y: pair_sum[x, y], ring_q, ring_x, 2, yh, out_q, last_q, qo, pair_y, 1)
    remote(last_k, last_k, send.at[0], recv.at[3, 0], pair_r).wait_recv()
    ko[...] += last_k[...].astype(jnp.float32)
    remote(last_q, last_q, send.at[0], recv.at[3, 1], pair_y).wait_recv()
    qo[...] += last_q[...].astype(jnp.float32)
    sends.drain()


def reduce(qp, kp):
    bf = jnp.bfloat16
    return pl.pallas_call(
        reduce_kernel,
        in_specs=[VM] * 2,
        out_specs=[VM] * 2,
        out_shape=[jax.ShapeDtypeStruct((128, 512), jnp.float32)] * 2,
        scratch_shapes=[
            pltpu.VMEM((4, 2, 128, 512), bf),
            pltpu.VMEM((4, 2, 128, 512), bf),
            pltpu.VMEM((4, 2, 128, 512), bf),
            pltpu.VMEM((4, 2, 128, 512), bf),
            pltpu.VMEM((128, 512), bf),
            pltpu.VMEM((128, 512), bf),
            pltpu.VMEM((128, 512), bf),
            pltpu.VMEM((128, 512), bf),
            pltpu.SemaphoreType.DMA((16,)),
            pltpu.SemaphoreType.DMA((4, 4)),
        ],
        compiler_params=pltpu.CompilerParams(
            collective_id=2, has_side_effects=True, vmem_limit_bytes=40 << 20
        ),
        name="reduce",
    )(qp, kp)


def mask_keys(k_ref, km):
    half = lax.broadcasted_iota(jnp.int32, (128, 128), 1) < HEAD
    for block in range(8):
        for h in range(HEADS):
            kk = k_ref[block, :, (h // 2) * 128 : (h // 2 + 1) * 128]
            keep = half if h % 2 == 0 else jnp.logical_not(half)
            km[h, block * 128 : (block + 1) * 128, :] = jnp.where(keep, kk, jnp.zeros_like(kk))


def tile_terms(i, j, q_ref, f_ref, bt, grains, pu_ref):
    f = jnp.concatenate([f_ref[2 * i], f_ref[2 * i + 1]], axis=1)
    counts = nn(bt[pl.ds(pl.multiple_of(j * VC, VC), VC), :], f)
    off = lax.broadcasted_iota(jnp.int32, (GRAIN, UB), 0)
    per = VC // GRAIN
    pv = jnp.concatenate([off + GRAIN * grains[j * per + t] for t in range(per)], axis=0)
    valid = pv >= pu_ref[pl.ds(i, 1), :]
    return counts, valid


def queries_of(i, q_ref):
    q = jnp.concatenate([q_ref[2 * i], q_ref[2 * i + 1]], axis=0)
    return q * jnp.bfloat16(SCALE)


def stats_kernel(q_ref, k_ref, f_ref, b_ref, grains, pu_ref, out, km, bt):
    mask_keys(k_ref, km)
    for block in range(8):
        bt[block * 128 : (block + 1) * 128, :] = b_ref[block].T

    def sources(i, _):
        q = queries_of(i, q_ref)

        def targets(j, state):
            counts, valid = tile_terms(i, j, q_ref, f_ref, bt, grains, pu_ref)
            vs = pl.multiple_of(j * VC, VC)
            after = []
            for h in range(HEADS):
                top, total, expect = state[h]
                s = nt(km[h, pl.ds(vs, VC), :], q[:, (h // 2) * 128 : (h // 2 + 1) * 128])
                s = jnp.where(valid, s, NEG)
                higher = jnp.maximum(top, jnp.max(s, axis=0, keepdims=True))
                w = jnp.exp(s - higher)
                w = jnp.where(valid, w, 0.0)
                shrink = jnp.exp(top - higher)
                total = total * shrink + jnp.sum(w, axis=0, keepdims=True)
                expect = expect * shrink + jnp.sum(w * counts, axis=0, keepdims=True)
                after.append((higher, total, expect))
            return tuple(after)

        zero = jnp.zeros((1, UB), jnp.float32)
        state = lax.fori_loop(
            0, 1024 // VC, targets, tuple((zero + NEG, zero, zero) for _ in range(HEADS))
        )
        for h in range(HEADS):
            top, total, expect = state[h]
            some = total > 0.0
            safe = jnp.where(some, total, 1.0)
            log = jnp.where(some, top + jnp.log(safe), NEG)
            mean = expect / safe
            for t in range(UB // 128):
                out[2 * i + t, h : h + 1, :] = log[:, t * 128 : (t + 1) * 128]
                out[2 * i + t, HEADS + h : HEADS + h + 1, :] = mean[:, t * 128 : (t + 1) * 128]
        return 0

    lax.fori_loop(0, 2048 // UB, sources, 0)


def stats(q, k, f, b, grains, pu):
    return pl.pallas_call(
        stats_kernel,
        in_specs=[VM] * 4 + [SM, VM],
        out_specs=VM,
        out_shape=jax.ShapeDtypeStruct((16, 16, 128), jnp.float32),
        scratch_shapes=[
            pltpu.VMEM((HEADS, 1024, 128), jnp.bfloat16),
            pltpu.VMEM((1024, 256), jnp.bfloat16),
        ],
        compiler_params=pltpu.CompilerParams(vmem_limit_bytes=40 << 20),
        name="stats",
    )(q, k, f, b, grains, pu)


def grads_kernel(q_ref, k_ref, f_ref, b_ref, grains, pu_ref, st, qg, kg, km, kt, bt, qacc, kacc):
    mask_keys(k_ref, km)
    for block in range(8):
        bt[block * 128 : (block + 1) * 128, :] = b_ref[block].T
        kt[:, block * 128 : (block + 1) * 128] = k_ref[block].T
    kacc[...] = jnp.zeros_like(kacc)
    low = lax.broadcasted_iota(jnp.int32, (VC, 128), 1) < HEAD

    def sources(i, _):
        q = queries_of(i, q_ref)
        both = jnp.concatenate([st[2 * i], st[2 * i + 1]], axis=1)
        qacc[...] = jnp.zeros_like(qacc)

        def targets(j, _):
            counts, valid = tile_terms(i, j, q_ref, f_ref, bt, grains, pu_ref)
            vs = pl.multiple_of(j * VC, VC)
            pair = []
            for h in range(HEADS):
                qp = q[:, (h // 2) * 128 : (h // 2 + 1) * 128]
                s = nt(km[h, pl.ds(vs, VC), :], qp)
                w = jnp.exp(jnp.where(valid, s - both[h : h + 1], NEG))
                g = (w * (both[HEADS + h : HEADS + h + 1] - counts)).astype(jnp.bfloat16)
                hs = slice(h * HEAD, (h + 1) * HEAD)
                qacc[hs, :] += nn(kt[hs, pl.ds(vs, VC)], g)
                pair.append(nn(g, qp))
                if h % 2:
                    cols = slice((h // 2) * 128, (h // 2 + 1) * 128)
                    kacc[pl.ds(vs, VC), cols] += jnp.where(low, pair[-2], pair[-1])
            return 0

        lax.fori_loop(0, 1024 // VC, targets, 0)
        turned = (qacc[...] * SCALE).T.astype(jnp.bfloat16)
        for t in range(UB // 128):
            qg[2 * i + t] = turned[t * 128 : (t + 1) * 128]
        return 0

    lax.fori_loop(0, 2048 // UB, sources, 0)
    for block in range(8):
        kg[block] = kacc[block * 128 : (block + 1) * 128, :].astype(jnp.bfloat16)


def grads(q, k, f, b, grains, pu, st):
    bf = jnp.bfloat16
    return pl.pallas_call(
        grads_kernel,
        in_specs=[VM] * 4 + [SM, VM, VM],
        out_specs=[VM] * 2,
        out_shape=[
            jax.ShapeDtypeStruct((16, 128, 512), bf),
            jax.ShapeDtypeStruct((8, 128, 512), bf),
        ],
        scratch_shapes=[
            pltpu.VMEM((HEADS, 1024, 128), bf),
            pltpu.VMEM((512, 1024), bf),
            pltpu.VMEM((1024, 256), bf),
            pltpu.VMEM((512, UB), jnp.float32),
            pltpu.VMEM((1024, 512), jnp.float32),
        ],
        compiler_params=pltpu.CompilerParams(vmem_limit_bytes=40 << 20),
        name="grads",
    )(q, k, f, b, grains, pu, st)


def local(queries, keys, fwd_table, bwd_table, step_weight, block_order):
    row_id = lax.axis_index("row")
    col_id = lax.axis_index("col")
    scaled = (bwd_table.astype(jnp.float32) * step_weight[:, None]).astype(jnp.bfloat16)
    sf = fwd_table.reshape(2, 8, 16, 128).transpose(1, 2, 0, 3)
    sb = scaled.reshape(2, 8, 16, 128).transpose(1, 2, 0, 3)
    grid = block_order.reshape(8, 16, 4)
    line = lax.dynamic_index_in_dim(grid, row_id, 0, keepdims=False).reshape(64)
    column = lax.dynamic_index_in_dim(grid, col_id, 1, keepdims=False).reshape(32)
    offsets = jnp.arange(GRAIN, dtype=jnp.int32)
    pu = (line[:, None] * GRAIN + offsets[None, :]).reshape(2048 // UB, UB)
    q, k, f, b = gather(queries, keys, sf, sb)
    f = f.reshape(16, 256, 128)
    b = b.reshape(8, 256, 128)
    merged = merge(stats(q, k, f, b, column, pu))
    qg, kg = grads(q, k, f, b, column, pu, merged)
    return reduce(qg.reshape(4, 2, 2, 128, 512), kg.reshape(2, 4, 128, 512))


def solution(mesh):
    return jax.shard_map(
        local,
        mesh=mesh,
        in_specs=(
            P(("row", "col"), None),
            P(("row", "col"), None),
            P(("row", "col"), None),
            P(("row", "col"), None),
            P(("row", "col")),
            P(),
        ),
        out_specs=(P(("row", "col"), None), P(("row", "col"), None)),
        check_vma=False,
    )
```

```python
import jax
import jax.numpy as jnp
from jax import lax
from jax.experimental import pallas as pl
from jax.experimental.pallas import tpu as pltpu
from jax.sharding import PartitionSpec as P

HEADS = 8
HEAD = 64
GRAIN = 32
SCALE = HEAD**-0.5
LOG_HEADS = 2.0794415416798357
NEG = -1e30
TOP = -1e29
NU = 64
NV = 32
UB1, VC1 = 256, 128
UB2, VC2 = 256, 128
MESH = pl.DeviceIdType.MESH
VM = pl.BlockSpec(memory_space=pltpu.VMEM)
SM = pl.BlockSpec(memory_space=pltpu.SMEM)


def nn(a, b):
    return lax.dot_general(a, b, (((1,), (0,)), ((), ())), preferred_element_type=jnp.float32)


def nt(a, b):
    return lax.dot_general(a, b, (((1,), (1,)), ((), ())), preferred_element_type=jnp.float32)


def remote(src, dst, send, recv, peer):
    return pltpu.make_async_remote_copy(
        src_ref=src, dst_ref=dst, send_sem=send, recv_sem=recv, device_id=peer, device_id_type=MESH
    )


def enter(peers):
    barrier = pltpu.get_barrier_semaphore()
    for peer in peers:
        pl.semaphore_signal(barrier, inc=1, device_id=peer, device_id_type=MESH)
    pl.semaphore_wait(barrier, len(peers))


class Sends:
    def __init__(self, sems):
        self.sems = sems
        self.started = []

    def start(self, src, dst, recv, peer):
        copy = remote(src, dst, self.sems.at[len(self.started)], recv, peer)
        copy.start()
        self.started.append(copy)

    def drain(self):
        for copy in self.started:
            copy.wait_send()


def gather_kernel(q, k, sf, sb, qa, ka, fa, ba, send, recv_q, recv_f, recv_k, recv_b, in_f, in_b, own):
    row, col = lax.axis_index("row"), lax.axis_index("col")
    x, yh, core = col // 4, (col // 2) % 2, col % 2
    yl, z = row // 4, row % 4

    def at(r=None, c=None):
        return {"row": row if r is None else r, "col": col if c is None else c}

    def cslot(xx, yy, cc):
        return xx * 4 + yy * 2 + cc

    enter(
        [at(r=(row + d) % 8) for d in range(1, 8)] + [at(c=(col + d) % 16) for d in range(1, 16)]
    )
    sends = Sends(send)
    local = [
        pltpu.make_async_copy(q, qa.at[col], own.at[0]),
        pltpu.make_async_copy(k, ka.at[row], own.at[1]),
        pltpu.make_async_copy(sf.at[row], fa.at[:, col, row], own.at[2]),
        pltpu.make_async_copy(sb.at[:, col], ba.at[:, col, row], own.at[3]),
    ]
    for copy in local:
        copy.start()
    for d in range(1, 8):
        to = (row + d) % 8
        sends.start(sf.at[to], fa.at[:, col, row], in_f.at[row], at(r=to))
    for d in range(1, 16):
        to = (col + d) % 16
        sends.start(sb.at[:, to], ba.at[:, col, row], in_b.at[col], at(c=to))

    def q_part(slot, half=None):
        return qa.at[slot] if half is None else qa.at[slot, pl.ds(half * 64, 64)]

    def f_part(slot, half=None):
        return fa.at[:, slot] if half is None else fa.at[pl.ds(half * 8, 8), slot]

    def k_part(slot, half=None):
        return ka.at[slot] if half is None else ka.at[slot, pl.ds(half * 64, 64)]

    def b_part(slot, half=None):
        return ba.at[:, :, slot] if half is None else ba.at[pl.ds(half * 4, 4), :, slot]

    def src_slot(dx, dy, cc=None):
        return cslot((x + dx) % 4, (yh + dy) % 2, core if cc is None else cc)

    def tgt_slot(dz, dy):
        return ((yl + dy) % 2) * 4 + (z + dz) % 4

    def src_dev(dx, dy, dc=0):
        return at(c=cslot((x + dx) % 4, (yh + dy) % 2, (core + dc) % 2))

    def tgt_dev(dz, dy):
        return at(r=tgt_slot(dz, dy))

    source = (src_slot, src_dev, True)
    target = (tgt_slot, tgt_dev, False)
    streams = {
        "q": (q_part, recv_q, source),
        "f": (f_part, recv_f, source),
        "k": (k_part, recv_k, target),
        "b": (b_part, recv_b, target),
    }

    def push(kind, slot, peer, half=None):
        part, recv, _ = streams[kind]
        ref = part(slot, half)
        sends.start(ref, ref, recv.at[slot, 0 if half is None else half], peer)

    def arrived(kind, slot, half=None):
        part, recv, _ = streams[kind]
        ref = part(slot, half)
        remote(ref, ref, send.at[0], recv.at[slot, 0 if half is None else half], at()).wait_recv()

    def first(kind):
        slot_of, dev_of, pair = streams[kind][2]
        mine = slot_of(0, 0)
        push(kind, mine, dev_of(0, 1))
        push(kind, mine, dev_of(1, 0))
        push(kind, mine, dev_of(3, 0))
        if pair:
            push(kind, mine, dev_of(0, 0, 1))

    def second(kind):
        slot_of, dev_of, pair = streams[kind][2]
        other = slot_of(0, 1)
        arrived(kind, other)
        push(kind, other, dev_of(1, 0))
        push(kind, other, dev_of(3, 0))
        if pair:
            push(kind, other, dev_of(0, 0, 1))

    def relay(kind, dy):
        slot_of, dev_of, pair = streams[kind][2]
        for step, half in ((3, 0), (1, 1)):
            slot = slot_of(step, dy)
            arrived(kind, slot)
            push(kind, slot, dev_of(4 - step, 0), half)
            if pair:
                push(kind, slot, dev_of(0, 0, 1))

    def last(kind, dy):
        slot_of, dev_of, pair = streams[kind][2]
        slot = slot_of(2, dy)
        arrived(kind, slot, 0)
        arrived(kind, slot, 1)
        if pair:
            push(kind, slot, dev_of(0, 0, 1))

    local[0].wait()
    local[1].wait()
    first("q")
    first("k")
    local[2].wait()
    for d in range(1, 8):
        frm = (row + d) % 8
        ref = fa.at[:, col, frm]
        remote(ref, ref, send.at[0], in_f.at[frm], at()).wait_recv()
    first("f")
    local[3].wait()
    for d in range(1, 16):
        frm = (col + d) % 16
        ref = ba.at[:, frm, row]
        remote(ref, ref, send.at[0], in_b.at[frm], at()).wait_recv()
    first("b")
    second("k")
    second("q")
    relay("k", 0)
    relay("q", 0)
    second("b")
    second("f")
    relay("k", 1)
    relay("q", 1)
    relay("b", 0)
    relay("f", 0)
    relay("b", 1)
    relay("f", 1)
    for kind in ("k", "q", "b", "f"):
        last(kind, 0)
        last(kind, 1)
    for kind in ("q", "f"):
        for dx in range(4):
            for dy in range(2):
                arrived(kind, src_slot(dx, dy, 1 - core))
    sends.drain()


def gather(q, k, sf, sb):
    bf = jnp.bfloat16
    return pl.pallas_call(
        gather_kernel,
        in_specs=[VM] * 4,
        out_specs=[VM] * 4,
        out_shape=[
            jax.ShapeDtypeStruct((16, 128, 512), bf),
            jax.ShapeDtypeStruct((8, 128, 512), bf),
            jax.ShapeDtypeStruct((16, 16, 8, 2, 128), bf),
            jax.ShapeDtypeStruct((8, 16, 8, 2, 128), bf),
        ],
        scratch_shapes=[
            pltpu.SemaphoreType.DMA((100,)),
            pltpu.SemaphoreType.DMA((16, 2)),
            pltpu.SemaphoreType.DMA((16, 2)),
            pltpu.SemaphoreType.DMA((8, 2)),
            pltpu.SemaphoreType.DMA((8, 2)),
            pltpu.SemaphoreType.DMA((8,)),
            pltpu.SemaphoreType.DMA((16,)),
            pltpu.SemaphoreType.DMA((4,)),
        ],
        compiler_params=pltpu.CompilerParams(
            collective_id=0, has_side_effects=True, vmem_limit_bytes=16 << 20
        ),
        name="gather",
    )(q, k, sf, sb)


def merge_kernel(part, out, landed, mine, send, recv, recv2, own):
    row, col = lax.axis_index("row"), lax.axis_index("col")
    peers = [{"row": row, "col": (col + d) % 16} for d in range(1, 16)]
    enter(peers)
    sends = Sends(send)
    keep = pltpu.make_async_copy(part.at[col], landed.at[col], own.at[0])
    keep.start()
    for d, peer in enumerate(peers):
        sends.start(part.at[peer["col"]], landed.at[col], recv.at[col], peer)
    keep.wait()
    for peer in peers:
        ref = landed.at[peer["col"]]
        remote(ref, ref, send.at[0], recv.at[peer["col"]], peer).wait_recv()
    logs = landed[:, 0:8]
    top = jnp.max(logs, axis=0)
    weight = jnp.exp(logs - top[None])
    total = jnp.sum(weight, axis=0)
    mean = jnp.sum(weight * landed[:, 8:16], axis=0) / total
    mine[0:8, :] = top + jnp.log(total) + LOG_HEADS
    mine[8:16, :] = mean
    keep = pltpu.make_async_copy(mine, out.at[col], own.at[1])
    keep.start()
    for peer in peers:
        sends.start(mine, out.at[col], recv2.at[col], peer)
    keep.wait()
    for peer in peers:
        ref = out.at[peer["col"]]
        remote(ref, ref, send.at[0], recv2.at[peer["col"]], peer).wait_recv()
    sends.drain()


def merge(part):
    return pl.pallas_call(
        merge_kernel,
        in_specs=[VM],
        out_specs=VM,
        out_shape=jax.ShapeDtypeStruct((16, 16, 128), jnp.float32),
        scratch_shapes=[
            pltpu.VMEM((16, 16, 128), jnp.float32),
            pltpu.VMEM((16, 128), jnp.float32),
            pltpu.SemaphoreType.DMA((30,)),
            pltpu.SemaphoreType.DMA((16,)),
            pltpu.SemaphoreType.DMA((16,)),
            pltpu.SemaphoreType.DMA((2,)),
        ],
        compiler_params=pltpu.CompilerParams(
            collective_id=1, has_side_effects=True, vmem_limit_bytes=4 << 20
        ),
        name="merge",
    )(part)


def reduce_kernel(qp, kp, qo, ko, pair_in, pair_sum, ring_q, ring_k, out_q, out_k, last_q, last_k, send, recv):
    row, col = lax.axis_index("row"), lax.axis_index("col")
    x, yh, core = col // 4, (col // 2) % 2, col % 2
    yl, z = row // 4, row % 4

    def q_dev(xx, yy, cc):
        return {"row": row, "col": xx * 4 + yy * 2 + cc}

    def k_dev(yy, zz):
        return {"row": yy * 4 + zz, "col": col}

    sibling = q_dev(x, yh, 1 - core)
    ring_x = [(x + d) % 4 for d in range(1, 4)]
    ring_z = [(z + d) % 4 for d in range(1, 4)]
    enter(
        [sibling, q_dev(x, 1 - yh, core), k_dev(1 - yl, z)]
        + [q_dev(xx, yh, core) for xx in ring_x]
        + [k_dev(yl, zz) for zz in ring_z]
    )
    sends = Sends(send)
    for xx in ring_x + [x]:
        sends.start(
            qp.at[xx, :, 1 - core], pair_in.at[xx], recv.at[0, xx], sibling
        )
    for zz in ring_z:
        sends.start(kp.at[:, zz], ring_k.at[z], recv.at[1, z], k_dev(yl, zz))
    for xx in ring_x + [x]:
        ref = pair_in.at[xx]
        remote(ref, ref, send.at[0], recv.at[0, xx], sibling).wait_recv()
        pair_sum[xx] = (
            qp[xx, :, core].astype(jnp.float32) + pair_in[xx].astype(jnp.float32)
        ).astype(jnp.bfloat16)
    for xx in ring_x:
        sends.start(pair_sum.at[xx], ring_q.at[x], recv.at[2, x], q_dev(xx, yh, core))

    def finish(own, landed, ring, which, pos, stage, last, out, peer, slot):
        for at in ring:
            ref = landed.at[at]
            remote(ref, ref, send.at[0], recv.at[which, at], peer).wait_recv()
        total = own(1 - pos).astype(jnp.float32)
        for at in ring:
            total = total + landed[at, 1 - pos].astype(jnp.float32)
        stage[...] = total.astype(jnp.bfloat16)
        sends.start(stage, last, recv.at[3, slot], peer)
        total = own(pos).astype(jnp.float32)
        for at in ring:
            total = total + landed[at, pos].astype(jnp.float32)
        out[...] = total

    pair_y = q_dev(x, 1 - yh, core)
    pair_r = k_dev(1 - yl, z)
    finish(lambda y: kp[y, z], ring_k, ring_z, 1, yl, out_k, last_k, ko, pair_r, 0)
    finish(lambda y: pair_sum[x, y], ring_q, ring_x, 2, yh, out_q, last_q, qo, pair_y, 1)
    remote(last_k, last_k, send.at[0], recv.at[3, 0], pair_r).wait_recv()
    ko[...] += last_k[...].astype(jnp.float32)
    remote(last_q, last_q, send.at[0], recv.at[3, 1], pair_y).wait_recv()
    qo[...] += last_q[...].astype(jnp.float32)
    sends.drain()


def reduce(qp, kp):
    bf = jnp.bfloat16
    return pl.pallas_call(
        reduce_kernel,
        in_specs=[VM] * 2,
        out_specs=[VM] * 2,
        out_shape=[jax.ShapeDtypeStruct((128, 512), jnp.float32)] * 2,
        scratch_shapes=[
            pltpu.VMEM((4, 2, 128, 512), bf),
            pltpu.VMEM((4, 2, 128, 512), bf),
            pltpu.VMEM((4, 2, 128, 512), bf),
            pltpu.VMEM((4, 2, 128, 512), bf),
            pltpu.VMEM((128, 512), bf),
            pltpu.VMEM((128, 512), bf),
            pltpu.VMEM((128, 512), bf),
            pltpu.VMEM((128, 512), bf),
            pltpu.SemaphoreType.DMA((16,)),
            pltpu.SemaphoreType.DMA((4, 4)),
        ],
        compiler_params=pltpu.CompilerParams(
            collective_id=2, has_side_effects=True, vmem_limit_bytes=16 << 20
        ),
        name="reduce",
    )(qp, kp)


def mask_keys(ks, km):
    half = lax.broadcasted_iota(jnp.int32, (128, 128), 1) < HEAD
    for block in range(8):
        rows = slice(block * 128, (block + 1) * 128)
        for h in range(HEADS):
            kk = ks[rows, (h // 2) * 128 : (h // 2 + 1) * 128]
            keep = half if h % 2 == 0 else jnp.logical_not(half)
            km[h, rows, :] = jnp.where(keep, kk, jnp.zeros_like(kk))


def order_of(meta, which, g):
    return meta[which * NU + g]


def place_of(meta, which, g):
    return meta[NU + NV + which * NU + g]


def rows_of(g):
    return pl.ds(pl.multiple_of(g * GRAIN, GRAIN), GRAIN)


def chunk_bounds(meta, i, ub, vc):
    low = place_of(meta, 0, i * (ub // GRAIN))
    high = place_of(meta, 0, (i + 1) * (ub // GRAIN) - 1)
    per = vc // GRAIN
    first = jnp.int32(0)
    full = jnp.int32(0)
    for j in range(NV // per):
        first += (place_of(meta, 1, (j + 1) * per - 1) < low).astype(jnp.int32)
        full += (place_of(meta, 1, j * per) <= high).astype(jnp.int32)
    return first, full


def chunk_valid(meta, pu, j, ub, vc):
    off = lax.broadcasted_iota(jnp.int32, (GRAIN, ub), 0)
    per = vc // GRAIN
    pv = jnp.concatenate(
        [off + GRAIN * place_of(meta, 1, j * per + t) for t in range(per)], axis=0
    )
    return pv >= pu


def stats_kernel(q_ref, k_ref, f_ref, b_ref, meta, pu_ref, out, qs, ks, fs, bs, km, ft, bt, run_m, run_t, run_e):
    ub, vc = UB1, VC1
    for block in range(16):
        ft[block * 128 : (block + 1) * 128, :] = f_ref[block].T
    for block in range(8):
        bt[block * 128 : (block + 1) * 128, :] = b_ref[block].T

    def sort_sources(g, _):
        frm = rows_of(order_of(meta, 0, g))
        qs[rows_of(g), :] = q_ref[frm, :] * jnp.bfloat16(SCALE)
        fs[rows_of(g), :] = ft[frm, :]
        return 0

    def sort_targets(g, _):
        frm = rows_of(order_of(meta, 1, g))
        ks[rows_of(g), :] = k_ref[frm, :]
        bs[rows_of(g), :] = bt[frm, :]
        return 0

    lax.fori_loop(0, NU, sort_sources, 0)
    lax.fori_loop(0, NV, sort_targets, 0)
    mask_keys(ks, km)

    def sources(i, _):
        us = pl.ds(pl.multiple_of(i * ub, ub), ub)
        first, full = chunk_bounds(meta, i, ub, vc)
        run_m[...] = jnp.full_like(run_m, TOP)
        run_t[...] = jnp.zeros_like(run_t)
        run_e[...] = jnp.zeros_like(run_e)

        def targets(j, masked):
            vs = pl.ds(pl.multiple_of(j * vc, vc), vc)
            counts = nt(bs[vs, :], fs[us, :]).reshape(vc // 8, 8, ub)
            if masked:
                valid = chunk_valid(meta, pu_ref[pl.ds(i, 1), :], j, ub, vc)
            for h in range(HEADS):
                s = nt(km[h, vs, :], qs[us, (h // 2) * 128 : (h // 2 + 1) * 128])
                if masked:
                    s = jnp.where(valid, s, NEG)
                s = s.reshape(vc // 8, 8, ub)
                old = run_m[h]
                new = jnp.maximum(old, jnp.max(s, axis=0))
                w = jnp.exp(s - new[None])
                shrink = jnp.exp(old - new)
                run_m[h] = new
                run_t[h] = run_t[h] * shrink + jnp.sum(w, axis=0)
                run_e[h] = run_e[h] * shrink + jnp.sum(w * counts, axis=0)

        def masked_step(j, _):
            targets(j, True)
            return 0

        def open_step(j, _):
            targets(j, False)
            return 0

        lax.fori_loop(first, full, masked_step, 0)
        lax.fori_loop(full, 1024 // vc, open_step, 0)
        for h in range(HEADS):
            part_m = run_m[h]
            top = jnp.max(part_m, axis=0, keepdims=True)
            weight = jnp.exp(part_m - top)
            total = jnp.sum(run_t[h] * weight, axis=0, keepdims=True)
            expect = jnp.sum(run_e[h] * weight, axis=0, keepdims=True)
            some = total > 0.0
            safe = jnp.where(some, total, 1.0)
            log = jnp.where(some, top + jnp.log(safe), NEG)
            mean = expect / safe
            for t in range(ub // 128):
                at = i * (ub // 128) + t
                out[at, h : h + 1, :] = log[:, t * 128 : (t + 1) * 128]
                out[at, HEADS + h : HEADS + h + 1, :] = mean[:, t * 128 : (t + 1) * 128]
        return 0

    lax.fori_loop(0, 2048 // ub, sources, 0)


def stats(q, k, f, b, meta, pu):
    bf = jnp.bfloat16
    return pl.pallas_call(
        stats_kernel,
        in_specs=[VM] * 4 + [SM, VM],
        out_specs=[VM] * 5,
        out_shape=[
            jax.ShapeDtypeStruct((16, 16, 128), jnp.float32),
            jax.ShapeDtypeStruct((2048, 512), bf),
            jax.ShapeDtypeStruct((1024, 512), bf),
            jax.ShapeDtypeStruct((2048, 256), bf),
            jax.ShapeDtypeStruct((1024, 256), bf),
        ],
        scratch_shapes=[
            pltpu.VMEM((HEADS, 1024, 128), bf),
            pltpu.VMEM((2048, 256), bf),
            pltpu.VMEM((1024, 256), bf),
            pltpu.VMEM((HEADS, 8, UB1), jnp.float32),
            pltpu.VMEM((HEADS, 8, UB1), jnp.float32),
            pltpu.VMEM((HEADS, 8, UB1), jnp.float32),
        ],
        compiler_params=pltpu.CompilerParams(vmem_limit_bytes=24 << 20),
        name="stats",
    )(q, k, f, b, meta, pu)


def grads_kernel(qs, ks, fs, bs, meta, pu_ref, st, qg, kg, km, kt, qacc, kacc):
    ub, vc = UB2, VC2
    mask_keys(ks, km)
    for block in range(8):
        rows = slice(block * 128, (block + 1) * 128)
        kt[:, rows] = ks[rows, :].T
    kacc[...] = jnp.zeros_like(kacc)
    low = lax.broadcasted_iota(jnp.int32, (vc, 128), 1) < HEAD

    def sources(i, _):
        us = pl.ds(pl.multiple_of(i * ub, ub), ub)
        first, full = chunk_bounds(meta, i, ub, vc)
        both = jnp.concatenate([st[i * (ub // 128) + t] for t in range(ub // 128)], axis=1)
        qacc[...] = jnp.zeros_like(qacc)

        def targets(j, masked):
            vs = pl.ds(pl.multiple_of(j * vc, vc), vc)
            counts = nt(bs[vs, :], fs[us, :])
            if masked:
                valid = chunk_valid(meta, pu_ref[pl.ds(i, 1), :], j, ub, vc)
            pair = []
            for h in range(HEADS):
                qp = qs[us, (h // 2) * 128 : (h // 2 + 1) * 128]
                s = nt(km[h, vs, :], qp) - both[h : h + 1]
                if masked:
                    s = jnp.where(valid, s, NEG)
                g = (jnp.exp(s) * (both[HEADS + h : HEADS + h + 1] - counts)).astype(jnp.bfloat16)
                hs = slice(h * HEAD, (h + 1) * HEAD)
                qacc[hs, :] += nn(kt[hs, vs], g)
                pair.append(nn(g, qp))
                if h % 2:
                    cols = slice((h // 2) * 128, (h // 2 + 1) * 128)
                    kacc[vs, cols] += jnp.where(low, pair[-2], pair[-1])

        def masked_step(j, _):
            targets(j, True)
            return 0

        def open_step(j, _):
            targets(j, False)
            return 0

        lax.fori_loop(first, full, masked_step, 0)
        lax.fori_loop(full, 1024 // vc, open_step, 0)
        turned = (qacc[...] * SCALE).T.astype(jnp.bfloat16)
        for t in range(ub // GRAIN):
            to = order_of(meta, 0, i * (ub // GRAIN) + t)
            qg[rows_of(to), :] = turned[t * GRAIN : (t + 1) * GRAIN]
        return 0

    lax.fori_loop(0, 2048 // ub, sources, 0)

    def unsort(g, _):
        kg[rows_of(order_of(meta, 1, g)), :] = kacc[rows_of(g), :].astype(jnp.bfloat16)
        return 0

    lax.fori_loop(0, NV, unsort, 0)


def grads(qs, ks, fs, bs, meta, pu, st):
    bf = jnp.bfloat16
    return pl.pallas_call(
        grads_kernel,
        in_specs=[VM] * 4 + [SM, VM, VM],
        out_specs=[VM] * 2,
        out_shape=[
            jax.ShapeDtypeStruct((2048, 512), bf),
            jax.ShapeDtypeStruct((1024, 512), bf),
        ],
        scratch_shapes=[
            pltpu.VMEM((HEADS, 1024, 128), bf),
            pltpu.VMEM((512, 1024), bf),
            pltpu.VMEM((512, UB2), jnp.float32),
            pltpu.VMEM((1024, 512), jnp.float32),
        ],
        compiler_params=pltpu.CompilerParams(vmem_limit_bytes=24 << 20),
        name="grads",
    )(qs, ks, fs, bs, meta, pu, st)


def in_order(places):
    n = places.shape[0]
    rank = jnp.sum((places[None, :] < places[:, None]).astype(jnp.int32), axis=1)
    index = jnp.arange(n, dtype=jnp.int32)
    hit = rank[None, :] == index[:, None]
    return (
        jnp.sum(jnp.where(hit, index[None, :], 0), axis=1),
        jnp.sum(jnp.where(hit, places[None, :], 0), axis=1),
    )


def local(queries, keys, fwd_table, bwd_table, step_weight, block_order):
    row_id = lax.axis_index("row")
    col_id = lax.axis_index("col")
    scaled = (bwd_table.astype(jnp.float32) * step_weight[:, None]).astype(jnp.bfloat16)
    sf = fwd_table.reshape(2, 8, 16, 128).transpose(1, 2, 0, 3)
    sb = scaled.reshape(2, 8, 16, 128).transpose(1, 2, 0, 3)
    grid = block_order.reshape(8, 16, 4)
    line = lax.dynamic_index_in_dim(grid, row_id, 0, keepdims=False).reshape(64)
    column = lax.dynamic_index_in_dim(grid, col_id, 1, keepdims=False).reshape(32)
    order_u, place_u = in_order(line)
    order_v, place_v = in_order(column)
    meta = jnp.concatenate([order_u, order_v, place_u, place_v])
    offsets = jnp.arange(GRAIN, dtype=jnp.int32)
    pu = (place_u[:, None] * GRAIN + offsets[None, :]).reshape(8, 256)
    q, k, f, b = gather(queries, keys, sf, sb)
    part, qs, ks, fs, bs = stats(
        q.reshape(2048, 512),
        k.reshape(1024, 512),
        f.reshape(16, 256, 128),
        b.reshape(8, 256, 128),
        meta,
        pu,
    )
    qg, kg = grads(qs, ks, fs, bs, meta, pu, merge(part))
    return reduce(qg.reshape(4, 2, 2, 128, 512), kg.reshape(2, 4, 128, 512))


def solution(mesh):
    return jax.shard_map(
        local,
        mesh=mesh,
        in_specs=(
            P(("row", "col"), None),
            P(("row", "col"), None),
            P(("row", "col"), None),
            P(("row", "col"), None),
            P(("row", "col")),
            P(),
        ),
        out_specs=(P(("row", "col"), None), P(("row", "col"), None)),
        check_vma=False,
    )
```

```python
import jax
import jax.numpy as jnp
from jax import lax
from jax.experimental import pallas as pl
from jax.experimental.pallas import tpu as pltpu
from jax.sharding import PartitionSpec as P

HEADS = 8
HEAD = 64
GRAIN = 32
SCALE = HEAD**-0.5
LOG_HEADS = 2.0794415416798357
NEG = -1e30
TOP = -1e29
NU = 64
NV = 32
TILES = 64
SLOTS = 4
UB = 256
VC = 128
SUB = 128
MESH = pl.DeviceIdType.MESH
VM = pl.BlockSpec(memory_space=pltpu.VMEM)
SM = pl.BlockSpec(memory_space=pltpu.SMEM)


def nn(a, b):
    return lax.dot_general(a, b, (((1,), (0,)), ((), ())), preferred_element_type=jnp.float32)


def nt(a, b):
    return lax.dot_general(a, b, (((1,), (1,)), ((), ())), preferred_element_type=jnp.float32)


def remote(src, dst, send, recv, peer):
    return pltpu.make_async_remote_copy(
        src_ref=src, dst_ref=dst, send_sem=send, recv_sem=recv, device_id=peer, device_id_type=MESH
    )


def enter(peers):
    barrier = pltpu.get_barrier_semaphore()
    for peer in peers:
        pl.semaphore_signal(barrier, inc=1, device_id=peer, device_id_type=MESH)
    pl.semaphore_wait(barrier, len(peers))


class Sends:
    def __init__(self, sems):
        self.sems = sems
        self.started = []

    def start(self, src, dst, recv, peer):
        copy = remote(src, dst, self.sems.at[len(self.started)], recv, peer)
        copy.start()
        self.started.append(copy)

    def drain(self):
        for copy in self.started:
            copy.wait_send()


def gather_kernel(q, k, sf, sb, qa, ka, fa, ba, send, recv_q, recv_f, recv_k, recv_b, in_f, in_b, own):
    row, col = lax.axis_index("row"), lax.axis_index("col")
    x, yh, core = col // 4, (col // 2) % 2, col % 2
    yl, z = row // 4, row % 4

    def at(r=None, c=None):
        return {"row": row if r is None else r, "col": col if c is None else c}

    def cslot(xx, yy, cc):
        return xx * 4 + yy * 2 + cc

    enter(
        [at(r=(row + d) % 8) for d in range(1, 8)] + [at(c=(col + d) % 16) for d in range(1, 16)]
    )
    sends = Sends(send)
    local = [
        pltpu.make_async_copy(q, qa.at[col], own.at[0]),
        pltpu.make_async_copy(k, ka.at[row], own.at[1]),
        pltpu.make_async_copy(sf.at[row], fa.at[:, col, row], own.at[2]),
        pltpu.make_async_copy(sb.at[:, col], ba.at[:, col, row], own.at[3]),
    ]
    for copy in local:
        copy.start()
    for d in range(1, 8):
        to = (row + d) % 8
        sends.start(sf.at[to], fa.at[:, col, row], in_f.at[row], at(r=to))
    for d in range(1, 16):
        to = (col + d) % 16
        sends.start(sb.at[:, to], ba.at[:, col, row], in_b.at[col], at(c=to))

    def q_part(slot, half=None):
        return qa.at[slot] if half is None else qa.at[slot, pl.ds(half * 64, 64)]

    def f_part(slot, half=None):
        return fa.at[:, slot] if half is None else fa.at[pl.ds(half * 8, 8), slot]

    def k_part(slot, half=None):
        return ka.at[slot] if half is None else ka.at[slot, pl.ds(half * 64, 64)]

    def b_part(slot, half=None):
        return ba.at[:, :, slot] if half is None else ba.at[pl.ds(half * 4, 4), :, slot]

    def src_slot(dx, dy, cc=None):
        return cslot((x + dx) % 4, (yh + dy) % 2, core if cc is None else cc)

    def tgt_slot(dz, dy):
        return ((yl + dy) % 2) * 4 + (z + dz) % 4

    def src_dev(dx, dy, dc=0):
        return at(c=cslot((x + dx) % 4, (yh + dy) % 2, (core + dc) % 2))

    def tgt_dev(dz, dy):
        return at(r=tgt_slot(dz, dy))

    source = (src_slot, src_dev, True)
    target = (tgt_slot, tgt_dev, False)
    streams = {
        "q": (q_part, recv_q, source),
        "f": (f_part, recv_f, source),
        "k": (k_part, recv_k, target),
        "b": (b_part, recv_b, target),
    }

    def push(kind, slot, peer, half=None):
        part, recv, _ = streams[kind]
        ref = part(slot, half)
        sends.start(ref, ref, recv.at[slot, 0 if half is None else half], peer)

    def arrived(kind, slot, half=None):
        part, recv, _ = streams[kind]
        ref = part(slot, half)
        remote(ref, ref, send.at[0], recv.at[slot, 0 if half is None else half], at()).wait_recv()

    def first(kind):
        slot_of, dev_of, pair = streams[kind][2]
        mine = slot_of(0, 0)
        push(kind, mine, dev_of(0, 1))
        push(kind, mine, dev_of(1, 0))
        push(kind, mine, dev_of(3, 0))
        if pair:
            push(kind, mine, dev_of(0, 0, 1))

    def second(kind):
        slot_of, dev_of, pair = streams[kind][2]
        other = slot_of(0, 1)
        arrived(kind, other)
        push(kind, other, dev_of(1, 0))
        push(kind, other, dev_of(3, 0))
        if pair:
            push(kind, other, dev_of(0, 0, 1))

    def relay(kind, dy):
        slot_of, dev_of, pair = streams[kind][2]
        for step, half in ((3, 0), (1, 1)):
            slot = slot_of(step, dy)
            arrived(kind, slot)
            push(kind, slot, dev_of(4 - step, 0), half)
            if pair:
                push(kind, slot, dev_of(0, 0, 1))

    def last(kind, dy):
        slot_of, dev_of, pair = streams[kind][2]
        slot = slot_of(2, dy)
        arrived(kind, slot, 0)
        arrived(kind, slot, 1)
        if pair:
            push(kind, slot, dev_of(0, 0, 1))

    local[0].wait()
    local[1].wait()
    first("q")
    first("k")
    local[2].wait()
    for d in range(1, 8):
        frm = (row + d) % 8
        ref = fa.at[:, col, frm]
        remote(ref, ref, send.at[0], in_f.at[frm], at()).wait_recv()
    first("f")
    local[3].wait()
    for d in range(1, 16):
        frm = (col + d) % 16
        ref = ba.at[:, frm, row]
        remote(ref, ref, send.at[0], in_b.at[frm], at()).wait_recv()
    first("b")
    second("k")
    second("q")
    relay("k", 0)
    relay("q", 0)
    second("b")
    second("f")
    relay("k", 1)
    relay("q", 1)
    relay("b", 0)
    relay("f", 0)
    relay("b", 1)
    relay("f", 1)
    for kind in ("k", "q", "b", "f"):
        last(kind, 0)
        last(kind, 1)
    for kind in ("q", "f"):
        for dx in range(4):
            for dy in range(2):
                arrived(kind, src_slot(dx, dy, 1 - core))
    sends.drain()


def gather(q, k, sf, sb):
    bf = jnp.bfloat16
    return pl.pallas_call(
        gather_kernel,
        in_specs=[VM] * 4,
        out_specs=[VM] * 4,
        out_shape=[
            jax.ShapeDtypeStruct((16, 128, 512), bf),
            jax.ShapeDtypeStruct((8, 128, 512), bf),
            jax.ShapeDtypeStruct((16, 16, 8, 2, 128), bf),
            jax.ShapeDtypeStruct((8, 16, 8, 2, 128), bf),
        ],
        scratch_shapes=[
            pltpu.SemaphoreType.DMA((100,)),
            pltpu.SemaphoreType.DMA((16, 2)),
            pltpu.SemaphoreType.DMA((16, 2)),
            pltpu.SemaphoreType.DMA((8, 2)),
            pltpu.SemaphoreType.DMA((8, 2)),
            pltpu.SemaphoreType.DMA((8,)),
            pltpu.SemaphoreType.DMA((16,)),
            pltpu.SemaphoreType.DMA((4,)),
        ],
        compiler_params=pltpu.CompilerParams(
            collective_id=0, has_side_effects=True, vmem_limit_bytes=16 << 20
        ),
        name="gather",
    )(q, k, sf, sb)


def merge_kernel(part, out, landed, mine, send, recv, recv2, own):
    row, col = lax.axis_index("row"), lax.axis_index("col")
    peers = [{"row": row, "col": (col + d) % 16} for d in range(1, 16)]
    enter(peers)
    sends = Sends(send)
    keep = pltpu.make_async_copy(part.at[col], landed.at[col], own.at[0])
    keep.start()
    for d, peer in enumerate(peers):
        sends.start(part.at[peer["col"]], landed.at[col], recv.at[col], peer)
    keep.wait()
    for peer in peers:
        ref = landed.at[peer["col"]]
        remote(ref, ref, send.at[0], recv.at[peer["col"]], peer).wait_recv()
    logs = landed[:, 0:8]
    top = jnp.max(logs, axis=0)
    weight = jnp.exp(logs - top[None])
    total = jnp.sum(weight, axis=0)
    mean = jnp.sum(weight * landed[:, 8:16], axis=0) / total
    mine[0:8, :] = top + jnp.log(total) + LOG_HEADS
    mine[8:16, :] = mean
    keep = pltpu.make_async_copy(mine, out.at[col], own.at[1])
    keep.start()
    for peer in peers:
        sends.start(mine, out.at[col], recv2.at[col], peer)
    keep.wait()
    for peer in peers:
        ref = out.at[peer["col"]]
        remote(ref, ref, send.at[0], recv2.at[peer["col"]], peer).wait_recv()
    sends.drain()


def merge(part):
    return pl.pallas_call(
        merge_kernel,
        in_specs=[VM],
        out_specs=VM,
        out_shape=jax.ShapeDtypeStruct((16, 16, 128), jnp.float32),
        scratch_shapes=[
            pltpu.VMEM((16, 16, 128), jnp.float32),
            pltpu.VMEM((16, 128), jnp.float32),
            pltpu.SemaphoreType.DMA((30,)),
            pltpu.SemaphoreType.DMA((16,)),
            pltpu.SemaphoreType.DMA((16,)),
            pltpu.SemaphoreType.DMA((2,)),
        ],
        compiler_params=pltpu.CompilerParams(
            collective_id=1, has_side_effects=True, vmem_limit_bytes=4 << 20
        ),
        name="merge",
    )(part)


def reduce_kernel(qp, kp, qo, ko, pair_in, pair_sum, ring_q, ring_k, out_q, out_k, last_q, last_k, send, recv):
    row, col = lax.axis_index("row"), lax.axis_index("col")
    x, yh, core = col // 4, (col // 2) % 2, col % 2
    yl, z = row // 4, row % 4

    def q_dev(xx, yy, cc):
        return {"row": row, "col": xx * 4 + yy * 2 + cc}

    def k_dev(yy, zz):
        return {"row": yy * 4 + zz, "col": col}

    sibling = q_dev(x, yh, 1 - core)
    ring_x = [(x + d) % 4 for d in range(1, 4)]
    ring_z = [(z + d) % 4 for d in range(1, 4)]
    enter(
        [sibling, q_dev(x, 1 - yh, core), k_dev(1 - yl, z)]
        + [q_dev(xx, yh, core) for xx in ring_x]
        + [k_dev(yl, zz) for zz in ring_z]
    )
    sends = Sends(send)
    for xx in ring_x + [x]:
        sends.start(
            qp.at[xx, :, 1 - core], pair_in.at[xx], recv.at[0, xx], sibling
        )
    for zz in ring_z:
        sends.start(kp.at[:, zz], ring_k.at[z], recv.at[1, z], k_dev(yl, zz))
    for xx in ring_x + [x]:
        ref = pair_in.at[xx]
        remote(ref, ref, send.at[0], recv.at[0, xx], sibling).wait_recv()
        pair_sum[xx] = (
            qp[xx, :, core].astype(jnp.float32) + pair_in[xx].astype(jnp.float32)
        ).astype(jnp.bfloat16)
    for xx in ring_x:
        sends.start(pair_sum.at[xx], ring_q.at[x], recv.at[2, x], q_dev(xx, yh, core))

    def finish(own, landed, ring, which, pos, stage, last, out, peer, slot):
        for at in ring:
            ref = landed.at[at]
            remote(ref, ref, send.at[0], recv.at[which, at], peer).wait_recv()
        total = own(1 - pos).astype(jnp.float32)
        for at in ring:
            total = total + landed[at, 1 - pos].astype(jnp.float32)
        stage[...] = total.astype(jnp.bfloat16)
        sends.start(stage, last, recv.at[3, slot], peer)
        total = own(pos).astype(jnp.float32)
        for at in ring:
            total = total + landed[at, pos].astype(jnp.float32)
        out[...] = total

    pair_y = q_dev(x, 1 - yh, core)
    pair_r = k_dev(1 - yl, z)
    finish(lambda y: kp[y, z], ring_k, ring_z, 1, yl, out_k, last_k, ko, pair_r, 0)
    finish(lambda y: pair_sum[x, y], ring_q, ring_x, 2, yh, out_q, last_q, qo, pair_y, 1)
    remote(last_k, last_k, send.at[0], recv.at[3, 0], pair_r).wait_recv()
    ko[...] += last_k[...].astype(jnp.float32)
    remote(last_q, last_q, send.at[0], recv.at[3, 1], pair_y).wait_recv()
    qo[...] += last_q[...].astype(jnp.float32)
    sends.drain()


def reduce(qp, kp):
    bf = jnp.bfloat16
    return pl.pallas_call(
        reduce_kernel,
        in_specs=[VM] * 2,
        out_specs=[VM] * 2,
        out_shape=[jax.ShapeDtypeStruct((128, 512), jnp.float32)] * 2,
        scratch_shapes=[
            pltpu.VMEM((4, 2, 128, 512), bf),
            pltpu.VMEM((4, 2, 128, 512), bf),
            pltpu.VMEM((4, 2, 128, 512), bf),
            pltpu.VMEM((4, 2, 128, 512), bf),
            pltpu.VMEM((128, 512), bf),
            pltpu.VMEM((128, 512), bf),
            pltpu.VMEM((128, 512), bf),
            pltpu.VMEM((128, 512), bf),
            pltpu.SemaphoreType.DMA((16,)),
            pltpu.SemaphoreType.DMA((4, 4)),
        ],
        compiler_params=pltpu.CompilerParams(
            collective_id=2, has_side_effects=True, vmem_limit_bytes=16 << 20
        ),
        name="reduce",
    )(qp, kp)


def mask_keys(ks, km):
    half = lax.broadcasted_iota(jnp.int32, (128, 128), 1) < HEAD
    for block in range(8):
        rows = slice(block * 128, (block + 1) * 128)
        for h in range(HEADS):
            kk = ks[rows, (h // 2) * 128 : (h // 2 + 1) * 128]
            keep = half if h % 2 == 0 else jnp.logical_not(half)
            km[h, rows, :] = jnp.where(keep, kk, jnp.zeros_like(kk))


def order_of(meta, which, g):
    return meta[which * NU + g]


def place_of(meta, which, g):
    return meta[NU + NV + which * NU + g]


def rows_of(g):
    return pl.ds(pl.multiple_of(g * GRAIN, GRAIN), GRAIN)


def chunk_bounds(meta, i):
    low = place_of(meta, 0, i * (UB // GRAIN))
    high = place_of(meta, 0, (i + 1) * (UB // GRAIN) - 1)
    per = VC // GRAIN
    first = jnp.int32(0)
    full = jnp.int32(0)
    for j in range(NV // per):
        first += (place_of(meta, 1, (j + 1) * per - 1) < low).astype(jnp.int32)
        full += (place_of(meta, 1, j * per) <= high).astype(jnp.int32)
    return first, full


def chunk_valid(meta, pu, j):
    off = lax.broadcasted_iota(jnp.int32, (GRAIN, UB), 0)
    per = VC // GRAIN
    pv = jnp.concatenate(
        [off + GRAIN * place_of(meta, 1, j * per + t) for t in range(per)], axis=0
    )
    return pv >= pu


def stats_kernel(
    q_ref, k_ref, f_ref, b_ref, meta, pu_ref, out, qs, ks, fs, bs, ws, ms, km, ft, bt, run_m, run_t, run_e, held, sem
):
    def flush(n):
        slot = n % SLOTS
        return pltpu.make_async_copy(held.at[slot], ws.at[n], sem.at[slot])

    for block in range(16):
        ft[block * 128 : (block + 1) * 128, :] = f_ref[block].T
    for block in range(8):
        bt[block * 128 : (block + 1) * 128, :] = b_ref[block].T

    def sort_sources(g, _):
        frm = rows_of(order_of(meta, 0, g))
        qs[rows_of(g), :] = q_ref[frm, :] * jnp.bfloat16(SCALE)
        fs[rows_of(g), :] = ft[frm, :]
        return 0

    def sort_targets(g, _):
        frm = rows_of(order_of(meta, 1, g))
        ks[rows_of(g), :] = k_ref[frm, :]
        bs[rows_of(g), :] = bt[frm, :]
        return 0

    lax.fori_loop(0, NU, sort_sources, 0)
    lax.fori_loop(0, NV, sort_targets, 0)
    mask_keys(ks, km)

    def sources(i, tile):
        us = pl.ds(pl.multiple_of(i * UB, UB), UB)
        first, full = chunk_bounds(meta, i)
        full += full % 2
        run_m[...] = jnp.full_like(run_m, TOP)
        run_t[...] = jnp.zeros_like(run_t)
        run_e[...] = jnp.zeros_like(run_e)

        def targets(j, width, masked):
            rows = width * VC
            vs = pl.ds(pl.multiple_of(j * VC, VC), rows)
            n = tile + j - first
            for t in range(width):

                @pl.when(n + t >= SLOTS)
                def _():
                    flush(n + t - SLOTS).wait()

            counts = nt(bs[vs, :], fs[us, :])
            if masked:
                valid = chunk_valid(meta, pu_ref[pl.ds(i, 1), :], j)
            for h in range(HEADS):
                scores = nt(km[h, vs, :], qs[us, (h // 2) * 128 : (h // 2 + 1) * 128])
                if masked:
                    scores = jnp.where(valid, scores, NEG)
                for t in range(rows // SUB):
                    part = slice(t * SUB, (t + 1) * SUB)
                    s = scores[part].reshape(SUB // 8, 8, UB)
                    old = run_m[h]
                    new = jnp.maximum(old, jnp.max(s, axis=0))
                    w = jnp.exp(s - new[None])
                    shrink = jnp.exp(old - new)
                    run_m[h] = new
                    run_t[h] = run_t[h] * shrink + jnp.sum(w, axis=0)
                    run_e[h] = run_e[h] * shrink + jnp.sum(
                        w * counts[part].reshape(SUB // 8, 8, UB), axis=0
                    )
                    at = t * SUB // VC
                    inner = t % (VC // SUB)
                    held[(n + at) % SLOTS, h, inner * SUB : (inner + 1) * SUB, :] = w.reshape(
                        SUB, UB
                    ).astype(jnp.bfloat16)
                    ms[n + at, h, inner] = new
            for t in range(width):
                flush(n + t).start()

        def masked_step(j, _):
            targets(j, 1, True)
            return 0

        def open_step(j, _):
            targets(full + 2 * j, 2, False)
            return 0

        lax.fori_loop(first, full, masked_step, 0)
        lax.fori_loop(0, (1024 // VC - full) // 2, open_step, 0)
        for h in range(HEADS):
            part_m = run_m[h]
            top = jnp.max(part_m, axis=0, keepdims=True)
            weight = jnp.exp(part_m - top)
            total = jnp.sum(run_t[h] * weight, axis=0, keepdims=True)
            expect = jnp.sum(run_e[h] * weight, axis=0, keepdims=True)
            some = total > 0.0
            safe = jnp.where(some, total, 1.0)
            log = jnp.where(some, top + jnp.log(safe), NEG)
            mean = expect / safe
            for t in range(UB // 128):
                at = i * (UB // 128) + t
                out[at, h : h + 1, :] = log[:, t * 128 : (t + 1) * 128]
                out[at, HEADS + h : HEADS + h + 1, :] = mean[:, t * 128 : (t + 1) * 128]
        return tile + 1024 // VC - first

    count = lax.fori_loop(0, 2048 // UB, sources, jnp.int32(0))
    for back in range(1, SLOTS + 1):

        @pl.when(count >= back)
        def _():
            flush(count - back).wait()


def stats(q, k, f, b, meta, pu):
    bf = jnp.bfloat16
    return pl.pallas_call(
        stats_kernel,
        in_specs=[VM] * 4 + [SM, VM],
        out_specs=[VM] * 5 + [pl.BlockSpec(memory_space=pl.ANY), VM],
        out_shape=[
            jax.ShapeDtypeStruct((16, 16, 128), jnp.float32),
            jax.ShapeDtypeStruct((2048, 512), bf),
            jax.ShapeDtypeStruct((1024, 512), bf),
            jax.ShapeDtypeStruct((2048, 256), bf),
            jax.ShapeDtypeStruct((1024, 256), bf),
            jax.ShapeDtypeStruct((TILES, HEADS, VC, UB), bf),
            jax.ShapeDtypeStruct((TILES, HEADS, VC // SUB, 8, UB), jnp.float32),
        ],
        scratch_shapes=[
            pltpu.VMEM((HEADS, 1024, 128), bf),
            pltpu.VMEM((2048, 256), bf),
            pltpu.VMEM((1024, 256), bf),
            pltpu.VMEM((HEADS, 8, UB), jnp.float32),
            pltpu.VMEM((HEADS, 8, UB), jnp.float32),
            pltpu.VMEM((HEADS, 8, UB), jnp.float32),
            pltpu.VMEM((SLOTS, HEADS, VC, UB), bf),
            pltpu.SemaphoreType.DMA((SLOTS,)),
        ],
        compiler_params=pltpu.CompilerParams(vmem_limit_bytes=12 << 20),
        name="stats",
    )(q, k, f, b, meta, pu)


def grads_kernel(qs, ks, fs, bs, ws, ms, meta, st, qg, kg, kt, qacc, kacc, held, sem):
    def fetch(n):
        slot = n % SLOTS
        return pltpu.make_async_copy(ws.at[n], held.at[slot], sem.at[slot])

    count = jnp.int32(0)
    for i in range(2048 // UB):
        count += 1024 // VC - chunk_bounds(meta, i)[0]
    for n in range(SLOTS):

        @pl.when(count > n)
        def _():
            fetch(n).start()

    for block in range(8):
        rows = slice(block * 128, (block + 1) * 128)
        kt[:, rows] = ks[rows, :].T
    kacc[...] = jnp.zeros_like(kacc)

    def sources(i, tile):
        us = pl.ds(pl.multiple_of(i * UB, UB), UB)
        first, _ = chunk_bounds(meta, i)
        both = jnp.concatenate([st[i * (UB // 128) + t] for t in range(UB // 128)], axis=1)
        qacc[...] = jnp.zeros_like(qacc)

        def targets(j, width):
            rows = width * VC
            vs = pl.ds(pl.multiple_of(j * VC, VC), rows)
            n = tile + j - first
            for t in range(width):
                fetch(n + t).wait()
            counts = nt(bs[vs, :], fs[us, :])
            low = lax.broadcasted_iota(jnp.int32, (rows, 128), 1) < HEAD
            pair = []
            for h in range(HEADS):
                log = both[h : h + 1]
                mean = both[HEADS + h : HEADS + h + 1]
                parts = []
                for t in range(rows // SUB):
                    at = t * SUB // VC
                    inner = t % (VC // SUB)
                    part = slice(t * SUB, (t + 1) * SUB)
                    w = held[(n + at) % SLOTS, h, inner * SUB : (inner + 1) * SUB, :].astype(
                        jnp.float32
                    )
                    scale = jnp.exp(ms[n + at, h, inner] - log)
                    w = (w.reshape(SUB // 8, 8, UB) * scale[None]).reshape(SUB, UB)
                    parts.append((w * (mean - counts[part])).astype(jnp.bfloat16))
                g = jnp.concatenate(parts, axis=0)
                hs = slice(h * HEAD, (h + 1) * HEAD)
                qacc[hs, :] += nn(kt[hs, vs], g)
                pair.append(nn(g, qs[us, (h // 2) * 128 : (h // 2 + 1) * 128]))
                if h % 2:
                    cols = slice((h // 2) * 128, (h // 2 + 1) * 128)
                    kacc[vs, cols] += jnp.where(low, pair[-2], pair[-1])
            for t in range(width):

                @pl.when(n + t + SLOTS < count)
                def _():
                    fetch(n + t + SLOTS).start()

        odd = first % 2

        def single(j, _):
            targets(first, 1)
            return 0

        def double(j, _):
            targets(first + odd + 2 * j, 2)
            return 0

        lax.fori_loop(0, odd, single, 0)
        lax.fori_loop(0, (1024 // VC - first) // 2, double, 0)
        turned = (qacc[...] * SCALE).T.astype(jnp.bfloat16)
        for t in range(UB // GRAIN):
            to = order_of(meta, 0, i * (UB // GRAIN) + t)
            qg[rows_of(to), :] = turned[t * GRAIN : (t + 1) * GRAIN]
        return tile + 1024 // VC - first

    lax.fori_loop(0, 2048 // UB, sources, jnp.int32(0))

    def unsort(g, _):
        kg[rows_of(order_of(meta, 1, g)), :] = kacc[rows_of(g), :].astype(jnp.bfloat16)
        return 0

    lax.fori_loop(0, NV, unsort, 0)


def grads(qs, ks, fs, bs, ws, ms, meta, st):
    bf = jnp.bfloat16
    return pl.pallas_call(
        grads_kernel,
        in_specs=[VM] * 4 + [pl.BlockSpec(memory_space=pl.ANY), VM, SM, VM],
        out_specs=[VM] * 2,
        out_shape=[
            jax.ShapeDtypeStruct((2048, 512), bf),
            jax.ShapeDtypeStruct((1024, 512), bf),
        ],
        scratch_shapes=[
            pltpu.VMEM((512, 1024), bf),
            pltpu.VMEM((512, UB), jnp.float32),
            pltpu.VMEM((1024, 512), jnp.float32),
            pltpu.VMEM((SLOTS, HEADS, VC, UB), bf),
            pltpu.SemaphoreType.DMA((SLOTS,)),
        ],
        compiler_params=pltpu.CompilerParams(vmem_limit_bytes=12 << 20),
        name="grads",
    )(qs, ks, fs, bs, ws, ms, meta, st)


def in_order(places):
    n = places.shape[0]
    rank = jnp.sum((places[None, :] < places[:, None]).astype(jnp.int32), axis=1)
    index = jnp.arange(n, dtype=jnp.int32)
    hit = rank[None, :] == index[:, None]
    return (
        jnp.sum(jnp.where(hit, index[None, :], 0), axis=1),
        jnp.sum(jnp.where(hit, places[None, :], 0), axis=1),
    )


def local(queries, keys, fwd_table, bwd_table, step_weight, block_order):
    row_id = lax.axis_index("row")
    col_id = lax.axis_index("col")
    scaled = (bwd_table.astype(jnp.float32) * step_weight[:, None]).astype(jnp.bfloat16)
    sf = fwd_table.reshape(2, 8, 16, 128).transpose(1, 2, 0, 3)
    sb = scaled.reshape(2, 8, 16, 128).transpose(1, 2, 0, 3)
    grid = block_order.reshape(8, 16, 4)
    line = lax.dynamic_index_in_dim(grid, row_id, 0, keepdims=False).reshape(64)
    column = lax.dynamic_index_in_dim(grid, col_id, 1, keepdims=False).reshape(32)
    order_u, place_u = in_order(line)
    order_v, place_v = in_order(column)
    meta = jnp.concatenate([order_u, order_v, place_u, place_v])
    offsets = jnp.arange(GRAIN, dtype=jnp.int32)
    pu = (place_u[:, None] * GRAIN + offsets[None, :]).reshape(8, 256)
    q, k, f, b = gather(queries, keys, sf, sb)
    part, qs, ks, fs, bs, ws, ms = stats(
        q.reshape(2048, 512),
        k.reshape(1024, 512),
        f.reshape(16, 256, 128),
        b.reshape(8, 256, 128),
        meta,
        pu,
    )
    qg, kg = grads(qs, ks, fs, bs, ws, ms, meta, merge(part))
    return reduce(qg.reshape(4, 2, 2, 128, 512), kg.reshape(2, 4, 128, 512))


def solution(mesh):
    return jax.shard_map(
        local,
        mesh=mesh,
        in_specs=(
            P(("row", "col"), None),
            P(("row", "col"), None),
            P(("row", "col"), None),
            P(("row", "col"), None),
            P(("row", "col")),
            P(),
        ),
        out_specs=(P(("row", "col"), None), P(("row", "col"), None)),
        check_vma=False,
    )
```

```python
import jax
import jax.numpy as jnp
from jax import lax
from jax.experimental import pallas as pl
from jax.experimental.pallas import tpu as pltpu
from jax.sharding import PartitionSpec as P

HEADS = 8
HEAD = 64
GRAIN = 32
SCALE = HEAD**-0.5
LOG_HEADS = 2.0794415416798357
NEG = -1e30
TOP = -1e29
NU = 64
NV = 32
TILES = 64
SLOTS = 4
UB = 256
VC = 128
SUB = 128
MESH = pl.DeviceIdType.MESH
VM = pl.BlockSpec(memory_space=pltpu.VMEM)
SM = pl.BlockSpec(memory_space=pltpu.SMEM)
HB = pl.BlockSpec(memory_space=pltpu.MemorySpace.HBM)


def nn(a, b):
    return lax.dot_general(a, b, (((1,), (0,)), ((), ())), preferred_element_type=jnp.float32)


def nt(a, b):
    return lax.dot_general(a, b, (((1,), (1,)), ((), ())), preferred_element_type=jnp.float32)


def remote(src, dst, send, recv, peer):
    return pltpu.make_async_remote_copy(
        src_ref=src, dst_ref=dst, send_sem=send, recv_sem=recv, device_id=peer, device_id_type=MESH
    )


def greet(peers):
    barrier = pltpu.get_barrier_semaphore()
    for peer in peers:
        pl.semaphore_signal(barrier, inc=1, device_id=peer, device_id_type=MESH)


def enter(peers):
    greet(peers)
    pl.semaphore_wait(pltpu.get_barrier_semaphore(), len(peers))


class Sends:
    def __init__(self, sems):
        self.sems = sems
        self.started = []

    def start(self, src, dst, recv, peer):
        copy = remote(src, dst, self.sems.at[len(self.started)], recv, peer)
        copy.start()
        self.started.append(copy)

    def drain(self):
        for copy in self.started:
            copy.wait_send()


def gather_kernel(
    q, k, fwd, bwd, weight, qa, ka, fa, ba, fv, bv, sf, sb, send, recv_q, recv_f, recv_k, recv_b, in_f, in_b, own
):
    row, col = lax.axis_index("row"), lax.axis_index("col")
    x, yh, core = col // 4, (col // 2) % 2, col % 2
    yl, z = row // 4, row % 4

    def at(r=None, c=None):
        return {"row": row if r is None else r, "col": col if c is None else c}

    def cslot(xx, yy, cc):
        return xx * 4 + yy * 2 + cc

    peers = [at(r=(row + d) % 8) for d in range(1, 8)] + [at(c=(col + d) % 16) for d in range(1, 16)]
    greet(peers)
    tables = [pltpu.make_async_copy(fwd, fv, own.at[0]), pltpu.make_async_copy(bwd, bv, own.at[1])]
    local = [
        pltpu.make_async_copy(q, qa.at[col], own.at[2]),
        pltpu.make_async_copy(k, ka.at[row], own.at[3]),
    ]
    for copy in tables + local:
        copy.start()
    step = jnp.where(lax.broadcasted_iota(jnp.int32, (2, 128), 0) == 0, weight[0], weight[1])
    tables[0].wait()
    tables[1].wait()
    for r in range(8):
        for c in range(16):
            cut = slice((r * 16 + c) * 128, (r * 16 + c + 1) * 128)
            sf[r, c] = fv[:, cut]
            sb[r, c] = (bv[:, cut].astype(jnp.float32) * step).astype(jnp.bfloat16)
    pl.semaphore_wait(pltpu.get_barrier_semaphore(), len(peers))
    sends = Sends(send)
    local += [
        pltpu.make_async_copy(sf.at[row], fa.at[:, col, row], own.at[4]),
        pltpu.make_async_copy(sb.at[:, col], ba.at[:, col, row], own.at[5]),
    ]
    local[2].start()
    local[3].start()
    for d in range(1, 16):
        to = (col + d) % 16
        sends.start(sb.at[:, to], ba.at[:, col, row], in_b.at[col], at(c=to))
    for d in range(1, 8):
        to = (row + d) % 8
        sends.start(sf.at[to], fa.at[:, col, row], in_f.at[row], at(r=to))

    def q_part(slot, half=None):
        return qa.at[slot] if half is None else qa.at[slot, pl.ds(half * 64, 64)]

    def f_part(slot, half=None):
        return fa.at[:, slot] if half is None else fa.at[pl.ds(half * 8, 8), slot]

    def k_part(slot, half=None):
        return ka.at[slot] if half is None else ka.at[slot, pl.ds(half * 64, 64)]

    def b_part(slot, half=None):
        return ba.at[:, :, slot] if half is None else ba.at[pl.ds(half * 4, 4), :, slot]

    def src_slot(dx, dy, cc=None):
        return cslot((x + dx) % 4, (yh + dy) % 2, core if cc is None else cc)

    def tgt_slot(dz, dy):
        return ((yl + dy) % 2) * 4 + (z + dz) % 4

    def src_dev(dx, dy, dc=0):
        return at(c=cslot((x + dx) % 4, (yh + dy) % 2, (core + dc) % 2))

    def tgt_dev(dz, dy):
        return at(r=tgt_slot(dz, dy))

    source = (src_slot, src_dev, True)
    target = (tgt_slot, tgt_dev, False)
    streams = {
        "q": (q_part, recv_q, source),
        "f": (f_part, recv_f, source),
        "k": (k_part, recv_k, target),
        "b": (b_part, recv_b, target),
    }

    def push(kind, slot, peer, half=None):
        part, recv, _ = streams[kind]
        ref = part(slot, half)
        sends.start(ref, ref, recv.at[slot, 0 if half is None else half], peer)

    def arrived(kind, slot, half=None):
        part, recv, _ = streams[kind]
        ref = part(slot, half)
        remote(ref, ref, send.at[0], recv.at[slot, 0 if half is None else half], at()).wait_recv()

    def first(kind):
        slot_of, dev_of, pair = streams[kind][2]
        mine = slot_of(0, 0)
        push(kind, mine, dev_of(0, 1))
        push(kind, mine, dev_of(1, 0))
        push(kind, mine, dev_of(3, 0))
        if pair:
            push(kind, mine, dev_of(0, 0, 1))

    def second(kind):
        slot_of, dev_of, pair = streams[kind][2]
        other = slot_of(0, 1)
        arrived(kind, other)
        push(kind, other, dev_of(1, 0))
        push(kind, other, dev_of(3, 0))
        if pair:
            push(kind, other, dev_of(0, 0, 1))

    def relay(kind, dy):
        slot_of, dev_of, pair = streams[kind][2]
        for step, half in ((3, 0), (1, 1)):
            slot = slot_of(step, dy)
            arrived(kind, slot)
            push(kind, slot, dev_of(4 - step, 0), half)
            if pair:
                push(kind, slot, dev_of(0, 0, 1))

    def last(kind, dy):
        slot_of, dev_of, pair = streams[kind][2]
        slot = slot_of(2, dy)
        arrived(kind, slot, 0)
        arrived(kind, slot, 1)
        if pair:
            push(kind, slot, dev_of(0, 0, 1))

    local[0].wait()
    local[1].wait()
    first("q")
    first("k")
    local[2].wait()
    for d in range(1, 8):
        frm = (row + d) % 8
        ref = fa.at[:, col, frm]
        remote(ref, ref, send.at[0], in_f.at[frm], at()).wait_recv()
    first("f")
    local[3].wait()
    for d in range(1, 16):
        frm = (col + d) % 16
        ref = ba.at[:, frm, row]
        remote(ref, ref, send.at[0], in_b.at[frm], at()).wait_recv()
    first("b")
    relay("k", 0)
    relay("q", 0)
    second("k")
    second("q")
    relay("b", 0)
    relay("f", 0)
    second("b")
    second("f")
    relay("k", 1)
    relay("q", 1)
    relay("b", 1)
    relay("f", 1)
    for dy in range(2):
        for kind in ("k", "q", "b", "f"):
            last(kind, dy)
    for kind in ("q", "f"):
        for dx in range(4):
            for dy in range(2):
                arrived(kind, src_slot(dx, dy, 1 - core))
    sends.drain()


def gather(q, k, fwd, bwd, weight):
    bf = jnp.bfloat16
    return pl.pallas_call(
        gather_kernel,
        in_specs=[HB] * 4 + [SM],
        out_specs=[VM] * 4,
        out_shape=[
            jax.ShapeDtypeStruct((16, 128, 512), bf),
            jax.ShapeDtypeStruct((8, 128, 512), bf),
            jax.ShapeDtypeStruct((16, 16, 8, 2, 128), bf),
            jax.ShapeDtypeStruct((8, 16, 8, 2, 128), bf),
        ],
        scratch_shapes=[
            pltpu.VMEM((2, 16384), bf),
            pltpu.VMEM((2, 16384), bf),
            pltpu.VMEM((8, 16, 2, 128), bf),
            pltpu.VMEM((8, 16, 2, 128), bf),
            pltpu.SemaphoreType.DMA((100,)),
            pltpu.SemaphoreType.DMA((16, 2)),
            pltpu.SemaphoreType.DMA((16, 2)),
            pltpu.SemaphoreType.DMA((8, 2)),
            pltpu.SemaphoreType.DMA((8, 2)),
            pltpu.SemaphoreType.DMA((8,)),
            pltpu.SemaphoreType.DMA((16,)),
            pltpu.SemaphoreType.DMA((6,)),
        ],
        compiler_params=pltpu.CompilerParams(
            collective_id=0, has_side_effects=True, vmem_limit_bytes=16 << 20
        ),
        name="gather",
    )(q, k, fwd, bwd, weight)


def merge_kernel(part, out, landed, mine, send, recv, recv2, own):
    row, col = lax.axis_index("row"), lax.axis_index("col")
    peers = [{"row": row, "col": (col + d) % 16} for d in range(1, 16)]
    enter(peers)
    sends = Sends(send)
    keep = pltpu.make_async_copy(part.at[col], landed.at[col], own.at[0])
    keep.start()
    for d, peer in enumerate(peers):
        sends.start(part.at[peer["col"]], landed.at[col], recv.at[col], peer)
    keep.wait()
    for peer in peers:
        ref = landed.at[peer["col"]]
        remote(ref, ref, send.at[0], recv.at[peer["col"]], peer).wait_recv()
    logs = landed[:, 0:8]
    top = jnp.max(logs, axis=0)
    weight = jnp.exp(logs - top[None])
    total = jnp.sum(weight, axis=0)
    mean = jnp.sum(weight * landed[:, 8:16], axis=0) / total
    mine[0:8, :] = top + jnp.log(total) + LOG_HEADS
    mine[8:16, :] = mean
    keep = pltpu.make_async_copy(mine, out.at[col], own.at[1])
    keep.start()
    for peer in peers:
        sends.start(mine, out.at[col], recv2.at[col], peer)
    keep.wait()
    for peer in peers:
        ref = out.at[peer["col"]]
        remote(ref, ref, send.at[0], recv2.at[peer["col"]], peer).wait_recv()
    sends.drain()


def merge(part):
    return pl.pallas_call(
        merge_kernel,
        in_specs=[VM],
        out_specs=VM,
        out_shape=jax.ShapeDtypeStruct((16, 16, 128), jnp.float32),
        scratch_shapes=[
            pltpu.VMEM((16, 16, 128), jnp.float32),
            pltpu.VMEM((16, 128), jnp.float32),
            pltpu.SemaphoreType.DMA((30,)),
            pltpu.SemaphoreType.DMA((16,)),
            pltpu.SemaphoreType.DMA((16,)),
            pltpu.SemaphoreType.DMA((2,)),
        ],
        compiler_params=pltpu.CompilerParams(
            collective_id=1, has_side_effects=True, vmem_limit_bytes=4 << 20
        ),
        name="merge",
    )(part)


def reduce_kernel(qp, kp, qo, ko, pair_in, pair_sum, ring_q, ring_k, out_q, out_k, last_q, last_k, send, recv):
    row, col = lax.axis_index("row"), lax.axis_index("col")
    x, yh, core = col // 4, (col // 2) % 2, col % 2
    yl, z = row // 4, row % 4

    def q_dev(xx, yy, cc):
        return {"row": row, "col": xx * 4 + yy * 2 + cc}

    def k_dev(yy, zz):
        return {"row": yy * 4 + zz, "col": col}

    sibling = q_dev(x, yh, 1 - core)
    ring_x = [(x + d) % 4 for d in range(1, 4)]
    ring_z = [(z + d) % 4 for d in range(1, 4)]
    enter(
        [sibling, q_dev(x, 1 - yh, core), k_dev(1 - yl, z)]
        + [q_dev(xx, yh, core) for xx in ring_x]
        + [k_dev(yl, zz) for zz in ring_z]
    )
    sends = Sends(send)
    order_x = [ring_x[1], ring_x[0], ring_x[2], x]
    for xx in order_x:
        sends.start(qp.at[xx, :, 1 - core], pair_in.at[xx], recv.at[0, xx], sibling)
    for zz in (ring_z[1], ring_z[0], ring_z[2]):
        sends.start(kp.at[:, zz], ring_k.at[z], recv.at[1, z], k_dev(yl, zz))
    for at, xx in enumerate(order_x):
        ref = pair_in.at[xx]
        remote(ref, ref, send.at[0], recv.at[0, xx], sibling).wait_recv()
        pair_sum[xx] = (
            qp[xx, :, core].astype(jnp.float32) + pair_in[xx].astype(jnp.float32)
        ).astype(jnp.bfloat16)
        if at < 3:
            sends.start(pair_sum.at[xx], ring_q.at[x], recv.at[2, x], q_dev(xx, yh, core))

    def finish(own, landed, ring, which, pos, stage, last, out, peer, slot):
        for at in ring:
            ref = landed.at[at]
            remote(ref, ref, send.at[0], recv.at[which, at], peer).wait_recv()
        total = own(1 - pos).astype(jnp.float32)
        for at in ring:
            total = total + landed[at, 1 - pos].astype(jnp.float32)
        stage[...] = total.astype(jnp.bfloat16)
        sends.start(stage, last, recv.at[3, slot], peer)
        total = own(pos).astype(jnp.float32)
        for at in ring:
            total = total + landed[at, pos].astype(jnp.float32)
        out[...] = total

    pair_y = q_dev(x, 1 - yh, core)
    pair_r = k_dev(1 - yl, z)
    finish(lambda y: kp[y, z], ring_k, ring_z, 1, yl, out_k, last_k, ko, pair_r, 0)
    finish(lambda y: pair_sum[x, y], ring_q, ring_x, 2, yh, out_q, last_q, qo, pair_y, 1)
    remote(last_k, last_k, send.at[0], recv.at[3, 0], pair_r).wait_recv()
    ko[...] += last_k[...].astype(jnp.float32)
    remote(last_q, last_q, send.at[0], recv.at[3, 1], pair_y).wait_recv()
    qo[...] += last_q[...].astype(jnp.float32)
    sends.drain()


def reduce(qp, kp):
    bf = jnp.bfloat16
    return pl.pallas_call(
        reduce_kernel,
        in_specs=[VM] * 2,
        out_specs=[VM] * 2,
        out_shape=[jax.ShapeDtypeStruct((128, 512), jnp.float32)] * 2,
        scratch_shapes=[
            pltpu.VMEM((4, 2, 128, 512), bf),
            pltpu.VMEM((4, 2, 128, 512), bf),
            pltpu.VMEM((4, 2, 128, 512), bf),
            pltpu.VMEM((4, 2, 128, 512), bf),
            pltpu.VMEM((128, 512), bf),
            pltpu.VMEM((128, 512), bf),
            pltpu.VMEM((128, 512), bf),
            pltpu.VMEM((128, 512), bf),
            pltpu.SemaphoreType.DMA((16,)),
            pltpu.SemaphoreType.DMA((4, 4)),
        ],
        compiler_params=pltpu.CompilerParams(
            collective_id=2, has_side_effects=True, vmem_limit_bytes=16 << 20
        ),
        name="reduce",
    )(qp, kp)


def mask_keys(ks, km):
    half = lax.broadcasted_iota(jnp.int32, (128, 128), 1) < HEAD
    for block in range(8):
        rows = slice(block * 128, (block + 1) * 128)
        for h in range(HEADS):
            kk = ks[rows, (h // 2) * 128 : (h // 2 + 1) * 128]
            keep = half if h % 2 == 0 else jnp.logical_not(half)
            km[h, rows, :] = jnp.where(keep, kk, jnp.zeros_like(kk))


def order_of(meta, which, g):
    return meta[which * NU + g]


def place_of(meta, which, g):
    return meta[NU + NV + which * NU + g]


def rows_of(g):
    return pl.ds(pl.multiple_of(g * GRAIN, GRAIN), GRAIN)


def chunk_bounds(meta, i):
    low = place_of(meta, 0, i * (UB // GRAIN))
    high = place_of(meta, 0, (i + 1) * (UB // GRAIN) - 1)
    per = VC // GRAIN
    first = jnp.int32(0)
    full = jnp.int32(0)
    for j in range(NV // per):
        first += (place_of(meta, 1, (j + 1) * per - 1) < low).astype(jnp.int32)
        full += (place_of(meta, 1, j * per) <= high).astype(jnp.int32)
    return first, full


def chunk_valid(meta, pu, j):
    off = lax.broadcasted_iota(jnp.int32, (GRAIN, UB), 0)
    per = VC // GRAIN
    pv = jnp.concatenate(
        [off + GRAIN * place_of(meta, 1, j * per + t) for t in range(per)], axis=0
    )
    return pv >= pu


def stats_kernel(
    q_ref, k_ref, f_ref, b_ref, meta, pu_ref, out, qs, ks, ws, ms, cs, fs, bs, km, ft, bt, run_m, run_t, run_e, held, sem
):
    def flush(n):
        slot = n % SLOTS
        return pltpu.make_async_copy(held.at[slot], ws.at[n], sem.at[slot])

    for block in range(16):
        ft[block * 128 : (block + 1) * 128, :] = f_ref[block].T
    for block in range(8):
        bt[block * 128 : (block + 1) * 128, :] = b_ref[block].T

    def sort_sources(g, _):
        frm = rows_of(order_of(meta, 0, g))
        qs[rows_of(g), :] = q_ref[frm, :] * jnp.bfloat16(SCALE)
        fs[rows_of(g), :] = ft[frm, :]
        return 0

    def sort_targets(g, _):
        frm = rows_of(order_of(meta, 1, g))
        ks[rows_of(g), :] = k_ref[frm, :]
        bs[rows_of(g), :] = bt[frm, :]
        return 0

    lax.fori_loop(0, NU, sort_sources, 0)
    lax.fori_loop(0, NV, sort_targets, 0)
    mask_keys(ks, km)

    def sources(i, tile):
        us = pl.ds(pl.multiple_of(i * UB, UB), UB)
        first, full = chunk_bounds(meta, i)
        full += full % 2
        run_m[...] = jnp.full_like(run_m, TOP)
        run_t[...] = jnp.zeros_like(run_t)
        run_e[...] = jnp.zeros_like(run_e)

        def targets(j, width, masked):
            rows = width * VC
            vs = pl.ds(pl.multiple_of(j * VC, VC), rows)
            n = tile + j - first
            for t in range(width):

                @pl.when(n + t >= SLOTS)
                def _():
                    flush(n + t - SLOTS).wait()

            counts = nt(bs[vs, :], fs[us, :])
            if masked:
                valid = chunk_valid(meta, pu_ref[pl.ds(i, 1), :], j)
            for h in range(HEADS):
                scores = nt(km[h, vs, :], qs[us, (h // 2) * 128 : (h // 2 + 1) * 128])
                if masked:
                    scores = jnp.where(valid, scores, NEG)
                for t in range(rows // SUB):
                    part = slice(t * SUB, (t + 1) * SUB)
                    s = scores[part].reshape(SUB // 8, 8, UB)
                    old = run_m[h]
                    new = jnp.maximum(old, jnp.max(s, axis=0))
                    w = jnp.exp(s - new[None])
                    shrink = jnp.exp(old - new)
                    run_m[h] = new
                    run_t[h] = run_t[h] * shrink + jnp.sum(w, axis=0)
                    run_e[h] = run_e[h] * shrink + jnp.sum(
                        w * counts[part].reshape(SUB // 8, 8, UB), axis=0
                    )
                    at = t * SUB // VC
                    inner = t % (VC // SUB)
                    held[(n + at) % SLOTS, h, inner * SUB : (inner + 1) * SUB, :] = w.reshape(
                        SUB, UB
                    ).astype(jnp.bfloat16)
                    ms[n + at, h, inner] = new
            for t in range(width):
                cs[n + t] = counts[t * VC : (t + 1) * VC]
                flush(n + t).start()

        def masked_step(j, _):
            targets(j, 1, True)
            return 0

        def open_step(j, _):
            targets(full + 2 * j, 2, False)
            return 0

        lax.fori_loop(first, full, masked_step, 0)
        lax.fori_loop(0, (1024 // VC - full) // 2, open_step, 0)
        for h in range(HEADS):
            part_m = run_m[h]
            top = jnp.max(part_m, axis=0, keepdims=True)
            weight = jnp.exp(part_m - top)
            total = jnp.sum(run_t[h] * weight, axis=0, keepdims=True)
            expect = jnp.sum(run_e[h] * weight, axis=0, keepdims=True)
            some = total > 0.0
            safe = jnp.where(some, total, 1.0)
            log = jnp.where(some, top + jnp.log(safe), NEG)
            mean = expect / safe
            for t in range(UB // 128):
                at = i * (UB // 128) + t
                out[at, h : h + 1, :] = log[:, t * 128 : (t + 1) * 128]
                out[at, HEADS + h : HEADS + h + 1, :] = mean[:, t * 128 : (t + 1) * 128]
        return tile + 1024 // VC - first

    count = lax.fori_loop(0, 2048 // UB, sources, jnp.int32(0))
    for back in range(1, SLOTS + 1):

        @pl.when(count >= back)
        def _():
            flush(count - back).wait()


def stats(q, k, f, b, meta, pu):
    bf = jnp.bfloat16
    return pl.pallas_call(
        stats_kernel,
        in_specs=[VM] * 4 + [SM, VM],
        out_specs=[VM] * 3 + [pl.BlockSpec(memory_space=pl.ANY), VM, VM],
        out_shape=[
            jax.ShapeDtypeStruct((16, 16, 128), jnp.float32),
            jax.ShapeDtypeStruct((2048, 512), bf),
            jax.ShapeDtypeStruct((1024, 512), bf),
            jax.ShapeDtypeStruct((TILES, HEADS, VC, UB), bf),
            jax.ShapeDtypeStruct((TILES, HEADS, VC // SUB, 8, UB), jnp.float32),
            jax.ShapeDtypeStruct((TILES, VC, UB), jnp.float32),
        ],
        scratch_shapes=[
            pltpu.VMEM((2048, 256), bf),
            pltpu.VMEM((1024, 256), bf),
            pltpu.VMEM((HEADS, 1024, 128), bf),
            pltpu.VMEM((2048, 256), bf),
            pltpu.VMEM((1024, 256), bf),
            pltpu.VMEM((HEADS, 8, UB), jnp.float32),
            pltpu.VMEM((HEADS, 8, UB), jnp.float32),
            pltpu.VMEM((HEADS, 8, UB), jnp.float32),
            pltpu.VMEM((SLOTS, HEADS, VC, UB), bf),
            pltpu.SemaphoreType.DMA((SLOTS,)),
        ],
        compiler_params=pltpu.CompilerParams(vmem_limit_bytes=12 << 20),
        name="stats",
    )(q, k, f, b, meta, pu)


def grads_kernel(qs, ks, ws, ms, cs, meta, st, qg, kg, kt, qacc, kacc, held, sem):
    def fetch(n):
        slot = n % SLOTS
        return pltpu.make_async_copy(ws.at[n], held.at[slot], sem.at[slot])

    count = jnp.int32(0)
    for i in range(2048 // UB):
        count += 1024 // VC - chunk_bounds(meta, i)[0]
    for n in range(SLOTS):

        @pl.when(count > n)
        def _():
            fetch(n).start()

    for block in range(8):
        rows = slice(block * 128, (block + 1) * 128)
        kt[:, rows] = ks[rows, :].T
    kacc[...] = jnp.zeros_like(kacc)

    def sources(i, tile):
        us = pl.ds(pl.multiple_of(i * UB, UB), UB)
        first, _ = chunk_bounds(meta, i)
        both = jnp.concatenate([st[i * (UB // 128) + t] for t in range(UB // 128)], axis=1)
        qacc[...] = jnp.zeros_like(qacc)

        def targets(j, width):
            rows = width * VC
            vs = pl.ds(pl.multiple_of(j * VC, VC), rows)
            n = tile + j - first
            for t in range(width):
                fetch(n + t).wait()
            low = lax.broadcasted_iota(jnp.int32, (rows, 128), 1) < HEAD
            pair = []
            for h in range(HEADS):
                log = both[h : h + 1]
                mean = both[HEADS + h : HEADS + h + 1]
                parts = []
                for t in range(rows // SUB):
                    at = t * SUB // VC
                    inner = t % (VC // SUB)
                    w = held[(n + at) % SLOTS, h, inner * SUB : (inner + 1) * SUB, :].astype(
                        jnp.float32
                    )
                    scale = jnp.exp(ms[n + at, h, inner] - log)
                    w = (w.reshape(SUB // 8, 8, UB) * scale[None]).reshape(SUB, UB)
                    counts = cs[n + at, inner * SUB : (inner + 1) * SUB, :]
                    parts.append((w * (mean - counts)).astype(jnp.bfloat16))
                g = jnp.concatenate(parts, axis=0)
                hs = slice(h * HEAD, (h + 1) * HEAD)
                qacc[hs, :] += nn(kt[hs, vs], g)
                pair.append(nn(g, qs[us, (h // 2) * 128 : (h // 2 + 1) * 128]))
                if h % 2:
                    cols = slice((h // 2) * 128, (h // 2 + 1) * 128)
                    kacc[vs, cols] += jnp.where(low, pair[-2], pair[-1])
            for t in range(width):

                @pl.when(n + t + SLOTS < count)
                def _():
                    fetch(n + t + SLOTS).start()

        odd = first % 2

        def single(j, _):
            targets(first, 1)
            return 0

        def double(j, _):
            targets(first + odd + 2 * j, 2)
            return 0

        lax.fori_loop(0, odd, single, 0)
        lax.fori_loop(0, (1024 // VC - first) // 2, double, 0)
        turned = (qacc[...] * SCALE).T.astype(jnp.bfloat16)
        for t in range(UB // GRAIN):
            to = order_of(meta, 0, i * (UB // GRAIN) + t)
            qg[rows_of(to), :] = turned[t * GRAIN : (t + 1) * GRAIN]
        return tile + 1024 // VC - first

    lax.fori_loop(0, 2048 // UB, sources, jnp.int32(0))

    def unsort(g, _):
        kg[rows_of(order_of(meta, 1, g)), :] = kacc[rows_of(g), :].astype(jnp.bfloat16)
        return 0

    lax.fori_loop(0, NV, unsort, 0)


def grads(qs, ks, ws, ms, cs, meta, st):
    bf = jnp.bfloat16
    return pl.pallas_call(
        grads_kernel,
        in_specs=[VM] * 2 + [pl.BlockSpec(memory_space=pl.ANY), VM, VM, SM, VM],
        out_specs=[VM] * 2,
        out_shape=[
            jax.ShapeDtypeStruct((2048, 512), bf),
            jax.ShapeDtypeStruct((1024, 512), bf),
        ],
        scratch_shapes=[
            pltpu.VMEM((512, 1024), bf),
            pltpu.VMEM((512, UB), jnp.float32),
            pltpu.VMEM((1024, 512), jnp.float32),
            pltpu.VMEM((SLOTS, HEADS, VC, UB), bf),
            pltpu.SemaphoreType.DMA((SLOTS,)),
        ],
        compiler_params=pltpu.CompilerParams(vmem_limit_bytes=12 << 20),
        name="grads",
    )(qs, ks, ws, ms, cs, meta, st)


def in_order(places):
    n = places.shape[0]
    rank = jnp.sum((places[None, :] < places[:, None]).astype(jnp.int32), axis=1)
    index = jnp.arange(n, dtype=jnp.int32)
    hit = rank[None, :] == index[:, None]
    return (
        jnp.sum(jnp.where(hit, index[None, :], 0), axis=1),
        jnp.sum(jnp.where(hit, places[None, :], 0), axis=1),
    )


def local(queries, keys, fwd_table, bwd_table, step_weight, block_order):
    row_id = lax.axis_index("row")
    col_id = lax.axis_index("col")
    grid = block_order.reshape(8, 16, 4)
    line = lax.dynamic_index_in_dim(grid, row_id, 0, keepdims=False).reshape(64)
    column = lax.dynamic_index_in_dim(grid, col_id, 1, keepdims=False).reshape(32)
    order_u, place_u = in_order(line)
    order_v, place_v = in_order(column)
    meta = jnp.concatenate([order_u, order_v, place_u, place_v])
    offsets = jnp.arange(GRAIN, dtype=jnp.int32)
    pu = (place_u[:, None] * GRAIN + offsets[None, :]).reshape(8, 256)
    here = [
        pltpu.with_memory_space_constraint(a, pltpu.MemorySpace.HBM)
        for a in (queries, keys, fwd_table, bwd_table)
    ]
    q, k, f, b = gather(*here, step_weight)
    part, qs, ks, ws, ms, cs = stats(
        q.reshape(2048, 512),
        k.reshape(1024, 512),
        f.reshape(16, 256, 128),
        b.reshape(8, 256, 128),
        meta,
        pu,
    )
    qg, kg = grads(qs, ks, ws, ms, cs, meta, merge(part))
    return reduce(qg.reshape(4, 2, 2, 128, 512), kg.reshape(2, 4, 128, 512))


def solution(mesh):
    return jax.shard_map(
        local,
        mesh=mesh,
        in_specs=(
            P(("row", "col"), None),
            P(("row", "col"), None),
            P(("row", "col"), None),
            P(("row", "col"), None),
            P(("row", "col")),
            P(),
        ),
        out_specs=(P(("row", "col"), None), P(("row", "col"), None)),
        check_vma=False,
    )
```

```python
import jax
import jax.numpy as jnp
from jax import lax
from jax.experimental import pallas as pl
from jax.experimental.pallas import tpu as pltpu
from jax.sharding import PartitionSpec as P

HEADS = 8
HEAD = 64
GRAIN = 32
SCALE = HEAD**-0.5
LOG_HEADS = 2.0794415416798357
NEG = -1e30
TOP = -1e29
NU = 64
NV = 32
TILES = 64
SLOTS = 4
UB = 256
VC = 128
SUB = 128
MESH = pl.DeviceIdType.MESH
VM = pl.BlockSpec(memory_space=pltpu.VMEM)
SM = pl.BlockSpec(memory_space=pltpu.SMEM)
HB = pl.BlockSpec(memory_space=pltpu.MemorySpace.HBM)


def nn(a, b):
    return lax.dot_general(a, b, (((1,), (0,)), ((), ())), preferred_element_type=jnp.float32)


def nt(a, b):
    return lax.dot_general(a, b, (((1,), (1,)), ((), ())), preferred_element_type=jnp.float32)


def remote(src, dst, send, recv, peer):
    return pltpu.make_async_remote_copy(
        src_ref=src, dst_ref=dst, send_sem=send, recv_sem=recv, device_id=peer, device_id_type=MESH
    )


def greet(peers):
    barrier = pltpu.get_barrier_semaphore()
    for peer in peers:
        pl.semaphore_signal(barrier, inc=1, device_id=peer, device_id_type=MESH)


def enter(peers):
    greet(peers)
    pl.semaphore_wait(pltpu.get_barrier_semaphore(), len(peers))


class Sends:
    def __init__(self, sems):
        self.sems = sems
        self.started = []

    def start(self, src, dst, recv, peer):
        copy = remote(src, dst, self.sems.at[len(self.started)], recv, peer)
        copy.start()
        self.started.append(copy)

    def drain(self):
        for copy in self.started:
            copy.wait_send()


def gather_kernel(
    q, k, fwd, bwd, weight, qa, ka, fa, ba, fv, bv, sf, sb, send, recv_q, recv_f, recv_k, recv_b, in_f, in_b, own
):
    row, col = lax.axis_index("row"), lax.axis_index("col")
    x, yh, core = col // 4, (col // 2) % 2, col % 2
    yl, z = row // 4, row % 4

    def at(r=None, c=None):
        return {"row": row if r is None else r, "col": col if c is None else c}

    def cslot(xx, yy, cc):
        return xx * 4 + yy * 2 + cc

    peers = [at(r=(row + d) % 8) for d in range(1, 8)] + [at(c=(col + d) % 16) for d in range(1, 16)]
    greet(peers)
    tables = [pltpu.make_async_copy(fwd, fv, own.at[0]), pltpu.make_async_copy(bwd, bv, own.at[1])]
    local = [
        pltpu.make_async_copy(q, qa.at[col], own.at[2]),
        pltpu.make_async_copy(k, ka.at[row], own.at[3]),
    ]
    for copy in tables + local:
        copy.start()
    step = jnp.where(lax.broadcasted_iota(jnp.int32, (2, 128), 0) == 0, weight[0], weight[1])
    tables[0].wait()
    tables[1].wait()
    for r in range(8):
        for c in range(16):
            cut = slice((r * 16 + c) * 128, (r * 16 + c + 1) * 128)
            sf[r, c] = fv[:, cut]
            sb[r, c] = (bv[:, cut].astype(jnp.float32) * step).astype(jnp.bfloat16)
    pl.semaphore_wait(pltpu.get_barrier_semaphore(), len(peers))
    sends = Sends(send)
    local += [
        pltpu.make_async_copy(sf.at[row], fa.at[:, col, row], own.at[4]),
        pltpu.make_async_copy(sb.at[:, col], ba.at[:, col, row], own.at[5]),
    ]
    local[2].start()
    local[3].start()
    for d in range(1, 16):
        to = (col + d) % 16
        sends.start(sb.at[:, to], ba.at[:, col, row], in_b.at[col], at(c=to))
    for d in range(1, 8):
        to = (row + d) % 8
        sends.start(sf.at[to], fa.at[:, col, row], in_f.at[row], at(r=to))

    def q_part(slot, half=None):
        return qa.at[slot] if half is None else qa.at[slot, pl.ds(half * 64, 64)]

    def f_part(slot, half=None):
        return fa.at[:, slot] if half is None else fa.at[pl.ds(half * 8, 8), slot]

    def k_part(slot, half=None):
        return ka.at[slot] if half is None else ka.at[slot, pl.ds(half * 64, 64)]

    def b_part(slot, half=None):
        return ba.at[:, :, slot] if half is None else ba.at[pl.ds(half * 4, 4), :, slot]

    def src_slot(dx, dy, cc=None):
        return cslot((x + dx) % 4, (yh + dy) % 2, core if cc is None else cc)

    def tgt_slot(dz, dy):
        return ((yl + dy) % 2) * 4 + (z + dz) % 4

    def src_dev(dx, dy, dc=0):
        return at(c=cslot((x + dx) % 4, (yh + dy) % 2, (core + dc) % 2))

    def tgt_dev(dz, dy):
        return at(r=tgt_slot(dz, dy))

    source = (src_slot, src_dev, True)
    target = (tgt_slot, tgt_dev, False)
    streams = {
        "q": (q_part, recv_q, source),
        "f": (f_part, recv_f, source),
        "k": (k_part, recv_k, target),
        "b": (b_part, recv_b, target),
    }

    def push(kind, slot, peer, half=None):
        part, recv, _ = streams[kind]
        ref = part(slot, half)
        sends.start(ref, ref, recv.at[slot, 0 if half is None else half], peer)

    def arrived(kind, slot, half=None):
        part, recv, _ = streams[kind]
        ref = part(slot, half)
        remote(ref, ref, send.at[0], recv.at[slot, 0 if half is None else half], at()).wait_recv()

    def first(kind):
        slot_of, dev_of, pair = streams[kind][2]
        mine = slot_of(0, 0)
        push(kind, mine, dev_of(0, 1))
        push(kind, mine, dev_of(1, 0))
        push(kind, mine, dev_of(3, 0))
        if pair:
            push(kind, mine, dev_of(0, 0, 1))

    def second(kind):
        slot_of, dev_of, pair = streams[kind][2]
        other = slot_of(0, 1)
        arrived(kind, other)
        push(kind, other, dev_of(1, 0))
        push(kind, other, dev_of(3, 0))
        if pair:
            push(kind, other, dev_of(0, 0, 1))

    def relay(kind, dy):
        slot_of, dev_of, pair = streams[kind][2]
        for step, half in ((3, 0), (1, 1)):
            slot = slot_of(step, dy)
            arrived(kind, slot)
            push(kind, slot, dev_of(4 - step, 0), half)
            if pair:
                push(kind, slot, dev_of(0, 0, 1))

    def last(kind, dy):
        slot_of, dev_of, pair = streams[kind][2]
        slot = slot_of(2, dy)
        arrived(kind, slot, 0)
        arrived(kind, slot, 1)
        if pair:
            push(kind, slot, dev_of(0, 0, 1))

    local[0].wait()
    local[1].wait()
    first("q")
    first("k")
    local[2].wait()
    for d in range(1, 8):
        frm = (row + d) % 8
        ref = fa.at[:, col, frm]
        remote(ref, ref, send.at[0], in_f.at[frm], at()).wait_recv()
    first("f")
    local[3].wait()
    for d in range(1, 16):
        frm = (col + d) % 16
        ref = ba.at[:, frm, row]
        remote(ref, ref, send.at[0], in_b.at[frm], at()).wait_recv()
    first("b")
    relay("k", 0)
    relay("q", 0)
    second("k")
    second("q")
    relay("b", 0)
    relay("f", 0)
    second("b")
    second("f")
    relay("k", 1)
    relay("q", 1)
    relay("b", 1)
    relay("f", 1)
    for dy in range(2):
        for kind in ("k", "q", "b", "f"):
            last(kind, dy)
    for kind in ("q", "f"):
        for dx in range(4):
            for dy in range(2):
                arrived(kind, src_slot(dx, dy, 1 - core))
    sends.drain()


def gather(q, k, fwd, bwd, weight):
    bf = jnp.bfloat16
    return pl.pallas_call(
        gather_kernel,
        in_specs=[HB] * 4 + [SM],
        out_specs=[VM] * 4,
        out_shape=[
            jax.ShapeDtypeStruct((16, 128, 512), bf),
            jax.ShapeDtypeStruct((8, 128, 512), bf),
            jax.ShapeDtypeStruct((16, 16, 8, 2, 128), bf),
            jax.ShapeDtypeStruct((8, 16, 8, 2, 128), bf),
        ],
        scratch_shapes=[
            pltpu.VMEM((2, 16384), bf),
            pltpu.VMEM((2, 16384), bf),
            pltpu.VMEM((8, 16, 2, 128), bf),
            pltpu.VMEM((8, 16, 2, 128), bf),
            pltpu.SemaphoreType.DMA((100,)),
            pltpu.SemaphoreType.DMA((16, 2)),
            pltpu.SemaphoreType.DMA((16, 2)),
            pltpu.SemaphoreType.DMA((8, 2)),
            pltpu.SemaphoreType.DMA((8, 2)),
            pltpu.SemaphoreType.DMA((8,)),
            pltpu.SemaphoreType.DMA((16,)),
            pltpu.SemaphoreType.DMA((6,)),
        ],
        compiler_params=pltpu.CompilerParams(
            collective_id=0, has_side_effects=True, vmem_limit_bytes=16 << 20
        ),
        name="gather",
    )(q, k, fwd, bwd, weight)


def merge_kernel(part, out, landed, mine, send, recv, recv2, own):
    row, col = lax.axis_index("row"), lax.axis_index("col")
    peers = [{"row": row, "col": (col + d) % 16} for d in range(1, 16)]
    enter(peers)
    sends = Sends(send)
    keep = pltpu.make_async_copy(part.at[col], landed.at[col], own.at[0])
    keep.start()
    for d, peer in enumerate(peers):
        sends.start(part.at[peer["col"]], landed.at[col], recv.at[col], peer)
    keep.wait()
    for peer in peers:
        ref = landed.at[peer["col"]]
        remote(ref, ref, send.at[0], recv.at[peer["col"]], peer).wait_recv()
    logs = landed[:, 0:8]
    top = jnp.max(logs, axis=0)
    weight = jnp.exp(logs - top[None])
    total = jnp.sum(weight, axis=0)
    mean = jnp.sum(weight * landed[:, 8:16], axis=0) / total
    mine[0:8, :] = top + jnp.log(total) + LOG_HEADS
    mine[8:16, :] = mean
    keep = pltpu.make_async_copy(mine, out.at[col], own.at[1])
    keep.start()
    for peer in peers:
        sends.start(mine, out.at[col], recv2.at[col], peer)
    keep.wait()
    for peer in peers:
        ref = out.at[peer["col"]]
        remote(ref, ref, send.at[0], recv2.at[peer["col"]], peer).wait_recv()
    sends.drain()


def merge(part):
    return pl.pallas_call(
        merge_kernel,
        in_specs=[VM],
        out_specs=VM,
        out_shape=jax.ShapeDtypeStruct((16, 16, 128), jnp.float32),
        scratch_shapes=[
            pltpu.VMEM((16, 16, 128), jnp.float32),
            pltpu.VMEM((16, 128), jnp.float32),
            pltpu.SemaphoreType.DMA((30,)),
            pltpu.SemaphoreType.DMA((16,)),
            pltpu.SemaphoreType.DMA((16,)),
            pltpu.SemaphoreType.DMA((2,)),
        ],
        compiler_params=pltpu.CompilerParams(
            collective_id=1, has_side_effects=True, vmem_limit_bytes=4 << 20
        ),
        name="merge",
    )(part)


def reduce_kernel(
    qp, kp, qo, ko, pair_in, pair_sum, hop_q, acc_q, fin_q, hop_k, acc_k, fin_k, out_q, out_k, last_q, last_k, send, recv
):
    row, col = lax.axis_index("row"), lax.axis_index("col")
    x, yh, core = col // 4, (col // 2) % 2, col % 2
    yl, z = row // 4, row % 4
    f32 = jnp.float32

    def q_dev(xx, yy, cc):
        return {"row": row, "col": xx * 4 + yy * 2 + cc}

    def k_dev(yy, zz):
        return {"row": yy * 4 + zz, "col": col}

    sibling = q_dev(x, yh, 1 - core)
    pair_y = q_dev(x, 1 - yh, core)
    pair_r = k_dev(1 - yl, z)
    sides_q = (q_dev((x + 1) % 4, yh, core), q_dev((x + 3) % 4, yh, core))
    sides_k = (k_dev(yl, (z + 1) % 4), k_dev(yl, (z + 3) % 4))
    enter([sibling, pair_y, pair_r, *sides_q, *sides_k])
    sends = Sends(send)

    def landed(ref, sem):
        remote(ref, ref, send.at[0], sem, sibling).wait_recv()
        return ref[...].astype(f32)

    class Ring:
        def __init__(self, block, me, sides, hop, acc, fin, which):
            self.block, self.me, self.sides = block, me, sides
            self.hop, self.acc, self.fin, self.which = hop, acc, fin, which

        def at(self, step, half):
            return self.block((self.me + step) % 4, half)

        def far(self):
            for half in range(2):
                sends.start(
                    self.at(2, half), self.hop.at[half], recv.at[self.which, half], self.sides[half]
                )

        def near(self):
            for side, step in ((0, 1), (1, 3)):
                sends.start(
                    self.at(step, 1 - side),
                    self.fin.at[side],
                    recv.at[self.which, 2 + side],
                    self.sides[side],
                )

        def turn(self):
            for side, step in ((0, 1), (1, 3)):
                came = landed(self.hop.at[side], recv.at[self.which, side])
                self.acc[side] = (came + self.at(step, side)[...].astype(f32)).astype(jnp.bfloat16)
                sends.start(
                    self.acc.at[side],
                    self.fin.at[2 + side],
                    recv.at[self.which, 4 + side],
                    self.sides[side],
                )

        def arrive(self):
            for slot in range(4):
                landed(self.fin.at[slot], recv.at[self.which, 2 + slot])

        def total(self, half):
            return (
                self.at(0, half)[...].astype(f32)
                + self.fin[1 - half].astype(f32)
                + self.fin[2 + half].astype(f32)
            )

    ring_q = Ring(lambda xx, half: pair_sum.at[xx, half], x, sides_q, hop_q, acc_q, fin_q, 1)
    ring_k = Ring(lambda zz, half: kp.at[half, zz], z, sides_k, hop_k, acc_k, fin_k, 2)
    order_x = [(x + d) % 4 for d in (2, 1, 3, 0)]
    for xx in order_x:
        sends.start(qp.at[xx, :, 1 - core], pair_in.at[xx], recv.at[0, xx], sibling)
    ring_k.far()
    ring_k.near()
    for n, xx in enumerate(order_x):
        came = landed(pair_in.at[xx], recv.at[0, xx])
        pair_sum[xx] = (qp[xx, :, core].astype(f32) + came).astype(jnp.bfloat16)
        if n == 0:
            ring_q.far()
        elif n == 2:
            ring_q.near()
    ring_k.turn()
    ring_q.turn()

    def across(ring, pos, stage, last, out, peer, slot):
        ring.arrive()
        for half in range(2):

            @pl.when(pos != half)
            def _():
                stage[...] = ring.total(half).astype(jnp.bfloat16)

            @pl.when(pos == half)
            def _():
                out[...] = ring.total(half)

        sends.start(stage, last, recv.at[3, slot], peer)

    across(ring_k, yl, out_k, last_k, ko, pair_r, 0)
    across(ring_q, yh, out_q, last_q, qo, pair_y, 1)
    ko[...] += landed(last_k, recv.at[3, 0])
    qo[...] += landed(last_q, recv.at[3, 1])
    sends.drain()


def reduce(qp, kp):
    bf = jnp.bfloat16
    block = (128, 512)
    return pl.pallas_call(
        reduce_kernel,
        in_specs=[VM] * 2,
        out_specs=[VM] * 2,
        out_shape=[jax.ShapeDtypeStruct(block, jnp.float32)] * 2,
        scratch_shapes=[
            pltpu.VMEM((4, 2, *block), bf),
            pltpu.VMEM((4, 2, *block), bf),
            pltpu.VMEM((2, *block), bf),
            pltpu.VMEM((2, *block), bf),
            pltpu.VMEM((4, *block), bf),
            pltpu.VMEM((2, *block), bf),
            pltpu.VMEM((2, *block), bf),
            pltpu.VMEM((4, *block), bf),
            pltpu.VMEM(block, bf),
            pltpu.VMEM(block, bf),
            pltpu.VMEM(block, bf),
            pltpu.VMEM(block, bf),
            pltpu.SemaphoreType.DMA((20,)),
            pltpu.SemaphoreType.DMA((4, 6)),
        ],
        compiler_params=pltpu.CompilerParams(
            collective_id=2, has_side_effects=True, vmem_limit_bytes=16 << 20
        ),
        name="reduce",
    )(qp, kp)


def mask_keys(ks, km):
    half = lax.broadcasted_iota(jnp.int32, (128, 128), 1) < HEAD
    for block in range(8):
        rows = slice(block * 128, (block + 1) * 128)
        for h in range(HEADS):
            kk = ks[rows, (h // 2) * 128 : (h // 2 + 1) * 128]
            keep = half if h % 2 == 0 else jnp.logical_not(half)
            km[h, rows, :] = jnp.where(keep, kk, jnp.zeros_like(kk))


def order_of(meta, which, g):
    return meta[which * NU + g]


def place_of(meta, which, g):
    return meta[NU + NV + which * NU + g]


def rows_of(g):
    return pl.ds(pl.multiple_of(g * GRAIN, GRAIN), GRAIN)


def chunk_bounds(meta, i):
    low = place_of(meta, 0, i * (UB // GRAIN))
    high = place_of(meta, 0, (i + 1) * (UB // GRAIN) - 1)
    per = VC // GRAIN
    first = jnp.int32(0)
    full = jnp.int32(0)
    for j in range(NV // per):
        first += (place_of(meta, 1, (j + 1) * per - 1) < low).astype(jnp.int32)
        full += (place_of(meta, 1, j * per) <= high).astype(jnp.int32)
    return first, full


def chunk_valid(meta, pu, j, width):
    off = lax.broadcasted_iota(jnp.int32, (GRAIN, UB), 0)
    per = VC // GRAIN
    pv = jnp.concatenate(
        [off + GRAIN * place_of(meta, 1, j * per + t) for t in range(width * per)], axis=0
    )
    return pv >= pu


def stats_kernel(
    q_ref, k_ref, f_ref, b_ref, meta, pu_ref, out, qs, ks, ws, ms, cs, fs, bs, km, ft, bt, run_m, run_t, run_e, held, sem
):
    def flush(n):
        slot = n % SLOTS
        return pltpu.make_async_copy(held.at[slot], ws.at[n], sem.at[slot])

    for block in range(16):
        ft[block * 128 : (block + 1) * 128, :] = f_ref[block].T
    for block in range(8):
        bt[block * 128 : (block + 1) * 128, :] = b_ref[block].T

    def sort_sources(g, _):
        frm = rows_of(order_of(meta, 0, g))
        qs[rows_of(g), :] = q_ref[frm, :] * jnp.bfloat16(SCALE)
        fs[rows_of(g), :] = ft[frm, :]
        return 0

    def sort_targets(g, _):
        frm = rows_of(order_of(meta, 1, g))
        ks[rows_of(g), :] = k_ref[frm, :]
        bs[rows_of(g), :] = bt[frm, :]
        return 0

    lax.fori_loop(0, NU, sort_sources, 0)
    lax.fori_loop(0, NV, sort_targets, 0)
    mask_keys(ks, km)

    def sources(i, tile):
        us = pl.ds(pl.multiple_of(i * UB, UB), UB)
        first, full = chunk_bounds(meta, i)
        odd = first % 2
        mixed = jnp.maximum(full - first - odd + 1, 0) // 2
        pairs = (1024 // VC - first) // 2
        run_m[...] = jnp.full_like(run_m, TOP)
        run_t[...] = jnp.zeros_like(run_t)
        run_e[...] = jnp.zeros_like(run_e)

        def targets(j, width, masked):
            rows = width * VC
            vs = pl.ds(pl.multiple_of(j * VC, VC), rows)
            n = tile + j - first
            for t in range(width):

                @pl.when(n + t >= SLOTS)
                def _():
                    flush(n + t - SLOTS).wait()

            counts = nt(bs[vs, :], fs[us, :])
            if masked:
                valid = chunk_valid(meta, pu_ref[pl.ds(i, 1), :], j, width)
            for h in range(HEADS):
                scores = nt(km[h, vs, :], qs[us, (h // 2) * 128 : (h // 2 + 1) * 128])
                if masked:
                    scores = jnp.where(valid, scores, NEG)
                for t in range(rows // SUB):
                    part = slice(t * SUB, (t + 1) * SUB)
                    s = scores[part].reshape(SUB // 8, 8, UB)
                    old = run_m[h]
                    new = jnp.maximum(old, jnp.max(s, axis=0))
                    w = jnp.exp(s - new[None])
                    shrink = jnp.exp(old - new)
                    run_m[h] = new
                    run_t[h] = run_t[h] * shrink + jnp.sum(w, axis=0)
                    run_e[h] = run_e[h] * shrink + jnp.sum(
                        w * counts[part].reshape(SUB // 8, 8, UB), axis=0
                    )
                    at = t * SUB // VC
                    inner = t % (VC // SUB)
                    held[(n + at) % SLOTS, h, inner * SUB : (inner + 1) * SUB, :] = w.reshape(
                        SUB, UB
                    ).astype(jnp.bfloat16)
                    ms[n + at, h, inner] = new
            for t in range(width):
                cs[n + t] = counts[t * VC : (t + 1) * VC]
                flush(n + t).start()

        def single(j, _):
            targets(first, 1, True)
            return 0

        def mixed_pair(j, _):
            targets(first + odd + 2 * j, 2, True)
            return 0

        def open_pair(j, _):
            targets(first + odd + 2 * j, 2, False)
            return 0

        lax.fori_loop(0, odd, single, 0)
        lax.fori_loop(0, mixed, mixed_pair, 0)
        lax.fori_loop(mixed, pairs, open_pair, 0)
        for h in range(HEADS):
            part_m = run_m[h]
            top = jnp.max(part_m, axis=0, keepdims=True)
            weight = jnp.exp(part_m - top)
            total = jnp.sum(run_t[h] * weight, axis=0, keepdims=True)
            expect = jnp.sum(run_e[h] * weight, axis=0, keepdims=True)
            some = total > 0.0
            safe = jnp.where(some, total, 1.0)
            log = jnp.where(some, top + jnp.log(safe), NEG)
            mean = expect / safe
            for t in range(UB // 128):
                at = i * (UB // 128) + t
                out[at, h : h + 1, :] = log[:, t * 128 : (t + 1) * 128]
                out[at, HEADS + h : HEADS + h + 1, :] = mean[:, t * 128 : (t + 1) * 128]
        return tile + 1024 // VC - first

    count = lax.fori_loop(0, 2048 // UB, sources, jnp.int32(0))
    for back in range(1, SLOTS + 1):

        @pl.when(count >= back)
        def _():
            flush(count - back).wait()


def stats(q, k, f, b, meta, pu):
    bf = jnp.bfloat16
    return pl.pallas_call(
        stats_kernel,
        in_specs=[VM] * 4 + [SM, VM],
        out_specs=[VM] * 3 + [pl.BlockSpec(memory_space=pl.ANY), VM, VM],
        out_shape=[
            jax.ShapeDtypeStruct((16, 16, 128), jnp.float32),
            jax.ShapeDtypeStruct((2048, 512), bf),
            jax.ShapeDtypeStruct((1024, 512), bf),
            jax.ShapeDtypeStruct((TILES, HEADS, VC, UB), bf),
            jax.ShapeDtypeStruct((TILES, HEADS, VC // SUB, 8, UB), jnp.float32),
            jax.ShapeDtypeStruct((TILES, VC, UB), jnp.float32),
        ],
        scratch_shapes=[
            pltpu.VMEM((2048, 256), bf),
            pltpu.VMEM((1024, 256), bf),
            pltpu.VMEM((HEADS, 1024, 128), bf),
            pltpu.VMEM((2048, 256), bf),
            pltpu.VMEM((1024, 256), bf),
            pltpu.VMEM((HEADS, 8, UB), jnp.float32),
            pltpu.VMEM((HEADS, 8, UB), jnp.float32),
            pltpu.VMEM((HEADS, 8, UB), jnp.float32),
            pltpu.VMEM((SLOTS, HEADS, VC, UB), bf),
            pltpu.SemaphoreType.DMA((SLOTS,)),
        ],
        compiler_params=pltpu.CompilerParams(vmem_limit_bytes=12 << 20),
        name="stats",
    )(q, k, f, b, meta, pu)


def grads_kernel(qs, ks, ws, ms, cs, meta, st, qg, kg, kt, qacc, kacc, held, sem):
    def fetch(n):
        slot = n % SLOTS
        return pltpu.make_async_copy(ws.at[n], held.at[slot], sem.at[slot])

    count = jnp.int32(0)
    for i in range(2048 // UB):
        count += 1024 // VC - chunk_bounds(meta, i)[0]
    for n in range(SLOTS):

        @pl.when(count > n)
        def _():
            fetch(n).start()

    for block in range(8):
        rows = slice(block * 128, (block + 1) * 128)
        kt[:, rows] = ks[rows, :].T
    kacc[...] = jnp.zeros_like(kacc)

    def sources(i, tile):
        us = pl.ds(pl.multiple_of(i * UB, UB), UB)
        first, _ = chunk_bounds(meta, i)
        both = jnp.concatenate([st[i * (UB // 128) + t] for t in range(UB // 128)], axis=1)
        qacc[...] = jnp.zeros_like(qacc)

        def targets(j, width):
            rows = width * VC
            vs = pl.ds(pl.multiple_of(j * VC, VC), rows)
            n = tile + j - first
            for t in range(width):
                fetch(n + t).wait()
            low = lax.broadcasted_iota(jnp.int32, (rows, 128), 1) < HEAD
            pair = []
            for h in range(HEADS):
                log = both[h : h + 1]
                mean = both[HEADS + h : HEADS + h + 1]
                parts = []
                for t in range(rows // SUB):
                    at = t * SUB // VC
                    inner = t % (VC // SUB)
                    w = held[(n + at) % SLOTS, h, inner * SUB : (inner + 1) * SUB, :].astype(
                        jnp.float32
                    )
                    scale = jnp.exp(ms[n + at, h, inner] - log)
                    w = (w.reshape(SUB // 8, 8, UB) * scale[None]).reshape(SUB, UB)
                    counts = cs[n + at, inner * SUB : (inner + 1) * SUB, :]
                    parts.append((w * (mean - counts)).astype(jnp.bfloat16))
                g = jnp.concatenate(parts, axis=0)
                hs = slice(h * HEAD, (h + 1) * HEAD)
                qacc[hs, :] += nn(kt[hs, vs], g)
                pair.append(nn(g, qs[us, (h // 2) * 128 : (h // 2 + 1) * 128]))
                if h % 2:
                    cols = slice((h // 2) * 128, (h // 2 + 1) * 128)
                    kacc[vs, cols] += jnp.where(low, pair[-2], pair[-1])
            for t in range(width):

                @pl.when(n + t + SLOTS < count)
                def _():
                    fetch(n + t + SLOTS).start()

        odd = first % 2

        def single(j, _):
            targets(first, 1)
            return 0

        def double(j, _):
            targets(first + odd + 2 * j, 2)
            return 0

        lax.fori_loop(0, odd, single, 0)
        lax.fori_loop(0, (1024 // VC - first) // 2, double, 0)
        turned = (qacc[...] * SCALE).T.astype(jnp.bfloat16)
        for t in range(UB // GRAIN):
            to = order_of(meta, 0, i * (UB // GRAIN) + t)
            qg[rows_of(to), :] = turned[t * GRAIN : (t + 1) * GRAIN]
        return tile + 1024 // VC - first

    lax.fori_loop(0, 2048 // UB, sources, jnp.int32(0))

    def unsort(g, _):
        kg[rows_of(order_of(meta, 1, g)), :] = kacc[rows_of(g), :].astype(jnp.bfloat16)
        return 0

    lax.fori_loop(0, NV, unsort, 0)


def grads(qs, ks, ws, ms, cs, meta, st):
    bf = jnp.bfloat16
    return pl.pallas_call(
        grads_kernel,
        in_specs=[VM] * 2 + [pl.BlockSpec(memory_space=pl.ANY), VM, VM, SM, VM],
        out_specs=[VM] * 2,
        out_shape=[
            jax.ShapeDtypeStruct((2048, 512), bf),
            jax.ShapeDtypeStruct((1024, 512), bf),
        ],
        scratch_shapes=[
            pltpu.VMEM((512, 1024), bf),
            pltpu.VMEM((512, UB), jnp.float32),
            pltpu.VMEM((1024, 512), jnp.float32),
            pltpu.VMEM((SLOTS, HEADS, VC, UB), bf),
            pltpu.SemaphoreType.DMA((SLOTS,)),
        ],
        compiler_params=pltpu.CompilerParams(vmem_limit_bytes=12 << 20),
        name="grads",
    )(qs, ks, ws, ms, cs, meta, st)


def in_order(places, member, index, count):
    rank = jnp.sum(
        (member[None, :] & (places[None, :] < places[:, None])).astype(jnp.int32), axis=1
    )
    hit = member[None, :] & (rank[None, :] == jnp.arange(count, dtype=jnp.int32)[:, None])
    return (
        jnp.sum(jnp.where(hit, index[None, :], 0), axis=1),
        jnp.sum(jnp.where(hit, places[None, :], 0), axis=1),
    )


def local(queries, keys, fwd_table, bwd_table, step_weight, block_order):
    row_id = lax.axis_index("row")
    col_id = lax.axis_index("col")
    grain = jnp.arange(512, dtype=jnp.int32)
    order_u, place_u = in_order(block_order, grain // NU == row_id, grain % NU, NU)
    order_v, place_v = in_order(
        block_order, (grain % NU) // 4 == col_id, grain // NU * 4 + grain % 4, NV
    )
    meta = jnp.concatenate([order_u, order_v, place_u, place_v])
    offsets = jnp.arange(GRAIN, dtype=jnp.int32)
    pu = (place_u[:, None] * GRAIN + offsets[None, :]).reshape(8, 256)
    here = [
        pltpu.with_memory_space_constraint(a, pltpu.MemorySpace.HBM)
        for a in (queries, keys, fwd_table, bwd_table, step_weight)
    ]
    q, k, f, b = gather(*here)
    part, qs, ks, ws, ms, cs = stats(
        q.reshape(2048, 512),
        k.reshape(1024, 512),
        f.reshape(16, 256, 128),
        b.reshape(8, 256, 128),
        meta,
        pu,
    )
    qg, kg = grads(qs, ks, ws, ms, cs, meta, merge(part))
    return reduce(qg.reshape(4, 2, 2, 128, 512), kg.reshape(2, 4, 128, 512))


def solution(mesh):
    return jax.shard_map(
        local,
        mesh=mesh,
        in_specs=(
            P(("row", "col"), None),
            P(("row", "col"), None),
            P(("row", "col"), None),
            P(("row", "col"), None),
            P(("row", "col")),
            P(),
        ),
        out_specs=(P(("row", "col"), None), P(("row", "col"), None)),
        check_vma=False,
    )
```

```python
import jax
import jax.numpy as jnp
from jax import lax
from jax.experimental import pallas as pl
from jax.experimental.pallas import tpu as pltpu
from jax.sharding import PartitionSpec as P

HEADS = 8
HEAD = 64
GRAIN = 32
SCALE = HEAD**-0.5
LOG_HEADS = 2.0794415416798357
NEG = -1e30
TOP = -1e29
NU = 64
NV = 32
TILES = 64
SLOTS = 4
UB = 256
VC = 128
SUB = 128
MESH = pl.DeviceIdType.MESH
VM = pl.BlockSpec(memory_space=pltpu.VMEM)
SM = pl.BlockSpec(memory_space=pltpu.SMEM)
HB = pl.BlockSpec(memory_space=pltpu.MemorySpace.HBM)


def nn(a, b):
    return lax.dot_general(a, b, (((1,), (0,)), ((), ())), preferred_element_type=jnp.float32)


def nt(a, b):
    return lax.dot_general(a, b, (((1,), (1,)), ((), ())), preferred_element_type=jnp.float32)


def remote(src, dst, send, recv, peer):
    return pltpu.make_async_remote_copy(
        src_ref=src, dst_ref=dst, send_sem=send, recv_sem=recv, device_id=peer, device_id_type=MESH
    )


def greet(peers):
    barrier = pltpu.get_barrier_semaphore()
    for peer in peers:
        pl.semaphore_signal(barrier, inc=1, device_id=peer, device_id_type=MESH)


def enter(peers):
    greet(peers)
    pl.semaphore_wait(pltpu.get_barrier_semaphore(), len(peers))


class Sends:
    def __init__(self, sems):
        self.sems = sems
        self.started = []

    def start(self, src, dst, recv, peer):
        copy = remote(src, dst, self.sems.at[len(self.started)], recv, peer)
        copy.start()
        self.started.append(copy)

    def drain(self):
        for copy in self.started:
            copy.wait_send()


def gather_kernel(
    q, k, fwd, bwd, weight, qa, ka, fa, ba, fv, bv, sf, sb, send, recv_q, recv_f, recv_k, recv_b, in_f, in_b, own
):
    row, col = lax.axis_index("row"), lax.axis_index("col")
    x, yh, core = col // 4, (col // 2) % 2, col % 2
    yl, z = row // 4, row % 4

    def at(r=None, c=None):
        return {"row": row if r is None else r, "col": col if c is None else c}

    def cslot(xx, yy, cc):
        return xx * 4 + yy * 2 + cc

    peers = [at(r=(row + d) % 8) for d in range(1, 8)] + [at(c=(col + d) % 16) for d in range(1, 16)]
    greet(peers)
    tables = [pltpu.make_async_copy(fwd, fv, own.at[0]), pltpu.make_async_copy(bwd, bv, own.at[1])]
    local = [
        pltpu.make_async_copy(q, qa.at[col], own.at[2]),
        pltpu.make_async_copy(k, ka.at[row], own.at[3]),
    ]
    for copy in tables + local:
        copy.start()
    step = jnp.where(lax.broadcasted_iota(jnp.int32, (2, 128), 0) == 0, weight[0], weight[1])
    tables[0].wait()
    tables[1].wait()
    for r in range(8):
        for c in range(16):
            cut = slice((r * 16 + c) * 128, (r * 16 + c + 1) * 128)
            sf[r, c] = fv[:, cut]
            sb[r, c] = (bv[:, cut].astype(jnp.float32) * step).astype(jnp.bfloat16)
    pl.semaphore_wait(pltpu.get_barrier_semaphore(), len(peers))
    sends = Sends(send)
    local += [
        pltpu.make_async_copy(sf.at[row], fa.at[:, col, row], own.at[4]),
        pltpu.make_async_copy(sb.at[:, col], ba.at[:, col, row], own.at[5]),
    ]
    local[2].start()
    local[3].start()
    for d in range(1, 16):
        to = (col + d) % 16
        sends.start(sb.at[:, to], ba.at[:, col, row], in_b.at[col], at(c=to))
    for d in range(1, 8):
        to = (row + d) % 8
        sends.start(sf.at[to], fa.at[:, col, row], in_f.at[row], at(r=to))

    def q_part(slot, half=None):
        return qa.at[slot] if half is None else qa.at[slot, pl.ds(half * 64, 64)]

    def f_part(slot, half=None):
        return fa.at[:, slot] if half is None else fa.at[pl.ds(half * 8, 8), slot]

    def k_part(slot, half=None):
        return ka.at[slot] if half is None else ka.at[slot, pl.ds(half * 64, 64)]

    def b_part(slot, half=None):
        return ba.at[:, :, slot] if half is None else ba.at[pl.ds(half * 4, 4), :, slot]

    def src_slot(dx, dy, cc=None):
        return cslot((x + dx) % 4, (yh + dy) % 2, core if cc is None else cc)

    def tgt_slot(dz, dy):
        return ((yl + dy) % 2) * 4 + (z + dz) % 4

    def src_dev(dx, dy, dc=0):
        return at(c=cslot((x + dx) % 4, (yh + dy) % 2, (core + dc) % 2))

    def tgt_dev(dz, dy):
        return at(r=tgt_slot(dz, dy))

    source = (src_slot, src_dev, True)
    target = (tgt_slot, tgt_dev, False)
    streams = {
        "q": (q_part, recv_q, source),
        "f": (f_part, recv_f, source),
        "k": (k_part, recv_k, target),
        "b": (b_part, recv_b, target),
    }

    def push(kind, slot, peer, half=None):
        part, recv, _ = streams[kind]
        ref = part(slot, half)
        sends.start(ref, ref, recv.at[slot, 0 if half is None else half], peer)

    def arrived(kind, slot, half=None):
        part, recv, _ = streams[kind]
        ref = part(slot, half)
        remote(ref, ref, send.at[0], recv.at[slot, 0 if half is None else half], at()).wait_recv()

    def first(kind):
        slot_of, dev_of, pair = streams[kind][2]
        mine = slot_of(0, 0)
        push(kind, mine, dev_of(0, 1))
        push(kind, mine, dev_of(1, 0))
        push(kind, mine, dev_of(3, 0))
        if pair:
            push(kind, mine, dev_of(0, 0, 1))

    def second(kind):
        slot_of, dev_of, pair = streams[kind][2]
        other = slot_of(0, 1)
        arrived(kind, other)
        push(kind, other, dev_of(1, 0))
        push(kind, other, dev_of(3, 0))
        if pair:
            push(kind, other, dev_of(0, 0, 1))

    def relay(kind, dy):
        slot_of, dev_of, pair = streams[kind][2]
        for step, half in ((3, 0), (1, 1)):
            slot = slot_of(step, dy)
            arrived(kind, slot)
            push(kind, slot, dev_of(4 - step, 0), half)
            if pair:
                push(kind, slot, dev_of(0, 0, 1))

    def last(kind, dy):
        slot_of, dev_of, pair = streams[kind][2]
        slot = slot_of(2, dy)
        arrived(kind, slot, 0)
        arrived(kind, slot, 1)
        if pair:
            push(kind, slot, dev_of(0, 0, 1))

    local[0].wait()
    local[1].wait()
    first("q")
    first("k")
    local[2].wait()
    for d in range(1, 8):
        frm = (row + d) % 8
        ref = fa.at[:, col, frm]
        remote(ref, ref, send.at[0], in_f.at[frm], at()).wait_recv()
    first("f")
    local[3].wait()
    for d in range(1, 16):
        frm = (col + d) % 16
        ref = ba.at[:, frm, row]
        remote(ref, ref, send.at[0], in_b.at[frm], at()).wait_recv()
    first("b")
    relay("k", 0)
    relay("q", 0)
    second("k")
    second("q")
    relay("b", 0)
    relay("f", 0)
    second("b")
    second("f")
    relay("k", 1)
    relay("q", 1)
    relay("b", 1)
    relay("f", 1)
    for dy in range(2):
        for kind in ("k", "q", "b", "f"):
            last(kind, dy)
    for kind in ("q", "f"):
        for dx in range(4):
            for dy in range(2):
                arrived(kind, src_slot(dx, dy, 1 - core))
    sends.drain()


def gather(q, k, fwd, bwd, weight):
    bf = jnp.bfloat16
    return pl.pallas_call(
        gather_kernel,
        in_specs=[HB] * 4 + [SM],
        out_specs=[VM] * 4,
        out_shape=[
            jax.ShapeDtypeStruct((16, 128, 512), bf),
            jax.ShapeDtypeStruct((8, 128, 512), bf),
            jax.ShapeDtypeStruct((16, 16, 8, 2, 128), bf),
            jax.ShapeDtypeStruct((8, 16, 8, 2, 128), bf),
        ],
        scratch_shapes=[
            pltpu.VMEM((2, 16384), bf),
            pltpu.VMEM((2, 16384), bf),
            pltpu.VMEM((8, 16, 2, 128), bf),
            pltpu.VMEM((8, 16, 2, 128), bf),
            pltpu.SemaphoreType.DMA((100,)),
            pltpu.SemaphoreType.DMA((16, 2)),
            pltpu.SemaphoreType.DMA((16, 2)),
            pltpu.SemaphoreType.DMA((8, 2)),
            pltpu.SemaphoreType.DMA((8, 2)),
            pltpu.SemaphoreType.DMA((8,)),
            pltpu.SemaphoreType.DMA((16,)),
            pltpu.SemaphoreType.DMA((6,)),
        ],
        compiler_params=pltpu.CompilerParams(
            collective_id=0, has_side_effects=True, vmem_limit_bytes=16 << 20
        ),
        name="gather",
    )(q, k, fwd, bwd, weight)


def merge_kernel(part, ks, out, kt, landed, mine, send, recv, recv2, own):
    row, col = lax.axis_index("row"), lax.axis_index("col")
    peers = [{"row": row, "col": (col + d) % 16} for d in range(1, 16)]
    enter(peers)
    sends = Sends(send)
    keep = pltpu.make_async_copy(part.at[col], landed.at[col], own.at[0])
    keep.start()
    for d, peer in enumerate(peers):
        sends.start(part.at[peer["col"]], landed.at[col], recv.at[col], peer)
    for block in range(8):
        rows = slice(block * 128, (block + 1) * 128)
        kt[:, rows] = ks[rows, :].T
    keep.wait()
    for peer in peers:
        ref = landed.at[peer["col"]]
        remote(ref, ref, send.at[0], recv.at[peer["col"]], peer).wait_recv()
    logs = landed[:, 0:8]
    top = jnp.max(logs, axis=0)
    weight = jnp.exp(logs - top[None])
    total = jnp.sum(weight, axis=0)
    mean = jnp.sum(weight * landed[:, 8:16], axis=0) / total
    mine[0:8, :] = top + jnp.log(total) + LOG_HEADS
    mine[8:16, :] = mean
    keep = pltpu.make_async_copy(mine, out.at[col], own.at[1])
    keep.start()
    for peer in peers:
        sends.start(mine, out.at[col], recv2.at[col], peer)
    keep.wait()
    for peer in peers:
        ref = out.at[peer["col"]]
        remote(ref, ref, send.at[0], recv2.at[peer["col"]], peer).wait_recv()
    sends.drain()


def merge(part, ks):
    return pl.pallas_call(
        merge_kernel,
        in_specs=[VM] * 2,
        out_specs=[VM] * 2,
        out_shape=[
            jax.ShapeDtypeStruct((16, 16, 128), jnp.float32),
            jax.ShapeDtypeStruct((512, 1024), jnp.bfloat16),
        ],
        scratch_shapes=[
            pltpu.VMEM((16, 16, 128), jnp.float32),
            pltpu.VMEM((16, 128), jnp.float32),
            pltpu.SemaphoreType.DMA((30,)),
            pltpu.SemaphoreType.DMA((16,)),
            pltpu.SemaphoreType.DMA((16,)),
            pltpu.SemaphoreType.DMA((2,)),
        ],
        compiler_params=pltpu.CompilerParams(
            collective_id=1, has_side_effects=True, vmem_limit_bytes=4 << 20
        ),
        name="merge",
    )(part, ks)


def reduce_kernel(
    qp, kp, qo, ko, last_q, last_k, pair_in, pair_sum, hop_q, acc_q, fin_q, hop_k, acc_k, fin_k, out_q, out_k, send, recv
):
    row, col = lax.axis_index("row"), lax.axis_index("col")
    x, yh, core = col // 4, (col // 2) % 2, col % 2
    yl, z = row // 4, row % 4
    f32 = jnp.float32

    def q_dev(xx, yy, cc):
        return {"row": row, "col": xx * 4 + yy * 2 + cc}

    def k_dev(yy, zz):
        return {"row": yy * 4 + zz, "col": col}

    sibling = q_dev(x, yh, 1 - core)
    pair_y = q_dev(x, 1 - yh, core)
    pair_r = k_dev(1 - yl, z)
    sides_q = (q_dev((x + 1) % 4, yh, core), q_dev((x + 3) % 4, yh, core))
    sides_k = (k_dev(yl, (z + 1) % 4), k_dev(yl, (z + 3) % 4))
    enter([sibling, pair_y, pair_r, *sides_q, *sides_k])
    sends = Sends(send)
    parts = [pl.ds(n * 64, 64) for n in range(2)]

    def landed(ref, sem):
        remote(ref, ref, send.at[0], sem, sibling).wait_recv()
        return ref

    class Ring:
        def __init__(self, block, me, sides, hop, acc, fin, which):
            self.block, self.me, self.sides = block, me, sides
            self.hop, self.acc, self.fin, self.which = hop, acc, fin, which

        def at(self, step, half):
            return self.block((self.me + step) % 4, half)

        def far(self):
            for half in range(2):
                sends.start(
                    self.at(2, half), self.hop.at[half], recv.at[self.which, half], self.sides[half]
                )

        def near(self):
            for side, step in ((0, 1), (1, 3)):
                sends.start(
                    self.at(step, 1 - side),
                    self.fin.at[side],
                    recv.at[self.which, 2 + side],
                    self.sides[side],
                )

        def turn(self):
            for side, step in ((0, 1), (1, 3)):
                came = landed(self.hop.at[side], recv.at[self.which, side])[...].astype(f32)
                self.acc[side] = (came + self.at(step, side)[...].astype(f32)).astype(jnp.bfloat16)
                for n, rows in enumerate(parts):
                    sends.start(
                        self.acc.at[side, rows],
                        self.fin.at[2 + side, rows],
                        recv.at[self.which, 4 + 2 * side + n],
                        self.sides[side],
                    )

        def near_arrive(self):
            for slot in range(2):
                landed(self.fin.at[slot], recv.at[self.which, 2 + slot])

        def arrive(self, n):
            for side in range(2):
                landed(self.fin.at[2 + side, parts[n]], recv.at[self.which, 4 + 2 * side + n])

        def total(self, half, rows):
            return (
                self.at(0, half)[rows, :].astype(f32)
                + self.fin[1 - half, rows, :].astype(f32)
                + self.fin[2 + half, rows, :].astype(f32)
            )

    ring_q = Ring(lambda xx, half: pair_sum.at[xx, half], x, sides_q, hop_q, acc_q, fin_q, 1)
    ring_k = Ring(lambda zz, half: kp.at[half, zz], z, sides_k, hop_k, acc_k, fin_k, 2)
    order_x = [(x + d) % 4 for d in (2, 1, 3, 0)]
    for xx in order_x:
        sends.start(qp.at[xx, :, 1 - core], pair_in.at[xx], recv.at[0, xx], sibling)
    ring_k.far()
    ring_k.near()
    for n, xx in enumerate(order_x):
        came = landed(pair_in.at[xx], recv.at[0, xx])[...].astype(f32)
        pair_sum[xx] = (qp[xx, :, core].astype(f32) + came).astype(jnp.bfloat16)
        if n == 0:
            ring_q.far()
        elif n == 2:
            ring_q.near()
    ring_k.turn()
    ring_q.turn()

    def across(ring, pos, stage, last, out, peer, slot, n):
        rows = parts[n]
        ring.arrive(n)
        for half in range(2):

            @pl.when(pos != half)
            def _():
                stage[rows, :] = ring.total(half, rows).astype(jnp.bfloat16)

            @pl.when(pos == half)
            def _():
                out[rows, :] = ring.total(half, rows)

        sends.start(stage.at[rows], last.at[rows], recv.at[3, 2 * slot + n], peer)

    ring_k.near_arrive()
    ring_q.near_arrive()
    for n in range(2):
        across(ring_k, yl, out_k, last_k, ko, pair_r, 0, n)
        across(ring_q, yh, out_q, last_q, qo, pair_y, 1, n)
    for n in range(2):
        landed(last_k.at[parts[n]], recv.at[3, n])
        landed(last_q.at[parts[n]], recv.at[3, 2 + n])
    sends.drain()


def reduce(qp, kp):
    bf = jnp.bfloat16
    block = (128, 512)
    return pl.pallas_call(
        reduce_kernel,
        in_specs=[VM] * 2,
        out_specs=[VM] * 4,
        out_shape=[jax.ShapeDtypeStruct(block, jnp.float32)] * 2
        + [jax.ShapeDtypeStruct(block, bf)] * 2,
        scratch_shapes=[
            pltpu.VMEM((4, 2, *block), bf),
            pltpu.VMEM((4, 2, *block), bf),
            pltpu.VMEM((2, *block), bf),
            pltpu.VMEM((2, *block), bf),
            pltpu.VMEM((4, *block), bf),
            pltpu.VMEM((2, *block), bf),
            pltpu.VMEM((2, *block), bf),
            pltpu.VMEM((4, *block), bf),
            pltpu.VMEM(block, bf),
            pltpu.VMEM(block, bf),
            pltpu.SemaphoreType.DMA((24,)),
            pltpu.SemaphoreType.DMA((4, 8)),
        ],
        compiler_params=pltpu.CompilerParams(
            collective_id=2, has_side_effects=True, vmem_limit_bytes=16 << 20
        ),
        name="reduce",
    )(qp, kp)


def mask_keys(ks, km):
    half = lax.broadcasted_iota(jnp.int32, (128, 128), 1) < HEAD
    for block in range(8):
        rows = slice(block * 128, (block + 1) * 128)
        for h in range(HEADS):
            kk = ks[rows, (h // 2) * 128 : (h // 2 + 1) * 128]
            keep = half if h % 2 == 0 else jnp.logical_not(half)
            km[h, rows, :] = jnp.where(keep, kk, jnp.zeros_like(kk))


def order_of(meta, which, g):
    return meta[which * NU + g]


def place_of(meta, which, g):
    return meta[NU + NV + which * NU + g]


def rows_of(g):
    return pl.ds(pl.multiple_of(g * GRAIN, GRAIN), GRAIN)


def chunk_bounds(meta, i):
    low = place_of(meta, 0, i * (UB // GRAIN))
    high = place_of(meta, 0, (i + 1) * (UB // GRAIN) - 1)
    per = VC // GRAIN
    first = jnp.int32(0)
    full = jnp.int32(0)
    for j in range(NV // per):
        first += (place_of(meta, 1, (j + 1) * per - 1) < low).astype(jnp.int32)
        full += (place_of(meta, 1, j * per) <= high).astype(jnp.int32)
    return first, full


def chunk_valid(meta, pu, j, width):
    off = lax.broadcasted_iota(jnp.int32, (GRAIN, UB), 0)
    per = VC // GRAIN
    pv = jnp.concatenate(
        [off + GRAIN * place_of(meta, 1, j * per + t) for t in range(width * per)], axis=0
    )
    return pv >= pu


def stats_kernel(
    q_ref, k_ref, f_ref, b_ref, meta, pu_ref, out, qs, ks, ws, ms, cs, fs, bs, km, ft, bt, run_m, run_t, run_e, held, sem
):
    def flush(n):
        slot = n % SLOTS
        return pltpu.make_async_copy(held.at[slot], ws.at[n], sem.at[slot])

    for block in range(16):
        ft[block * 128 : (block + 1) * 128, :] = f_ref[block].T
    for block in range(8):
        bt[block * 128 : (block + 1) * 128, :] = b_ref[block].T

    def sort_sources(g, _):
        frm = rows_of(order_of(meta, 0, g))
        qs[rows_of(g), :] = q_ref[frm, :] * jnp.bfloat16(SCALE)
        fs[rows_of(g), :] = ft[frm, :]
        return 0

    def sort_targets(g, _):
        frm = rows_of(order_of(meta, 1, g))
        ks[rows_of(g), :] = k_ref[frm, :]
        bs[rows_of(g), :] = bt[frm, :]
        return 0

    lax.fori_loop(0, NU, sort_sources, 0)
    lax.fori_loop(0, NV, sort_targets, 0)
    mask_keys(ks, km)

    def sources(i, tile):
        us = pl.ds(pl.multiple_of(i * UB, UB), UB)
        first, full = chunk_bounds(meta, i)
        odd = first % 2
        mixed = jnp.maximum(full - first - odd + 1, 0) // 2
        pairs = (1024 // VC - first) // 2
        run_m[...] = jnp.full_like(run_m, TOP)
        run_t[...] = jnp.zeros_like(run_t)
        run_e[...] = jnp.zeros_like(run_e)

        def targets(j, width, masked):
            rows = width * VC
            vs = pl.ds(pl.multiple_of(j * VC, VC), rows)
            n = tile + j - first
            for t in range(width):

                @pl.when(n + t >= SLOTS)
                def _():
                    flush(n + t - SLOTS).wait()

            counts = nt(bs[vs, :], fs[us, :])
            if masked:
                valid = chunk_valid(meta, pu_ref[pl.ds(i, 1), :], j, width)
            for h in range(HEADS):
                scores = nt(km[h, vs, :], qs[us, (h // 2) * 128 : (h // 2 + 1) * 128])
                if masked:
                    scores = jnp.where(valid, scores, NEG)
                for t in range(rows // SUB):
                    part = slice(t * SUB, (t + 1) * SUB)
                    s = scores[part].reshape(SUB // 8, 8, UB)
                    old = run_m[h]
                    new = jnp.maximum(old, jnp.max(s, axis=0))
                    w = jnp.exp(s - new[None])
                    shrink = jnp.exp(old - new)
                    run_m[h] = new
                    run_t[h] = run_t[h] * shrink + jnp.sum(w, axis=0)
                    run_e[h] = run_e[h] * shrink + jnp.sum(
                        w * counts[part].reshape(SUB // 8, 8, UB), axis=0
                    )
                    at = t * SUB // VC
                    inner = t % (VC // SUB)
                    held[(n + at) % SLOTS, h, inner * SUB : (inner + 1) * SUB, :] = w.reshape(
                        SUB, UB
                    ).astype(jnp.bfloat16)
                    ms[n + at, h, inner] = new
            for t in range(width):
                cs[n + t] = counts[t * VC : (t + 1) * VC]
                flush(n + t).start()

        def single(j, _):
            targets(first, 1, True)
            return 0

        def mixed_pair(j, _):
            targets(first + odd + 2 * j, 2, True)
            return 0

        def open_pair(j, _):
            targets(first + odd + 2 * j, 2, False)
            return 0

        lax.fori_loop(0, odd, single, 0)
        lax.fori_loop(0, mixed, mixed_pair, 0)
        lax.fori_loop(mixed, pairs, open_pair, 0)
        for h in range(HEADS):
            part_m = run_m[h]
            top = jnp.max(part_m, axis=0, keepdims=True)
            weight = jnp.exp(part_m - top)
            total = jnp.sum(run_t[h] * weight, axis=0, keepdims=True)
            expect = jnp.sum(run_e[h] * weight, axis=0, keepdims=True)
            some = total > 0.0
            safe = jnp.where(some, total, 1.0)
            log = jnp.where(some, top + jnp.log(safe), NEG)
            mean = expect / safe
            for t in range(UB // 128):
                at = i * (UB // 128) + t
                out[at, h : h + 1, :] = log[:, t * 128 : (t + 1) * 128]
                out[at, HEADS + h : HEADS + h + 1, :] = mean[:, t * 128 : (t + 1) * 128]
        return tile + 1024 // VC - first

    count = lax.fori_loop(0, 2048 // UB, sources, jnp.int32(0))
    for back in range(1, SLOTS + 1):

        @pl.when(count >= back)
        def _():
            flush(count - back).wait()


def stats(q, k, f, b, meta, pu):
    bf = jnp.bfloat16
    return pl.pallas_call(
        stats_kernel,
        in_specs=[VM] * 4 + [SM, VM],
        out_specs=[VM] * 3 + [pl.BlockSpec(memory_space=pl.ANY), VM, VM],
        out_shape=[
            jax.ShapeDtypeStruct((16, 16, 128), jnp.float32),
            jax.ShapeDtypeStruct((2048, 512), bf),
            jax.ShapeDtypeStruct((1024, 512), bf),
            jax.ShapeDtypeStruct((TILES, HEADS, VC, UB), bf),
            jax.ShapeDtypeStruct((TILES, HEADS, VC // SUB, 8, UB), jnp.float32),
            jax.ShapeDtypeStruct((TILES, VC, UB), jnp.float32),
        ],
        scratch_shapes=[
            pltpu.VMEM((2048, 256), bf),
            pltpu.VMEM((1024, 256), bf),
            pltpu.VMEM((HEADS, 1024, 128), bf),
            pltpu.VMEM((2048, 256), bf),
            pltpu.VMEM((1024, 256), bf),
            pltpu.VMEM((HEADS, 8, UB), jnp.float32),
            pltpu.VMEM((HEADS, 8, UB), jnp.float32),
            pltpu.VMEM((HEADS, 8, UB), jnp.float32),
            pltpu.VMEM((SLOTS, HEADS, VC, UB), bf),
            pltpu.SemaphoreType.DMA((SLOTS,)),
        ],
        compiler_params=pltpu.CompilerParams(vmem_limit_bytes=12 << 20),
        name="stats",
    )(q, k, f, b, meta, pu)


def grads_kernel(qs, kt, ws, ms, cs, meta, st, qg, kg, qacc, kacc, held, sem):
    def fetch(n):
        slot = n % SLOTS
        return pltpu.make_async_copy(ws.at[n], held.at[slot], sem.at[slot])

    count = jnp.int32(0)
    for i in range(2048 // UB):
        count += 1024 // VC - chunk_bounds(meta, i)[0]
    for n in range(SLOTS):

        @pl.when(count > n)
        def _():
            fetch(n).start()

    kacc[...] = jnp.zeros_like(kacc)

    def sources(i, tile):
        us = pl.ds(pl.multiple_of(i * UB, UB), UB)
        first, _ = chunk_bounds(meta, i)
        both = jnp.concatenate([st[i * (UB // 128) + t] for t in range(UB // 128)], axis=1)
        qacc[...] = jnp.zeros_like(qacc)

        def targets(j, width):
            rows = width * VC
            vs = pl.ds(pl.multiple_of(j * VC, VC), rows)
            n = tile + j - first
            for t in range(width):
                fetch(n + t).wait()
            low = lax.broadcasted_iota(jnp.int32, (rows, 128), 1) < HEAD
            pair = []
            for h in range(HEADS):
                log = both[h : h + 1]
                mean = both[HEADS + h : HEADS + h + 1]
                parts = []
                for t in range(rows // SUB):
                    at = t * SUB // VC
                    inner = t % (VC // SUB)
                    w = held[(n + at) % SLOTS, h, inner * SUB : (inner + 1) * SUB, :].astype(
                        jnp.float32
                    )
                    scale = jnp.exp(ms[n + at, h, inner] - log)
                    w = (w.reshape(SUB // 8, 8, UB) * scale[None]).reshape(SUB, UB)
                    counts = cs[n + at, inner * SUB : (inner + 1) * SUB, :]
                    parts.append((w * (mean - counts)).astype(jnp.bfloat16))
                g = jnp.concatenate(parts, axis=0)
                hs = slice(h * HEAD, (h + 1) * HEAD)
                qacc[hs, :] += nn(kt[hs, vs], g)
                pair.append(nn(g, qs[us, (h // 2) * 128 : (h // 2 + 1) * 128]))
                if h % 2:
                    cols = slice((h // 2) * 128, (h // 2 + 1) * 128)
                    kacc[vs, cols] += jnp.where(low, pair[-2], pair[-1])
            for t in range(width):

                @pl.when(n + t + SLOTS < count)
                def _():
                    fetch(n + t + SLOTS).start()

        odd = first % 2

        def single(j, _):
            targets(first, 1)
            return 0

        def double(j, _):
            targets(first + odd + 2 * j, 2)
            return 0

        lax.fori_loop(0, odd, single, 0)
        lax.fori_loop(0, (1024 // VC - first) // 2, double, 0)
        turned = (qacc[...] * SCALE).T.astype(jnp.bfloat16)
        for t in range(UB // GRAIN):
            to = order_of(meta, 0, i * (UB // GRAIN) + t)
            qg[rows_of(to), :] = turned[t * GRAIN : (t + 1) * GRAIN]
        return tile + 1024 // VC - first

    lax.fori_loop(0, 2048 // UB, sources, jnp.int32(0))

    def unsort(g, _):
        kg[rows_of(order_of(meta, 1, g)), :] = kacc[rows_of(g), :].astype(jnp.bfloat16)
        return 0

    lax.fori_loop(0, NV, unsort, 0)


def grads(qs, kt, ws, ms, cs, meta, st):
    bf = jnp.bfloat16
    return pl.pallas_call(
        grads_kernel,
        in_specs=[VM] * 2 + [pl.BlockSpec(memory_space=pl.ANY), VM, VM, SM, VM],
        out_specs=[VM] * 2,
        out_shape=[
            jax.ShapeDtypeStruct((2048, 512), bf),
            jax.ShapeDtypeStruct((1024, 512), bf),
        ],
        scratch_shapes=[
            pltpu.VMEM((512, UB), jnp.float32),
            pltpu.VMEM((1024, 512), jnp.float32),
            pltpu.VMEM((SLOTS, HEADS, VC, UB), bf),
            pltpu.SemaphoreType.DMA((SLOTS,)),
        ],
        compiler_params=pltpu.CompilerParams(vmem_limit_bytes=12 << 20),
        name="grads",
    )(qs, kt, ws, ms, cs, meta, st)


def in_order(places, index):
    n = places.shape[0]
    rank = jnp.sum((places[None, :] < places[:, None]).astype(jnp.int32), axis=1)
    hit = rank[None, :] == jnp.arange(n, dtype=jnp.int32)[:, None]
    return (
        jnp.sum(jnp.where(hit, index[None, :], 0), axis=1),
        jnp.sum(jnp.where(hit, places[None, :], 0), axis=1),
    )


def local(queries, keys, fwd_table, bwd_table, step_weight, block_order):
    row_id = lax.axis_index("row")
    col_id = lax.axis_index("col")
    line = lax.dynamic_slice_in_dim(block_order, row_id * NU, NU)
    pairs = block_order.reshape(4, 128)
    column = jnp.concatenate(
        [
            lax.dynamic_slice_in_dim(pairs, NU * odd + 4 * col_id, 4, axis=1).reshape(16)
            for odd in range(2)
        ]
    )
    at = jnp.arange(NV, dtype=jnp.int32)
    order_u, place_u = in_order(line, jnp.arange(NU, dtype=jnp.int32))
    order_v, place_v = in_order(column, at % 16 // 4 * 8 + at // 16 * 4 + at % 4)
    meta = jnp.concatenate([order_u, order_v, place_u, place_v])
    offsets = jnp.arange(GRAIN, dtype=jnp.int32)
    pu = (place_u[:, None] * GRAIN + offsets[None, :]).reshape(8, 256)
    here = [
        pltpu.with_memory_space_constraint(a, pltpu.MemorySpace.HBM)
        for a in (queries, keys, fwd_table, bwd_table, step_weight)
    ]
    q, k, f, b = gather(*here)
    part, qs, ks, ws, ms, cs = stats(
        q.reshape(2048, 512),
        k.reshape(1024, 512),
        f.reshape(16, 256, 128),
        b.reshape(8, 256, 128),
        meta,
        pu,
    )
    st, kt = merge(part, ks)
    qg, kg = grads(qs, kt, ws, ms, cs, meta, st)
    q_own, k_own, q_last, k_last = reduce(qg.reshape(4, 2, 2, 128, 512), kg.reshape(2, 4, 128, 512))
    return q_own + q_last.astype(jnp.float32), k_own + k_last.astype(jnp.float32)


def solution(mesh):
    return jax.shard_map(
        local,
        mesh=mesh,
        in_specs=(
            P(("row", "col"), None),
            P(("row", "col"), None),
            P(("row", "col"), None),
            P(("row", "col"), None),
            P(("row", "col")),
            P(),
        ),
        out_specs=(P(("row", "col"), None), P(("row", "col"), None)),
        check_vma=False,
    )
```

```python
import jax
import jax.numpy as jnp
from jax import lax
from jax.experimental import pallas as pl
from jax.experimental.pallas import tpu as pltpu
from jax.sharding import PartitionSpec as P

HEADS = 8
HEAD = 64
GRAIN = 32
SCALE = HEAD**-0.5
LOG_HEADS = 2.0794415416798357
NEG = -1e30
SAFE = 40.0
TOP = -1e29
NU = 64
NV = 32
TILES = 64
SLOTS = 4
UB = 256
VC = 128
SUB = 128
MESH = pl.DeviceIdType.MESH
VM = pl.BlockSpec(memory_space=pltpu.VMEM)
SM = pl.BlockSpec(memory_space=pltpu.SMEM)
HB = pl.BlockSpec(memory_space=pltpu.MemorySpace.HBM)


def nn(a, b):
    return lax.dot_general(a, b, (((1,), (0,)), ((), ())), preferred_element_type=jnp.float32)


def nt(a, b):
    return lax.dot_general(a, b, (((1,), (1,)), ((), ())), preferred_element_type=jnp.float32)


def remote(src, dst, send, recv, peer):
    return pltpu.make_async_remote_copy(
        src_ref=src, dst_ref=dst, send_sem=send, recv_sem=recv, device_id=peer, device_id_type=MESH
    )


def greet(peers):
    barrier = pltpu.get_barrier_semaphore()
    for peer in peers:
        pl.semaphore_signal(barrier, inc=1, device_id=peer, device_id_type=MESH)


def enter(peers):
    greet(peers)
    pl.semaphore_wait(pltpu.get_barrier_semaphore(), len(peers))


class Sends:
    def __init__(self, sems):
        self.sems = sems
        self.started = []

    def start(self, src, dst, recv, peer):
        copy = remote(src, dst, self.sems.at[len(self.started)], recv, peer)
        copy.start()
        self.started.append(copy)

    def drain(self):
        for copy in self.started:
            copy.wait_send()


def gather_kernel(
    q, k, fwd, bwd, weight, qa, ka, fa, ba, fv, bv, sf, sb, send, recv_q, recv_f, recv_k, recv_b, in_f, in_b, own
):
    row, col = lax.axis_index("row"), lax.axis_index("col")
    x, yh, core = col // 4, (col // 2) % 2, col % 2
    yl, z = row // 4, row % 4

    def at(r=None, c=None):
        return {"row": row if r is None else r, "col": col if c is None else c}

    def cslot(xx, yy, cc):
        return xx * 4 + yy * 2 + cc

    peers = [at(r=(row + d) % 8) for d in range(1, 8)] + [at(c=(col + d) % 16) for d in range(1, 16)]
    greet(peers)
    tables = [pltpu.make_async_copy(fwd, fv, own.at[0]), pltpu.make_async_copy(bwd, bv, own.at[1])]
    local = [
        pltpu.make_async_copy(q, qa.at[col], own.at[2]),
        pltpu.make_async_copy(k, ka.at[row], own.at[3]),
    ]
    for copy in tables + local:
        copy.start()
    step = jnp.where(lax.broadcasted_iota(jnp.int32, (2, 128), 0) == 0, weight[0], weight[1])
    tables[0].wait()
    tables[1].wait()
    for r in range(8):
        for c in range(16):
            cut = slice((r * 16 + c) * 128, (r * 16 + c + 1) * 128)
            sf[r, c] = fv[:, cut]
            sb[r, c] = (bv[:, cut].astype(jnp.float32) * step).astype(jnp.bfloat16)
    pl.semaphore_wait(pltpu.get_barrier_semaphore(), len(peers))
    sends = Sends(send)
    local += [
        pltpu.make_async_copy(sf.at[row], fa.at[:, col, row], own.at[4]),
        pltpu.make_async_copy(sb.at[:, col], ba.at[:, col, row], own.at[5]),
    ]
    local[2].start()
    local[3].start()
    for d in range(1, 16):
        to = (col + d) % 16
        sends.start(sb.at[:, to], ba.at[:, col, row], in_b.at[col], at(c=to))
    for d in range(1, 8):
        to = (row + d) % 8
        sends.start(sf.at[to], fa.at[:, col, row], in_f.at[row], at(r=to))

    def q_part(slot, half=None):
        return qa.at[slot] if half is None else qa.at[slot, pl.ds(half * 64, 64)]

    def f_part(slot, half=None):
        return fa.at[:, slot] if half is None else fa.at[pl.ds(half * 8, 8), slot]

    def k_part(slot, half=None):
        return ka.at[slot] if half is None else ka.at[slot, pl.ds(half * 64, 64)]

    def b_part(slot, half=None):
        return ba.at[:, :, slot] if half is None else ba.at[pl.ds(half * 4, 4), :, slot]

    def src_slot(dx, dy, cc=None):
        return cslot((x + dx) % 4, (yh + dy) % 2, core if cc is None else cc)

    def tgt_slot(dz, dy):
        return ((yl + dy) % 2) * 4 + (z + dz) % 4

    def src_dev(dx, dy, dc=0):
        return at(c=cslot((x + dx) % 4, (yh + dy) % 2, (core + dc) % 2))

    def tgt_dev(dz, dy):
        return at(r=tgt_slot(dz, dy))

    source = (src_slot, src_dev, True)
    target = (tgt_slot, tgt_dev, False)
    streams = {
        "q": (q_part, recv_q, source),
        "f": (f_part, recv_f, source),
        "k": (k_part, recv_k, target),
        "b": (b_part, recv_b, target),
    }

    def push(kind, slot, peer, half=None):
        part, recv, _ = streams[kind]
        ref = part(slot, half)
        sends.start(ref, ref, recv.at[slot, 0 if half is None else half], peer)

    def arrived(kind, slot, half=None):
        part, recv, _ = streams[kind]
        ref = part(slot, half)
        remote(ref, ref, send.at[0], recv.at[slot, 0 if half is None else half], at()).wait_recv()

    def first(kind):
        slot_of, dev_of, pair = streams[kind][2]
        mine = slot_of(0, 0)
        push(kind, mine, dev_of(0, 1))
        push(kind, mine, dev_of(1, 0))
        push(kind, mine, dev_of(3, 0))
        if pair:
            push(kind, mine, dev_of(0, 0, 1))

    def second(kind):
        slot_of, dev_of, pair = streams[kind][2]
        other = slot_of(0, 1)
        arrived(kind, other)
        push(kind, other, dev_of(1, 0))
        push(kind, other, dev_of(3, 0))
        if pair:
            push(kind, other, dev_of(0, 0, 1))

    def relay(kind, dy):
        slot_of, dev_of, pair = streams[kind][2]
        for step, half in ((3, 0), (1, 1)):
            slot = slot_of(step, dy)
            arrived(kind, slot)
            push(kind, slot, dev_of(4 - step, 0), half)
            if pair:
                push(kind, slot, dev_of(0, 0, 1))

    def last(kind, dy):
        slot_of, dev_of, pair = streams[kind][2]
        slot = slot_of(2, dy)
        arrived(kind, slot, 0)
        arrived(kind, slot, 1)
        if pair:
            push(kind, slot, dev_of(0, 0, 1))

    local[0].wait()
    local[1].wait()
    first("q")
    first("k")
    local[2].wait()
    for d in range(1, 8):
        frm = (row + d) % 8
        ref = fa.at[:, col, frm]
        remote(ref, ref, send.at[0], in_f.at[frm], at()).wait_recv()
    first("f")
    local[3].wait()
    for d in range(1, 16):
        frm = (col + d) % 16
        ref = ba.at[:, frm, row]
        remote(ref, ref, send.at[0], in_b.at[frm], at()).wait_recv()
    first("b")
    relay("k", 0)
    relay("q", 0)
    second("k")
    second("q")
    relay("b", 0)
    relay("f", 0)
    second("b")
    second("f")
    relay("k", 1)
    relay("q", 1)
    relay("b", 1)
    relay("f", 1)
    for dy in range(2):
        for kind in ("k", "q", "b", "f"):
            last(kind, dy)
    for kind in ("q", "f"):
        for dx in range(4):
            for dy in range(2):
                arrived(kind, src_slot(dx, dy, 1 - core))
    sends.drain()


def gather(q, k, fwd, bwd, weight):
    bf = jnp.bfloat16
    return pl.pallas_call(
        gather_kernel,
        in_specs=[HB] * 4 + [SM],
        out_specs=[VM] * 4,
        out_shape=[
            jax.ShapeDtypeStruct((16, 128, 512), bf),
            jax.ShapeDtypeStruct((8, 128, 512), bf),
            jax.ShapeDtypeStruct((16, 16, 8, 2, 128), bf),
            jax.ShapeDtypeStruct((8, 16, 8, 2, 128), bf),
        ],
        scratch_shapes=[
            pltpu.VMEM((2, 16384), bf),
            pltpu.VMEM((2, 16384), bf),
            pltpu.VMEM((8, 16, 2, 128), bf),
            pltpu.VMEM((8, 16, 2, 128), bf),
            pltpu.SemaphoreType.DMA((100,)),
            pltpu.SemaphoreType.DMA((16, 2)),
            pltpu.SemaphoreType.DMA((16, 2)),
            pltpu.SemaphoreType.DMA((8, 2)),
            pltpu.SemaphoreType.DMA((8, 2)),
            pltpu.SemaphoreType.DMA((8,)),
            pltpu.SemaphoreType.DMA((16,)),
            pltpu.SemaphoreType.DMA((6,)),
        ],
        compiler_params=pltpu.CompilerParams(
            collective_id=0, has_side_effects=True, vmem_limit_bytes=16 << 20
        ),
        name="gather",
    )(q, k, fwd, bwd, weight)


def merge_kernel(part, ks, out, kt, landed, mine, send, recv, recv2, own):
    row, col = lax.axis_index("row"), lax.axis_index("col")
    peers = [{"row": row, "col": (col + d) % 16} for d in range(1, 16)]
    enter(peers)
    sends = Sends(send)
    keep = pltpu.make_async_copy(part.at[col], landed.at[col], own.at[0])
    keep.start()
    for d, peer in enumerate(peers):
        sends.start(part.at[peer["col"]], landed.at[col], recv.at[col], peer)
    for block in range(8):
        rows = slice(block * 128, (block + 1) * 128)
        kt[:, rows] = ks[rows, :].T
    keep.wait()
    for peer in peers:
        ref = landed.at[peer["col"]]
        remote(ref, ref, send.at[0], recv.at[peer["col"]], peer).wait_recv()
    logs = landed[:, 0:8]
    top = jnp.max(logs, axis=0)
    weight = jnp.exp(logs - top[None])
    total = jnp.sum(weight, axis=0)
    mean = jnp.sum(weight * landed[:, 8:16], axis=0) / total
    mine[0:8, :] = top + jnp.log(total) + LOG_HEADS
    mine[8:16, :] = mean
    keep = pltpu.make_async_copy(mine, out.at[col], own.at[1])
    keep.start()
    for peer in peers:
        sends.start(mine, out.at[col], recv2.at[col], peer)
    keep.wait()
    for peer in peers:
        ref = out.at[peer["col"]]
        remote(ref, ref, send.at[0], recv2.at[peer["col"]], peer).wait_recv()
    sends.drain()


def merge(part, ks):
    return pl.pallas_call(
        merge_kernel,
        in_specs=[VM] * 2,
        out_specs=[VM] * 2,
        out_shape=[
            jax.ShapeDtypeStruct((16, 16, 128), jnp.float32),
            jax.ShapeDtypeStruct((512, 1024), jnp.bfloat16),
        ],
        scratch_shapes=[
            pltpu.VMEM((16, 16, 128), jnp.float32),
            pltpu.VMEM((16, 128), jnp.float32),
            pltpu.SemaphoreType.DMA((30,)),
            pltpu.SemaphoreType.DMA((16,)),
            pltpu.SemaphoreType.DMA((16,)),
            pltpu.SemaphoreType.DMA((2,)),
        ],
        compiler_params=pltpu.CompilerParams(
            collective_id=1, has_side_effects=True, vmem_limit_bytes=4 << 20
        ),
        name="merge",
    )(part, ks)


def reduce_kernel(
    qp, kp, qo, ko, last_q, last_k, pair_in, pair_sum, hop_q, acc_q, fin_q, hop_k, acc_k, fin_k, out_q, out_k, send, recv
):
    row, col = lax.axis_index("row"), lax.axis_index("col")
    x, yh, core = col // 4, (col // 2) % 2, col % 2
    yl, z = row // 4, row % 4
    f32 = jnp.float32

    def q_dev(xx, yy, cc):
        return {"row": row, "col": xx * 4 + yy * 2 + cc}

    def k_dev(yy, zz):
        return {"row": yy * 4 + zz, "col": col}

    sibling = q_dev(x, yh, 1 - core)
    pair_y = q_dev(x, 1 - yh, core)
    pair_r = k_dev(1 - yl, z)
    sides_q = (q_dev((x + 1) % 4, yh, core), q_dev((x + 3) % 4, yh, core))
    sides_k = (k_dev(yl, (z + 1) % 4), k_dev(yl, (z + 3) % 4))
    enter([sibling, pair_y, pair_r, *sides_q, *sides_k])
    sends = Sends(send)
    parts = [pl.ds(n * 64, 64) for n in range(2)]

    def landed(ref, sem):
        remote(ref, ref, send.at[0], sem, sibling).wait_recv()
        return ref

    class Ring:
        def __init__(self, block, me, sides, hop, acc, fin, which):
            self.block, self.me, self.sides = block, me, sides
            self.hop, self.acc, self.fin, self.which = hop, acc, fin, which

        def at(self, step, half):
            return self.block((self.me + step) % 4, half)

        def far(self):
            for half in range(2):
                sends.start(
                    self.at(2, half), self.hop.at[half], recv.at[self.which, half], self.sides[half]
                )

        def near(self):
            for side, step in ((0, 1), (1, 3)):
                sends.start(
                    self.at(step, 1 - side),
                    self.fin.at[side],
                    recv.at[self.which, 2 + side],
                    self.sides[side],
                )

        def turn(self):
            for side, step in ((0, 1), (1, 3)):
                came = landed(self.hop.at[side], recv.at[self.which, side])[...].astype(f32)
                self.acc[side] = (came + self.at(step, side)[...].astype(f32)).astype(jnp.bfloat16)
                for n, rows in enumerate(parts):
                    sends.start(
                        self.acc.at[side, rows],
                        self.fin.at[2 + side, rows],
                        recv.at[self.which, 4 + 2 * side + n],
                        self.sides[side],
                    )

        def near_arrive(self):
            for slot in range(2):
                landed(self.fin.at[slot], recv.at[self.which, 2 + slot])

        def arrive(self, n):
            for side in range(2):
                landed(self.fin.at[2 + side, parts[n]], recv.at[self.which, 4 + 2 * side + n])

        def total(self, half, rows):
            return (
                self.at(0, half)[rows, :].astype(f32)
                + self.fin[1 - half, rows, :].astype(f32)
                + self.fin[2 + half, rows, :].astype(f32)
            )

    ring_q = Ring(lambda xx, half: pair_sum.at[xx, half], x, sides_q, hop_q, acc_q, fin_q, 1)
    ring_k = Ring(lambda zz, half: kp.at[half, zz], z, sides_k, hop_k, acc_k, fin_k, 2)
    order_x = [(x + d) % 4 for d in (2, 1, 3, 0)]
    for xx in order_x:
        sends.start(qp.at[xx, :, 1 - core], pair_in.at[xx], recv.at[0, xx], sibling)
    ring_k.far()
    ring_k.near()
    for n, xx in enumerate(order_x):
        came = landed(pair_in.at[xx], recv.at[0, xx])[...].astype(f32)
        pair_sum[xx] = (qp[xx, :, core].astype(f32) + came).astype(jnp.bfloat16)
        if n == 0:
            ring_q.far()
        elif n == 2:
            ring_q.near()
    ring_k.turn()
    ring_q.turn()

    def across(ring, pos, stage, last, out, peer, slot, n):
        rows = parts[n]
        ring.arrive(n)
        for half in range(2):

            @pl.when(pos != half)
            def _():
                stage[rows, :] = ring.total(half, rows).astype(jnp.bfloat16)

            @pl.when(pos == half)
            def _():
                out[rows, :] = ring.total(half, rows)

        sends.start(stage.at[rows], last.at[rows], recv.at[3, 2 * slot + n], peer)

    ring_k.near_arrive()
    ring_q.near_arrive()
    for n in range(2):
        across(ring_k, yl, out_k, last_k, ko, pair_r, 0, n)
        across(ring_q, yh, out_q, last_q, qo, pair_y, 1, n)
    for n in range(2):
        landed(last_k.at[parts[n]], recv.at[3, n])
        landed(last_q.at[parts[n]], recv.at[3, 2 + n])
    sends.drain()


def reduce(qp, kp):
    bf = jnp.bfloat16
    block = (128, 512)
    return pl.pallas_call(
        reduce_kernel,
        in_specs=[VM] * 2,
        out_specs=[VM] * 4,
        out_shape=[jax.ShapeDtypeStruct(block, jnp.float32)] * 2
        + [jax.ShapeDtypeStruct(block, bf)] * 2,
        scratch_shapes=[
            pltpu.VMEM((4, 2, *block), bf),
            pltpu.VMEM((4, 2, *block), bf),
            pltpu.VMEM((2, *block), bf),
            pltpu.VMEM((2, *block), bf),
            pltpu.VMEM((4, *block), bf),
            pltpu.VMEM((2, *block), bf),
            pltpu.VMEM((2, *block), bf),
            pltpu.VMEM((4, *block), bf),
            pltpu.VMEM(block, bf),
            pltpu.VMEM(block, bf),
            pltpu.SemaphoreType.DMA((24,)),
            pltpu.SemaphoreType.DMA((4, 8)),
        ],
        compiler_params=pltpu.CompilerParams(
            collective_id=2, has_side_effects=True, vmem_limit_bytes=16 << 20
        ),
        name="reduce",
    )(qp, kp)


def mask_keys(ks, km):
    half = lax.broadcasted_iota(jnp.int32, (128, 128), 1) < HEAD
    for block in range(8):
        rows = slice(block * 128, (block + 1) * 128)
        for h in range(HEADS):
            kk = ks[rows, (h // 2) * 128 : (h // 2 + 1) * 128]
            keep = half if h % 2 == 0 else jnp.logical_not(half)
            km[h, rows, :] = jnp.where(keep, kk, jnp.zeros_like(kk))


def order_of(meta, which, g):
    return meta[which * NU + g]


def place_of(meta, which, g):
    return meta[NU + NV + which * NU + g]


def rows_of(g):
    return pl.ds(pl.multiple_of(g * GRAIN, GRAIN), GRAIN)


def chunk_bounds(meta, i):
    low = place_of(meta, 0, i * (UB // GRAIN))
    high = place_of(meta, 0, (i + 1) * (UB // GRAIN) - 1)
    per = VC // GRAIN
    first = jnp.int32(0)
    full = jnp.int32(0)
    for j in range(NV // per):
        first += (place_of(meta, 1, (j + 1) * per - 1) < low).astype(jnp.int32)
        full += (place_of(meta, 1, j * per) <= high).astype(jnp.int32)
    return first, full


def chunk_valid(meta, pu, j, width):
    off = lax.broadcasted_iota(jnp.int32, (GRAIN, UB), 0)
    per = VC // GRAIN
    pv = jnp.concatenate(
        [off + GRAIN * place_of(meta, 1, j * per + t) for t in range(width * per)], axis=0
    )
    return pv >= pu


def largest_norm(ref, n):
    width = HEADS * HEAD
    head = lax.broadcasted_iota(jnp.int32, (16, width), 1) // HEAD
    pick = (head == lax.broadcasted_iota(jnp.int32, (16, width), 0)).astype(jnp.bfloat16)
    best = jnp.zeros((16, 256), jnp.float32)
    for block in range(n // 256):
        rows = ref[block * 256 : (block + 1) * 256, :]
        best = jnp.maximum(best, nt(pick, rows * rows))
    return jnp.max(best) * 1.02


def stats_kernel(
    q_ref, k_ref, f_ref, b_ref, meta, pu_ref, out, qs, ks, ws, ms, cs, fs, bs, km, ft, bt, run_m, run_t, run_e, held, sem
):
    def flush(n):
        slot = n % SLOTS
        return pltpu.make_async_copy(held.at[slot], ws.at[n], sem.at[slot])

    for block in range(16):
        ft[block * 128 : (block + 1) * 128, :] = f_ref[block].T
    for block in range(8):
        bt[block * 128 : (block + 1) * 128, :] = b_ref[block].T

    def sort_sources(g, _):
        frm = rows_of(order_of(meta, 0, g))
        qs[rows_of(g), :] = q_ref[frm, :] * jnp.bfloat16(SCALE)
        fs[rows_of(g), :] = ft[frm, :]
        return 0

    def sort_targets(g, _):
        frm = rows_of(order_of(meta, 1, g))
        ks[rows_of(g), :] = k_ref[frm, :]
        bs[rows_of(g), :] = bt[frm, :]
        return 0

    lax.fori_loop(0, NU, sort_sources, 0)
    lax.fori_loop(0, NV, sort_targets, 0)
    mask_keys(ks, km)
    plain = largest_norm(qs, 2048) * largest_norm(ks, 1024) < SAFE * SAFE
    start = jnp.where(plain, 0.0, TOP)

    def sources(i, tile):
        us = pl.ds(pl.multiple_of(i * UB, UB), UB)
        first, full = chunk_bounds(meta, i)
        odd = first % 2
        mixed = jnp.maximum(full - first - odd + 1, 0) // 2
        pairs = (1024 // VC - first) // 2
        run_m[...] = jnp.full(run_m.shape, start, jnp.float32)
        run_t[...] = jnp.zeros_like(run_t)
        run_e[...] = jnp.zeros_like(run_e)

        def targets(j, width, masked, shift):
            rows = width * VC
            vs = pl.ds(pl.multiple_of(j * VC, VC), rows)
            n = tile + j - first
            for t in range(width):

                @pl.when(n + t >= SLOTS)
                def _():
                    flush(n + t - SLOTS).wait()

            counts = nt(bs[vs, :], fs[us, :])
            if masked:
                valid = chunk_valid(meta, pu_ref[pl.ds(i, 1), :], j, width)
            for h in range(HEADS):
                scores = nt(km[h, vs, :], qs[us, (h // 2) * 128 : (h // 2 + 1) * 128])
                if masked:
                    scores = jnp.where(valid, scores, NEG)
                for t in range(rows // SUB):
                    part = slice(t * SUB, (t + 1) * SUB)
                    s = scores[part].reshape(SUB // 8, 8, UB)
                    c = counts[part].reshape(SUB // 8, 8, UB)
                    if shift:
                        old = run_m[h]
                        new = jnp.maximum(old, jnp.max(s, axis=0))
                        w = jnp.exp(s - new[None])
                        shrink = jnp.exp(old - new)
                        run_m[h] = new
                        run_t[h] = run_t[h] * shrink + jnp.sum(w, axis=0)
                        run_e[h] = run_e[h] * shrink + jnp.sum(w * c, axis=0)
                    else:
                        new = jnp.zeros((8, UB), jnp.float32)
                        w = jnp.exp(s)
                        run_t[h] += jnp.sum(w, axis=0)
                        run_e[h] += jnp.sum(w * c, axis=0)
                    at = t * SUB // VC
                    inner = t % (VC // SUB)
                    held[(n + at) % SLOTS, h, inner * SUB : (inner + 1) * SUB, :] = w.reshape(
                        SUB, UB
                    ).astype(jnp.bfloat16)
                    ms[n + at, h, inner] = new
            for t in range(width):
                cs[n + t] = counts[t * VC : (t + 1) * VC]
                flush(n + t).start()

        def sweep(shift):
            def single(j, _):
                targets(first, 1, True, shift)
                return 0

            def mixed_pair(j, _):
                targets(first + odd + 2 * j, 2, True, shift)
                return 0

            def open_pair(j, _):
                targets(first + odd + 2 * j, 2, False, shift)
                return 0

            lax.fori_loop(0, odd, single, 0)
            lax.fori_loop(0, mixed, mixed_pair, 0)
            lax.fori_loop(mixed, pairs, open_pair, 0)

        @pl.when(plain)
        def _():
            sweep(False)

        @pl.when(jnp.logical_not(plain))
        def _():
            sweep(True)

        for h in range(HEADS):
            part_m = run_m[h]
            top = jnp.max(part_m, axis=0, keepdims=True)
            weight = jnp.exp(part_m - top)
            total = jnp.sum(run_t[h] * weight, axis=0, keepdims=True)
            expect = jnp.sum(run_e[h] * weight, axis=0, keepdims=True)
            some = total > 0.0
            safe = jnp.where(some, total, 1.0)
            log = jnp.where(some, top + jnp.log(safe), NEG)
            mean = expect / safe
            for t in range(UB // 128):
                at = i * (UB // 128) + t
                out[at, h : h + 1, :] = log[:, t * 128 : (t + 1) * 128]
                out[at, HEADS + h : HEADS + h + 1, :] = mean[:, t * 128 : (t + 1) * 128]
        return tile + 1024 // VC - first

    count = lax.fori_loop(0, 2048 // UB, sources, jnp.int32(0))
    for back in range(1, SLOTS + 1):

        @pl.when(count >= back)
        def _():
            flush(count - back).wait()


def stats(q, k, f, b, meta, pu):
    bf = jnp.bfloat16
    return pl.pallas_call(
        stats_kernel,
        in_specs=[VM] * 4 + [SM, VM],
        out_specs=[VM] * 3 + [pl.BlockSpec(memory_space=pl.ANY), VM, VM],
        out_shape=[
            jax.ShapeDtypeStruct((16, 16, 128), jnp.float32),
            jax.ShapeDtypeStruct((2048, 512), bf),
            jax.ShapeDtypeStruct((1024, 512), bf),
            jax.ShapeDtypeStruct((TILES, HEADS, VC, UB), bf),
            jax.ShapeDtypeStruct((TILES, HEADS, VC // SUB, 8, UB), jnp.float32),
            jax.ShapeDtypeStruct((TILES, VC, UB), jnp.float32),
        ],
        scratch_shapes=[
            pltpu.VMEM((2048, 256), bf),
            pltpu.VMEM((1024, 256), bf),
            pltpu.VMEM((HEADS, 1024, 128), bf),
            pltpu.VMEM((2048, 256), bf),
            pltpu.VMEM((1024, 256), bf),
            pltpu.VMEM((HEADS, 8, UB), jnp.float32),
            pltpu.VMEM((HEADS, 8, UB), jnp.float32),
            pltpu.VMEM((HEADS, 8, UB), jnp.float32),
            pltpu.VMEM((SLOTS, HEADS, VC, UB), bf),
            pltpu.SemaphoreType.DMA((SLOTS,)),
        ],
        compiler_params=pltpu.CompilerParams(vmem_limit_bytes=12 << 20),
        name="stats",
    )(q, k, f, b, meta, pu)


def grads_kernel(qs, kt, ws, ms, cs, meta, st, qg, kg, qacc, kacc, held, sem):
    def fetch(n):
        slot = n % SLOTS
        return pltpu.make_async_copy(ws.at[n], held.at[slot], sem.at[slot])

    count = jnp.int32(0)
    for i in range(2048 // UB):
        count += 1024 // VC - chunk_bounds(meta, i)[0]
    for n in range(SLOTS):

        @pl.when(count > n)
        def _():
            fetch(n).start()

    kacc[...] = jnp.zeros_like(kacc)

    def sources(i, tile):
        us = pl.ds(pl.multiple_of(i * UB, UB), UB)
        first, _ = chunk_bounds(meta, i)
        both = jnp.concatenate([st[i * (UB // 128) + t] for t in range(UB // 128)], axis=1)
        qacc[...] = jnp.zeros_like(qacc)

        def targets(j, width):
            rows = width * VC
            vs = pl.ds(pl.multiple_of(j * VC, VC), rows)
            n = tile + j - first
            for t in range(width):
                fetch(n + t).wait()
            low = lax.broadcasted_iota(jnp.int32, (rows, 128), 1) < HEAD
            pair = []
            for h in range(HEADS):
                log = both[h : h + 1]
                mean = both[HEADS + h : HEADS + h + 1]
                parts = []
                for t in range(rows // SUB):
                    at = t * SUB // VC
                    inner = t % (VC // SUB)
                    w = held[(n + at) % SLOTS, h, inner * SUB : (inner + 1) * SUB, :].astype(
                        jnp.float32
                    )
                    scale = jnp.exp(ms[n + at, h, inner] - log)
                    w = (w.reshape(SUB // 8, 8, UB) * scale[None]).reshape(SUB, UB)
                    counts = cs[n + at, inner * SUB : (inner + 1) * SUB, :]
                    parts.append((w * (mean - counts)).astype(jnp.bfloat16))
                g = jnp.concatenate(parts, axis=0)
                hs = slice(h * HEAD, (h + 1) * HEAD)
                qacc[hs, :] += nn(kt[hs, vs], g)
                pair.append(nn(g, qs[us, (h // 2) * 128 : (h // 2 + 1) * 128]))
                if h % 2:
                    cols = slice((h // 2) * 128, (h // 2 + 1) * 128)
                    kacc[vs, cols] += jnp.where(low, pair[-2], pair[-1])
            for t in range(width):

                @pl.when(n + t + SLOTS < count)
                def _():
                    fetch(n + t + SLOTS).start()

        odd = first % 2

        def single(j, _):
            targets(first, 1)
            return 0

        def double(j, _):
            targets(first + odd + 2 * j, 2)
            return 0

        lax.fori_loop(0, odd, single, 0)
        lax.fori_loop(0, (1024 // VC - first) // 2, double, 0)
        turned = (qacc[...] * SCALE).T.astype(jnp.bfloat16)
        for t in range(UB // GRAIN):
            to = order_of(meta, 0, i * (UB // GRAIN) + t)
            qg[rows_of(to), :] = turned[t * GRAIN : (t + 1) * GRAIN]
        return tile + 1024 // VC - first

    lax.fori_loop(0, 2048 // UB, sources, jnp.int32(0))

    def unsort(g, _):
        kg[rows_of(order_of(meta, 1, g)), :] = kacc[rows_of(g), :].astype(jnp.bfloat16)
        return 0

    lax.fori_loop(0, NV, unsort, 0)


def grads(qs, kt, ws, ms, cs, meta, st):
    bf = jnp.bfloat16
    return pl.pallas_call(
        grads_kernel,
        in_specs=[VM] * 2 + [pl.BlockSpec(memory_space=pl.ANY), VM, VM, SM, VM],
        out_specs=[VM] * 2,
        out_shape=[
            jax.ShapeDtypeStruct((2048, 512), bf),
            jax.ShapeDtypeStruct((1024, 512), bf),
        ],
        scratch_shapes=[
            pltpu.VMEM((512, UB), jnp.float32),
            pltpu.VMEM((1024, 512), jnp.float32),
            pltpu.VMEM((SLOTS, HEADS, VC, UB), bf),
            pltpu.SemaphoreType.DMA((SLOTS,)),
        ],
        compiler_params=pltpu.CompilerParams(vmem_limit_bytes=12 << 20),
        name="grads",
    )(qs, kt, ws, ms, cs, meta, st)


def in_order(places, index):
    n = places.shape[0]
    rank = jnp.sum((places[None, :] < places[:, None]).astype(jnp.int32), axis=1)
    hit = rank[None, :] == jnp.arange(n, dtype=jnp.int32)[:, None]
    return (
        jnp.sum(jnp.where(hit, index[None, :], 0), axis=1),
        jnp.sum(jnp.where(hit, places[None, :], 0), axis=1),
    )


def local(queries, keys, fwd_table, bwd_table, step_weight, block_order):
    row_id = lax.axis_index("row")
    col_id = lax.axis_index("col")
    block_order = lax.optimization_barrier(jnp.maximum(block_order, 0))
    line = lax.dynamic_slice_in_dim(block_order, row_id * NU, NU)
    pairs = block_order.reshape(4, 128)
    column = jnp.concatenate(
        [
            lax.dynamic_slice_in_dim(pairs, NU * odd + 4 * col_id, 4, axis=1).reshape(16)
            for odd in range(2)
        ]
    )
    at = jnp.arange(NV, dtype=jnp.int32)
    order_u, place_u = in_order(line, jnp.arange(NU, dtype=jnp.int32))
    order_v, place_v = in_order(column, at % 16 // 4 * 8 + at // 16 * 4 + at % 4)
    meta = jnp.concatenate([order_u, order_v, place_u, place_v])
    offsets = jnp.arange(GRAIN, dtype=jnp.int32)
    pu = (place_u[:, None] * GRAIN + offsets[None, :]).reshape(8, 256)
    here = [
        pltpu.with_memory_space_constraint(a, pltpu.MemorySpace.HBM)
        for a in (queries, keys, fwd_table, bwd_table, step_weight)
    ]
    q, k, f, b = gather(*here)
    part, qs, ks, ws, ms, cs = stats(
        q.reshape(2048, 512),
        k.reshape(1024, 512),
        f.reshape(16, 256, 128),
        b.reshape(8, 256, 128),
        meta,
        pu,
    )
    st, kt = merge(part, ks)
    qg, kg = grads(qs, kt, ws, ms, cs, meta, st)
    q_own, k_own, q_last, k_last = reduce(qg.reshape(4, 2, 2, 128, 512), kg.reshape(2, 4, 128, 512))
    return q_own + q_last.astype(jnp.float32), k_own + k_last.astype(jnp.float32)


def solution(mesh):
    return jax.shard_map(
        local,
        mesh=mesh,
        in_specs=(
            P(("row", "col"), None),
            P(("row", "col"), None),
            P(("row", "col"), None),
            P(("row", "col"), None),
            P(("row", "col")),
            P(),
        ),
        out_specs=(P(("row", "col"), None), P(("row", "col"), None)),
        check_vma=False,
    )
```

```python
import jax
import jax.numpy as jnp
from jax import lax
from jax.experimental import pallas as pl
from jax.experimental.pallas import tpu as pltpu
from jax.sharding import PartitionSpec as P

HEADS = 8
HEAD = 64
GRAIN = 32
SCALE = HEAD**-0.5
LOG_HEADS = 2.0794415416798357
NEG = -1e30
SAFE = 40.0
TOP = -1e29
NU = 64
NV = 32
TILES = 64
SLOTS = 4
UB = 256
VC = 128
SUB = 128
MESH = pl.DeviceIdType.MESH
VM = pl.BlockSpec(memory_space=pltpu.VMEM)
SM = pl.BlockSpec(memory_space=pltpu.SMEM)
HB = pl.BlockSpec(memory_space=pltpu.MemorySpace.HBM)


def nn(a, b):
    return lax.dot_general(a, b, (((1,), (0,)), ((), ())), preferred_element_type=jnp.float32)


def nt(a, b):
    return lax.dot_general(a, b, (((1,), (1,)), ((), ())), preferred_element_type=jnp.float32)


def remote(src, dst, send, recv, peer):
    return pltpu.make_async_remote_copy(
        src_ref=src, dst_ref=dst, send_sem=send, recv_sem=recv, device_id=peer, device_id_type=MESH
    )


def greet(peers):
    barrier = pltpu.get_barrier_semaphore()
    for peer in peers:
        pl.semaphore_signal(barrier, inc=1, device_id=peer, device_id_type=MESH)


def enter(peers):
    greet(peers)
    pl.semaphore_wait(pltpu.get_barrier_semaphore(), len(peers))


class Sends:
    def __init__(self, sems):
        self.sems = sems
        self.started = []

    def start(self, src, dst, recv, peer):
        copy = remote(src, dst, self.sems.at[len(self.started)], recv, peer)
        copy.start()
        self.started.append(copy)

    def drain(self):
        for copy in self.started:
            copy.wait_send()


def gather_kernel(
    q, k, fwd, bwd, weight, qa, ka, fa, ba, fv, bv, sf, sb, send, recv_q, recv_f, recv_k, recv_b, in_f, in_b, own
):
    row, col = lax.axis_index("row"), lax.axis_index("col")
    x, yh, core = col // 4, (col // 2) % 2, col % 2
    yl, z = row // 4, row % 4

    def at(r=None, c=None):
        return {"row": row if r is None else r, "col": col if c is None else c}

    def cslot(xx, yy, cc):
        return xx * 4 + yy * 2 + cc

    peers = [at(r=(row + d) % 8) for d in range(1, 8)] + [at(c=(col + d) % 16) for d in range(1, 16)]
    greet(peers)
    tables = [pltpu.make_async_copy(fwd, fv, own.at[0]), pltpu.make_async_copy(bwd, bv, own.at[1])]
    local = [
        pltpu.make_async_copy(q, qa.at[col], own.at[2]),
        pltpu.make_async_copy(k, ka.at[row], own.at[3]),
    ]
    for copy in tables + local:
        copy.start()
    step = jnp.where(lax.broadcasted_iota(jnp.int32, (2, 128), 0) == 0, weight[0], weight[1])
    tables[0].wait()
    tables[1].wait()
    for r in range(8):
        for c in range(16):
            cut = slice((r * 16 + c) * 128, (r * 16 + c + 1) * 128)
            sf[r, c] = fv[:, cut]
            sb[r, c] = (bv[:, cut].astype(jnp.float32) * step).astype(jnp.bfloat16)
    pl.semaphore_wait(pltpu.get_barrier_semaphore(), len(peers))
    sends = Sends(send)
    local += [
        pltpu.make_async_copy(sf.at[row], fa.at[:, col, row], own.at[4]),
        pltpu.make_async_copy(sb.at[:, col], ba.at[:, col, row], own.at[5]),
    ]
    local[2].start()
    local[3].start()
    for d in range(1, 16):
        to = (col + d) % 16
        sends.start(sb.at[:, to], ba.at[:, col, row], in_b.at[col], at(c=to))
    for d in range(1, 8):
        to = (row + d) % 8
        sends.start(sf.at[to], fa.at[:, col, row], in_f.at[row], at(r=to))

    def q_part(slot, half=None):
        return qa.at[slot] if half is None else qa.at[slot, pl.ds(half * 64, 64)]

    def f_part(slot, half=None):
        return fa.at[:, slot] if half is None else fa.at[pl.ds(half * 8, 8), slot]

    def k_part(slot, half=None):
        return ka.at[slot] if half is None else ka.at[slot, pl.ds(half * 64, 64)]

    def b_part(slot, half=None):
        return ba.at[:, :, slot] if half is None else ba.at[pl.ds(half * 4, 4), :, slot]

    def src_slot(dx, dy, cc=None):
        return cslot((x + dx) % 4, (yh + dy) % 2, core if cc is None else cc)

    def tgt_slot(dz, dy):
        return ((yl + dy) % 2) * 4 + (z + dz) % 4

    def src_dev(dx, dy, dc=0):
        return at(c=cslot((x + dx) % 4, (yh + dy) % 2, (core + dc) % 2))

    def tgt_dev(dz, dy):
        return at(r=tgt_slot(dz, dy))

    source = (src_slot, src_dev, True)
    target = (tgt_slot, tgt_dev, False)
    streams = {
        "q": (q_part, recv_q, source),
        "f": (f_part, recv_f, source),
        "k": (k_part, recv_k, target),
        "b": (b_part, recv_b, target),
    }

    def push(kind, slot, peer, half=None):
        part, recv, _ = streams[kind]
        ref = part(slot, half)
        sends.start(ref, ref, recv.at[slot, 0 if half is None else half], peer)

    def arrived(kind, slot, half=None):
        part, recv, _ = streams[kind]
        ref = part(slot, half)
        remote(ref, ref, send.at[0], recv.at[slot, 0 if half is None else half], at()).wait_recv()

    def first(kind):
        slot_of, dev_of, pair = streams[kind][2]
        mine = slot_of(0, 0)
        push(kind, mine, dev_of(0, 1))
        push(kind, mine, dev_of(1, 0))
        push(kind, mine, dev_of(3, 0))
        if pair:
            push(kind, mine, dev_of(0, 0, 1))

    def second(kind):
        slot_of, dev_of, pair = streams[kind][2]
        other = slot_of(0, 1)
        arrived(kind, other)
        push(kind, other, dev_of(1, 0))
        push(kind, other, dev_of(3, 0))
        if pair:
            push(kind, other, dev_of(0, 0, 1))

    def relay(kind, dy):
        slot_of, dev_of, pair = streams[kind][2]
        for step, half in ((3, 0), (1, 1)):
            slot = slot_of(step, dy)
            arrived(kind, slot)
            push(kind, slot, dev_of(4 - step, 0), half)
            if pair:
                push(kind, slot, dev_of(0, 0, 1))

    def last(kind, dy):
        slot_of, dev_of, pair = streams[kind][2]
        slot = slot_of(2, dy)
        arrived(kind, slot, 0)
        arrived(kind, slot, 1)
        if pair:
            push(kind, slot, dev_of(0, 0, 1))

    local[0].wait()
    local[1].wait()
    first("q")
    first("k")
    local[2].wait()
    for d in range(1, 8):
        frm = (row + d) % 8
        ref = fa.at[:, col, frm]
        remote(ref, ref, send.at[0], in_f.at[frm], at()).wait_recv()
    first("f")
    local[3].wait()
    for d in range(1, 16):
        frm = (col + d) % 16
        ref = ba.at[:, frm, row]
        remote(ref, ref, send.at[0], in_b.at[frm], at()).wait_recv()
    first("b")
    relay("k", 0)
    relay("q", 0)
    second("k")
    second("q")
    relay("b", 0)
    relay("f", 0)
    second("b")
    second("f")
    relay("k", 1)
    relay("q", 1)
    relay("b", 1)
    relay("f", 1)
    for dy in range(2):
        for kind in ("k", "q", "b", "f"):
            last(kind, dy)
    for kind in ("q", "f"):
        for dx in range(4):
            for dy in range(2):
                arrived(kind, src_slot(dx, dy, 1 - core))
    sends.drain()


def gather(q, k, fwd, bwd, weight):
    bf = jnp.bfloat16
    return pl.pallas_call(
        gather_kernel,
        in_specs=[HB] * 4 + [SM],
        out_specs=[VM] * 4,
        out_shape=[
            jax.ShapeDtypeStruct((16, 128, 512), bf),
            jax.ShapeDtypeStruct((8, 128, 512), bf),
            jax.ShapeDtypeStruct((16, 16, 8, 2, 128), bf),
            jax.ShapeDtypeStruct((8, 16, 8, 2, 128), bf),
        ],
        scratch_shapes=[
            pltpu.VMEM((2, 16384), bf),
            pltpu.VMEM((2, 16384), bf),
            pltpu.VMEM((8, 16, 2, 128), bf),
            pltpu.VMEM((8, 16, 2, 128), bf),
            pltpu.SemaphoreType.DMA((100,)),
            pltpu.SemaphoreType.DMA((16, 2)),
            pltpu.SemaphoreType.DMA((16, 2)),
            pltpu.SemaphoreType.DMA((8, 2)),
            pltpu.SemaphoreType.DMA((8, 2)),
            pltpu.SemaphoreType.DMA((8,)),
            pltpu.SemaphoreType.DMA((16,)),
            pltpu.SemaphoreType.DMA((6,)),
        ],
        compiler_params=pltpu.CompilerParams(
            collective_id=0, has_side_effects=True, vmem_limit_bytes=16 << 20
        ),
        name="gather",
    )(q, k, fwd, bwd, weight)


def merge_kernel(part, ks, out, kt, landed, mine, send, recv, recv2, own):
    row, col = lax.axis_index("row"), lax.axis_index("col")
    peers = [{"row": row, "col": (col + d) % 16} for d in range(1, 16)]
    enter(peers)
    sends = Sends(send)
    keep = pltpu.make_async_copy(part.at[col], landed.at[col], own.at[0])
    keep.start()
    for d, peer in enumerate(peers):
        sends.start(part.at[peer["col"]], landed.at[col], recv.at[col], peer)
    for block in range(8):
        rows = slice(block * 128, (block + 1) * 128)
        kt[:, rows] = ks[rows, :].T
    keep.wait()
    for peer in peers:
        ref = landed.at[peer["col"]]
        remote(ref, ref, send.at[0], recv.at[peer["col"]], peer).wait_recv()
    logs = landed[:, 0:8]
    top = jnp.max(logs, axis=0)
    weight = jnp.exp(logs - top[None])
    total = jnp.sum(weight, axis=0)
    mean = jnp.sum(weight * landed[:, 8:16], axis=0) / total
    mine[0:8, :] = top + jnp.log(total) + LOG_HEADS
    mine[8:16, :] = mean
    keep = pltpu.make_async_copy(mine, out.at[col], own.at[1])
    keep.start()
    for peer in peers:
        sends.start(mine, out.at[col], recv2.at[col], peer)
    keep.wait()
    for peer in peers:
        ref = out.at[peer["col"]]
        remote(ref, ref, send.at[0], recv2.at[peer["col"]], peer).wait_recv()
    sends.drain()


def merge(part, ks):
    return pl.pallas_call(
        merge_kernel,
        in_specs=[VM] * 2,
        out_specs=[VM] * 2,
        out_shape=[
            jax.ShapeDtypeStruct((16, 16, 128), jnp.float32),
            jax.ShapeDtypeStruct((512, 1024), jnp.bfloat16),
        ],
        scratch_shapes=[
            pltpu.VMEM((16, 16, 128), jnp.float32),
            pltpu.VMEM((16, 128), jnp.float32),
            pltpu.SemaphoreType.DMA((30,)),
            pltpu.SemaphoreType.DMA((16,)),
            pltpu.SemaphoreType.DMA((16,)),
            pltpu.SemaphoreType.DMA((2,)),
        ],
        compiler_params=pltpu.CompilerParams(
            collective_id=1, has_side_effects=True, vmem_limit_bytes=4 << 20
        ),
        name="merge",
    )(part, ks)


def reduce_kernel(
    qp, kp, own, last, pair_in, pair_sum, hop_q, acc_q, fin_q, hop_k, acc_k, fin_k, out_q, out_k, send, recv
):
    row, col = lax.axis_index("row"), lax.axis_index("col")
    x, yh, core = col // 4, (col // 2) % 2, col % 2
    yl, z = row // 4, row % 4
    f32 = jnp.float32
    qo, ko, last_q, last_k = own.at[0], own.at[1], last.at[0], last.at[1]

    def q_dev(xx, yy, cc):
        return {"row": row, "col": xx * 4 + yy * 2 + cc}

    def k_dev(yy, zz):
        return {"row": yy * 4 + zz, "col": col}

    sibling = q_dev(x, yh, 1 - core)
    pair_y = q_dev(x, 1 - yh, core)
    pair_r = k_dev(1 - yl, z)
    sides_q = (q_dev((x + 1) % 4, yh, core), q_dev((x + 3) % 4, yh, core))
    sides_k = (k_dev(yl, (z + 1) % 4), k_dev(yl, (z + 3) % 4))
    enter([sibling, pair_y, pair_r, *sides_q, *sides_k])
    sends = Sends(send)
    parts = [pl.ds(n * 64, 64) for n in range(2)]

    def landed(ref, sem):
        remote(ref, ref, send.at[0], sem, sibling).wait_recv()
        return ref

    class Ring:
        def __init__(self, block, me, sides, hop, acc, fin, which):
            self.block, self.me, self.sides = block, me, sides
            self.hop, self.acc, self.fin, self.which = hop, acc, fin, which

        def at(self, step, half):
            return self.block((self.me + step) % 4, half)

        def far(self):
            for half in range(2):
                sends.start(
                    self.at(2, half), self.hop.at[half], recv.at[self.which, half], self.sides[half]
                )

        def near(self):
            for side, step in ((0, 1), (1, 3)):
                sends.start(
                    self.at(step, 1 - side),
                    self.fin.at[side],
                    recv.at[self.which, 2 + side],
                    self.sides[side],
                )

        def turn(self):
            for side, step in ((0, 1), (1, 3)):
                came = landed(self.hop.at[side], recv.at[self.which, side])[...].astype(f32)
                self.acc[side] = (came + self.at(step, side)[...].astype(f32)).astype(jnp.bfloat16)
                for n, rows in enumerate(parts):
                    sends.start(
                        self.acc.at[side, rows],
                        self.fin.at[2 + side, rows],
                        recv.at[self.which, 4 + 2 * side + n],
                        self.sides[side],
                    )

        def near_arrive(self):
            for slot in range(2):
                landed(self.fin.at[slot], recv.at[self.which, 2 + slot])

        def arrive(self, n):
            for side in range(2):
                landed(self.fin.at[2 + side, parts[n]], recv.at[self.which, 4 + 2 * side + n])

        def total(self, half, rows):
            return (
                self.at(0, half)[rows, :].astype(f32)
                + self.fin[1 - half, rows, :].astype(f32)
                + self.fin[2 + half, rows, :].astype(f32)
            )

    ring_q = Ring(lambda xx, half: pair_sum.at[xx, half], x, sides_q, hop_q, acc_q, fin_q, 1)
    ring_k = Ring(lambda zz, half: kp.at[half, zz], z, sides_k, hop_k, acc_k, fin_k, 2)
    order_x = [(x + d) % 4 for d in (2, 1, 3, 0)]
    for xx in order_x:
        sends.start(qp.at[xx, :, 1 - core], pair_in.at[xx], recv.at[0, xx], sibling)
    ring_k.far()
    ring_k.near()
    for n, xx in enumerate(order_x):
        came = landed(pair_in.at[xx], recv.at[0, xx])[...].astype(f32)
        pair_sum[xx] = (qp[xx, :, core].astype(f32) + came).astype(jnp.bfloat16)
        if n == 0:
            ring_q.far()
        elif n == 2:
            ring_q.near()
    ring_k.turn()
    ring_q.turn()

    def across(ring, pos, stage, last, out, peer, slot, n):
        rows = parts[n]
        ring.arrive(n)
        for half in range(2):

            @pl.when(pos != half)
            def _():
                stage[rows, :] = ring.total(half, rows).astype(jnp.bfloat16)

            @pl.when(pos == half)
            def _():
                out[rows, :] = ring.total(half, rows)

        sends.start(stage.at[rows], last.at[rows], recv.at[3, 2 * slot + n], peer)

    ring_k.near_arrive()
    ring_q.near_arrive()
    for n in range(2):
        across(ring_k, yl, out_k, last_k, ko, pair_r, 0, n)
        across(ring_q, yh, out_q, last_q, qo, pair_y, 1, n)
    for n in range(2):
        landed(last_k.at[parts[n]], recv.at[3, n])
        landed(last_q.at[parts[n]], recv.at[3, 2 + n])
    sends.drain()


def reduce(qp, kp):
    bf = jnp.bfloat16
    block = (128, 512)
    return pl.pallas_call(
        reduce_kernel,
        in_specs=[VM] * 2,
        out_specs=[VM] * 2,
        out_shape=[
            jax.ShapeDtypeStruct((2, *block), jnp.float32),
            jax.ShapeDtypeStruct((2, *block), bf),
        ],
        scratch_shapes=[
            pltpu.VMEM((4, 2, *block), bf),
            pltpu.VMEM((4, 2, *block), bf),
            pltpu.VMEM((2, *block), bf),
            pltpu.VMEM((2, *block), bf),
            pltpu.VMEM((4, *block), bf),
            pltpu.VMEM((2, *block), bf),
            pltpu.VMEM((2, *block), bf),
            pltpu.VMEM((4, *block), bf),
            pltpu.VMEM(block, bf),
            pltpu.VMEM(block, bf),
            pltpu.SemaphoreType.DMA((24,)),
            pltpu.SemaphoreType.DMA((4, 8)),
        ],
        compiler_params=pltpu.CompilerParams(
            collective_id=2, has_side_effects=True, vmem_limit_bytes=16 << 20
        ),
        name="reduce",
    )(qp, kp)


def mask_keys(ks, km):
    half = lax.broadcasted_iota(jnp.int32, (128, 128), 1) < HEAD
    for block in range(8):
        rows = slice(block * 128, (block + 1) * 128)
        for h in range(HEADS):
            kk = ks[rows, (h // 2) * 128 : (h // 2 + 1) * 128]
            keep = half if h % 2 == 0 else jnp.logical_not(half)
            km[h, rows, :] = jnp.where(keep, kk, jnp.zeros_like(kk))


def order_of(meta, which, g):
    return meta[which * NU + g]


def place_of(meta, which, g):
    return meta[NU + NV + which * NU + g]


def rows_of(g):
    return pl.ds(pl.multiple_of(g * GRAIN, GRAIN), GRAIN)


def chunk_bounds(meta, i):
    low = place_of(meta, 0, i * (UB // GRAIN))
    high = place_of(meta, 0, (i + 1) * (UB // GRAIN) - 1)
    per = VC // GRAIN
    first = jnp.int32(0)
    full = jnp.int32(0)
    for j in range(NV // per):
        first += (place_of(meta, 1, (j + 1) * per - 1) < low).astype(jnp.int32)
        full += (place_of(meta, 1, j * per) <= high).astype(jnp.int32)
    return first, full


def chunk_valid(meta, pu, j, width):
    off = lax.broadcasted_iota(jnp.int32, (GRAIN, UB), 0)
    per = VC // GRAIN
    pv = jnp.concatenate(
        [off + GRAIN * place_of(meta, 1, j * per + t) for t in range(width * per)], axis=0
    )
    return pv >= pu


def largest_norm(ref, n):
    width = HEADS * HEAD
    head = lax.broadcasted_iota(jnp.int32, (16, width), 1) // HEAD
    pick = (head == lax.broadcasted_iota(jnp.int32, (16, width), 0)).astype(jnp.bfloat16)
    best = jnp.zeros((16, 256), jnp.float32)
    for block in range(n // 256):
        rows = ref[block * 256 : (block + 1) * 256, :]
        best = jnp.maximum(best, nt(pick, rows * rows))
    return jnp.max(best) * 1.02


def stats_kernel(
    q_ref, k_ref, f_ref, b_ref, meta, pu_ref, out, qs, ks, ws, ms, cs, fs, bs, km, ft, bt, run_m, run_t, run_e, held, sem
):
    def flush(n):
        slot = n % SLOTS
        return pltpu.make_async_copy(held.at[slot], ws.at[n], sem.at[slot])

    for block in range(16):
        ft[block * 128 : (block + 1) * 128, :] = f_ref[block].T
    for block in range(8):
        bt[block * 128 : (block + 1) * 128, :] = b_ref[block].T

    def sort_sources(g, _):
        frm = rows_of(order_of(meta, 0, g))
        qs[rows_of(g), :] = q_ref[frm, :] * jnp.bfloat16(SCALE)
        fs[rows_of(g), :] = ft[frm, :]
        return 0

    def sort_targets(g, _):
        frm = rows_of(order_of(meta, 1, g))
        ks[rows_of(g), :] = k_ref[frm, :]
        bs[rows_of(g), :] = bt[frm, :]
        return 0

    lax.fori_loop(0, NU, sort_sources, 0, unroll=8)
    lax.fori_loop(0, NV, sort_targets, 0, unroll=8)
    mask_keys(ks, km)
    plain = largest_norm(qs, 2048) * largest_norm(ks, 1024) < SAFE * SAFE
    start = jnp.where(plain, 0.0, TOP)

    def sources(i, tile):
        us = pl.ds(pl.multiple_of(i * UB, UB), UB)
        first, full = chunk_bounds(meta, i)
        odd = first % 2
        mixed = jnp.maximum(full - first - odd + 1, 0) // 2
        pairs = (1024 // VC - first) // 2
        run_m[...] = jnp.full(run_m.shape, start, jnp.float32)
        run_t[...] = jnp.zeros_like(run_t)
        run_e[...] = jnp.zeros_like(run_e)

        def targets(j, width, masked, shift):
            rows = width * VC
            vs = pl.ds(pl.multiple_of(j * VC, VC), rows)
            n = tile + j - first
            for t in range(width):

                @pl.when(n + t >= SLOTS)
                def _():
                    flush(n + t - SLOTS).wait()

            counts = nt(bs[vs, :], fs[us, :])
            if masked:
                valid = chunk_valid(meta, pu_ref[pl.ds(i, 1), :], j, width)
            for h in range(HEADS):
                scores = nt(km[h, vs, :], qs[us, (h // 2) * 128 : (h // 2 + 1) * 128])
                if masked:
                    scores = jnp.where(valid, scores, NEG)
                for t in range(rows // SUB):
                    part = slice(t * SUB, (t + 1) * SUB)
                    s = scores[part].reshape(SUB // 8, 8, UB)
                    c = counts[part].reshape(SUB // 8, 8, UB)
                    if shift:
                        old = run_m[h]
                        new = jnp.maximum(old, jnp.max(s, axis=0))
                        w = jnp.exp(s - new[None])
                        shrink = jnp.exp(old - new)
                        run_m[h] = new
                        run_t[h] = run_t[h] * shrink + jnp.sum(w, axis=0)
                        run_e[h] = run_e[h] * shrink + jnp.sum(w * c, axis=0)
                    else:
                        new = jnp.zeros((8, UB), jnp.float32)
                        w = jnp.exp(s)
                        run_t[h] += jnp.sum(w, axis=0)
                        run_e[h] += jnp.sum(w * c, axis=0)
                    at = t * SUB // VC
                    inner = t % (VC // SUB)
                    held[(n + at) % SLOTS, h, inner * SUB : (inner + 1) * SUB, :] = w.reshape(
                        SUB, UB
                    ).astype(jnp.bfloat16)
                    ms[n + at, h, inner] = new
            for t in range(width):
                cs[n + t] = counts[t * VC : (t + 1) * VC]
                flush(n + t).start()

        def sweep(shift):
            def single(j, _):
                targets(first, 1, True, shift)
                return 0

            def mixed_pair(j, _):
                targets(first + odd + 2 * j, 2, True, shift)
                return 0

            def open_pair(j, _):
                targets(first + odd + 2 * j, 2, False, shift)
                return 0

            lax.fori_loop(0, odd, single, 0)
            lax.fori_loop(0, mixed, mixed_pair, 0)
            lax.fori_loop(mixed, pairs, open_pair, 0)

        @pl.when(plain)
        def _():
            sweep(False)

        @pl.when(jnp.logical_not(plain))
        def _():
            sweep(True)

        for h in range(HEADS):
            part_m = run_m[h]
            top = jnp.max(part_m, axis=0, keepdims=True)
            weight = jnp.exp(part_m - top)
            total = jnp.sum(run_t[h] * weight, axis=0, keepdims=True)
            expect = jnp.sum(run_e[h] * weight, axis=0, keepdims=True)
            some = total > 0.0
            safe = jnp.where(some, total, 1.0)
            log = jnp.where(some, top + jnp.log(safe), NEG)
            mean = expect / safe
            for t in range(UB // 128):
                at = i * (UB // 128) + t
                out[at, h : h + 1, :] = log[:, t * 128 : (t + 1) * 128]
                out[at, HEADS + h : HEADS + h + 1, :] = mean[:, t * 128 : (t + 1) * 128]
        return tile + 1024 // VC - first

    count = lax.fori_loop(0, 2048 // UB, sources, jnp.int32(0))
    for back in range(1, SLOTS + 1):

        @pl.when(count >= back)
        def _():
            flush(count - back).wait()


def stats(q, k, f, b, meta, pu):
    bf = jnp.bfloat16
    return pl.pallas_call(
        stats_kernel,
        in_specs=[VM] * 4 + [SM, VM],
        out_specs=[VM] * 3 + [pl.BlockSpec(memory_space=pl.ANY), VM, VM],
        out_shape=[
            jax.ShapeDtypeStruct((16, 16, 128), jnp.float32),
            jax.ShapeDtypeStruct((2048, 512), bf),
            jax.ShapeDtypeStruct((1024, 512), bf),
            jax.ShapeDtypeStruct((TILES, HEADS, VC, UB), bf),
            jax.ShapeDtypeStruct((TILES, HEADS, VC // SUB, 8, UB), jnp.float32),
            jax.ShapeDtypeStruct((TILES, VC, UB), jnp.float32),
        ],
        scratch_shapes=[
            pltpu.VMEM((2048, 256), bf),
            pltpu.VMEM((1024, 256), bf),
            pltpu.VMEM((HEADS, 1024, 128), bf),
            pltpu.VMEM((2048, 256), bf),
            pltpu.VMEM((1024, 256), bf),
            pltpu.VMEM((HEADS, 8, UB), jnp.float32),
            pltpu.VMEM((HEADS, 8, UB), jnp.float32),
            pltpu.VMEM((HEADS, 8, UB), jnp.float32),
            pltpu.VMEM((SLOTS, HEADS, VC, UB), bf),
            pltpu.SemaphoreType.DMA((SLOTS,)),
        ],
        compiler_params=pltpu.CompilerParams(vmem_limit_bytes=12 << 20),
        name="stats",
    )(q, k, f, b, meta, pu)


def grads_kernel(qs, kt, ws, ms, cs, meta, st, qg, kg, qacc, kacc, held, sem):
    def fetch(n):
        slot = n % SLOTS
        return pltpu.make_async_copy(ws.at[n], held.at[slot], sem.at[slot])

    count = jnp.int32(0)
    for i in range(2048 // UB):
        count += 1024 // VC - chunk_bounds(meta, i)[0]
    for n in range(SLOTS):

        @pl.when(count > n)
        def _():
            fetch(n).start()

    kacc[...] = jnp.zeros_like(kacc)

    def sources(i, tile):
        us = pl.ds(pl.multiple_of(i * UB, UB), UB)
        first, _ = chunk_bounds(meta, i)
        both = jnp.concatenate([st[i * (UB // 128) + t] for t in range(UB // 128)], axis=1)
        qacc[...] = jnp.zeros_like(qacc)

        def targets(j, width):
            rows = width * VC
            vs = pl.ds(pl.multiple_of(j * VC, VC), rows)
            n = tile + j - first
            for t in range(width):
                fetch(n + t).wait()
            low = lax.broadcasted_iota(jnp.int32, (rows, 128), 1) < HEAD
            pair = []
            for h in range(HEADS):
                log = both[h : h + 1]
                mean = both[HEADS + h : HEADS + h + 1]
                parts = []
                for t in range(rows // SUB):
                    at = t * SUB // VC
                    inner = t % (VC // SUB)
                    w = held[(n + at) % SLOTS, h, inner * SUB : (inner + 1) * SUB, :].astype(
                        jnp.float32
                    )
                    scale = jnp.exp(ms[n + at, h, inner] - log)
                    w = (w.reshape(SUB // 8, 8, UB) * scale[None]).reshape(SUB, UB)
                    counts = cs[n + at, inner * SUB : (inner + 1) * SUB, :]
                    parts.append((w * (mean - counts)).astype(jnp.bfloat16))
                g = jnp.concatenate(parts, axis=0)
                hs = slice(h * HEAD, (h + 1) * HEAD)
                qacc[hs, :] += nn(kt[hs, vs], g)
                pair.append(nn(g, qs[us, (h // 2) * 128 : (h // 2 + 1) * 128]))
                if h % 2:
                    cols = slice((h // 2) * 128, (h // 2 + 1) * 128)
                    kacc[vs, cols] += jnp.where(low, pair[-2], pair[-1])
            for t in range(width):

                @pl.when(n + t + SLOTS < count)
                def _():
                    fetch(n + t + SLOTS).start()

        odd = first % 2

        def single(j, _):
            targets(first, 1)
            return 0

        def double(j, _):
            targets(first + odd + 2 * j, 2)
            return 0

        lax.fori_loop(0, odd, single, 0)
        lax.fori_loop(0, (1024 // VC - first) // 2, double, 0)
        turned = (qacc[...] * SCALE).T.astype(jnp.bfloat16)
        for t in range(UB // GRAIN):
            to = order_of(meta, 0, i * (UB // GRAIN) + t)
            qg[rows_of(to), :] = turned[t * GRAIN : (t + 1) * GRAIN]
        return tile + 1024 // VC - first

    lax.fori_loop(0, 2048 // UB, sources, jnp.int32(0))

    def unsort(g, _):
        kg[rows_of(order_of(meta, 1, g)), :] = kacc[rows_of(g), :].astype(jnp.bfloat16)
        return 0

    lax.fori_loop(0, NV, unsort, 0, unroll=4)


def grads(qs, kt, ws, ms, cs, meta, st):
    bf = jnp.bfloat16
    return pl.pallas_call(
        grads_kernel,
        in_specs=[VM] * 2 + [pl.BlockSpec(memory_space=pl.ANY), VM, VM, SM, VM],
        out_specs=[VM] * 2,
        out_shape=[
            jax.ShapeDtypeStruct((2048, 512), bf),
            jax.ShapeDtypeStruct((1024, 512), bf),
        ],
        scratch_shapes=[
            pltpu.VMEM((512, UB), jnp.float32),
            pltpu.VMEM((1024, 512), jnp.float32),
            pltpu.VMEM((SLOTS, HEADS, VC, UB), bf),
            pltpu.SemaphoreType.DMA((SLOTS,)),
        ],
        compiler_params=pltpu.CompilerParams(vmem_limit_bytes=12 << 20),
        name="grads",
    )(qs, kt, ws, ms, cs, meta, st)


def in_order(places, index):
    n = places.shape[0]
    rank = jnp.sum((places[None, :] < places[:, None]).astype(jnp.int32), axis=1)
    hit = rank[None, :] == jnp.arange(n, dtype=jnp.int32)[:, None]
    return (
        jnp.sum(jnp.where(hit, index[None, :], 0), axis=1),
        jnp.sum(jnp.where(hit, places[None, :], 0), axis=1),
    )


def local(queries, keys, fwd_table, bwd_table, step_weight, block_order):
    row_id = lax.axis_index("row")
    col_id = lax.axis_index("col")
    block_order = lax.optimization_barrier(jnp.maximum(block_order, 0))
    line = lax.dynamic_slice_in_dim(block_order, row_id * NU, NU)
    pairs = block_order.reshape(4, 128)
    column = jnp.concatenate(
        [
            lax.dynamic_slice_in_dim(pairs, NU * odd + 4 * col_id, 4, axis=1).reshape(16)
            for odd in range(2)
        ]
    )
    at = jnp.arange(NV, dtype=jnp.int32)
    order_u, place_u = in_order(line, jnp.arange(NU, dtype=jnp.int32))
    order_v, place_v = in_order(column, at % 16 // 4 * 8 + at // 16 * 4 + at % 4)
    meta = jnp.concatenate([order_u, order_v, place_u, place_v])
    offsets = jnp.arange(GRAIN, dtype=jnp.int32)
    pu = (place_u[:, None] * GRAIN + offsets[None, :]).reshape(8, 256)
    here = [
        pltpu.with_memory_space_constraint(a, pltpu.MemorySpace.HBM)
        for a in (queries, keys, fwd_table, bwd_table, step_weight)
    ]
    q, k, f, b = gather(*here)
    part, qs, ks, ws, ms, cs = stats(
        q.reshape(2048, 512),
        k.reshape(1024, 512),
        f.reshape(16, 256, 128),
        b.reshape(8, 256, 128),
        meta,
        pu,
    )
    st, kt = merge(part, ks)
    qg, kg = grads(qs, kt, ws, ms, cs, meta, st)
    own, last = reduce(qg.reshape(4, 2, 2, 128, 512), kg.reshape(2, 4, 128, 512))
    return own[0] + last[0].astype(jnp.float32), own[1] + last[1].astype(jnp.float32)


def solution(mesh):
    return jax.shard_map(
        local,
        mesh=mesh,
        in_specs=(
            P(("row", "col"), None),
            P(("row", "col"), None),
            P(("row", "col"), None),
            P(("row", "col"), None),
            P(("row", "col")),
            P(),
        ),
        out_specs=(P(("row", "col"), None), P(("row", "col"), None)),
        check_vma=False,
    )
```

```python
import jax
import jax.numpy as jnp
from jax import lax
from jax.experimental import pallas as pl
from jax.experimental.pallas import tpu as pltpu
from jax.sharding import PartitionSpec as P

HEADS = 8
HEAD = 64
GRAIN = 32
SCALE = HEAD**-0.5
LOG_HEADS = 2.0794415416798357
NEG = -1e30
SAFE = 40.0
TOP = -1e29
NU = 64
NV = 32
TILES = 64
SLOTS = 4
UB = 256
VC = 128
SUB = 128
MESH = pl.DeviceIdType.MESH
VM = pl.BlockSpec(memory_space=pltpu.VMEM)
SM = pl.BlockSpec(memory_space=pltpu.SMEM)
HB = pl.BlockSpec(memory_space=pltpu.MemorySpace.HBM)


def nn(a, b):
    return lax.dot_general(a, b, (((1,), (0,)), ((), ())), preferred_element_type=jnp.float32)


def nt(a, b):
    return lax.dot_general(a, b, (((1,), (1,)), ((), ())), preferred_element_type=jnp.float32)


def remote(src, dst, send, recv, peer):
    return pltpu.make_async_remote_copy(
        src_ref=src, dst_ref=dst, send_sem=send, recv_sem=recv, device_id=peer, device_id_type=MESH
    )


def greet(peers):
    barrier = pltpu.get_barrier_semaphore()
    for peer in peers:
        pl.semaphore_signal(barrier, inc=1, device_id=peer, device_id_type=MESH)


def enter(peers):
    greet(peers)
    pl.semaphore_wait(pltpu.get_barrier_semaphore(), len(peers))


class Sends:
    def __init__(self, sems):
        self.sems = sems
        self.started = []

    def start(self, src, dst, recv, peer):
        copy = remote(src, dst, self.sems.at[len(self.started)], recv, peer)
        copy.start()
        self.started.append(copy)

    def drain(self):
        for copy in self.started:
            copy.wait_send()


def gather_kernel(
    q, k, fwd, bwd, weight, qa, ka, fa, ba, fv, bv, sf, sb, send, recv_q, recv_f, recv_k, recv_b, in_f, in_b, own
):
    row, col = lax.axis_index("row"), lax.axis_index("col")
    x, yh, core = col // 4, (col // 2) % 2, col % 2
    yl, z = row // 4, row % 4

    def at(r=None, c=None):
        return {"row": row if r is None else r, "col": col if c is None else c}

    def cslot(xx, yy, cc):
        return xx * 4 + yy * 2 + cc

    peers = [at(r=(row + d) % 8) for d in range(1, 8)] + [at(c=(col + d) % 16) for d in range(1, 16)]
    greet(peers)
    tables = [pltpu.make_async_copy(fwd, fv, own.at[0]), pltpu.make_async_copy(bwd, bv, own.at[1])]
    local = [
        pltpu.make_async_copy(q, qa.at[col], own.at[2]),
        pltpu.make_async_copy(k, ka.at[row], own.at[3]),
    ]
    for copy in tables + local:
        copy.start()
    step = jnp.where(lax.broadcasted_iota(jnp.int32, (2, 128), 0) == 0, weight[0], weight[1])
    tables[0].wait()
    tables[1].wait()
    for r in range(8):
        for c in range(16):
            cut = slice((r * 16 + c) * 128, (r * 16 + c + 1) * 128)
            sf[r, c] = fv[:, cut]
            sb[r, c] = (bv[:, cut].astype(jnp.float32) * step).astype(jnp.bfloat16)
    pl.semaphore_wait(pltpu.get_barrier_semaphore(), len(peers))
    sends = Sends(send)
    local += [
        pltpu.make_async_copy(sf.at[row], fa.at[:, col, row], own.at[4]),
        pltpu.make_async_copy(sb.at[:, col], ba.at[:, col, row], own.at[5]),
    ]
    local[2].start()
    local[3].start()
    for d in range(1, 16):
        to = (col + d) % 16
        sends.start(sb.at[:, to], ba.at[:, col, row], in_b.at[col], at(c=to))
    for d in range(1, 8):
        to = (row + d) % 8
        sends.start(sf.at[to], fa.at[:, col, row], in_f.at[row], at(r=to))

    def q_part(slot, half=None):
        return qa.at[slot] if half is None else qa.at[slot, pl.ds(half * 64, 64)]

    def f_part(slot, half=None):
        return fa.at[:, slot] if half is None else fa.at[pl.ds(half * 8, 8), slot]

    def k_part(slot, half=None):
        return ka.at[slot] if half is None else ka.at[slot, pl.ds(half * 64, 64)]

    def b_part(slot, half=None):
        return ba.at[:, :, slot] if half is None else ba.at[pl.ds(half * 4, 4), :, slot]

    def src_slot(dx, dy, cc=None):
        return cslot((x + dx) % 4, (yh + dy) % 2, core if cc is None else cc)

    def tgt_slot(dz, dy):
        return ((yl + dy) % 2) * 4 + (z + dz) % 4

    def src_dev(dx, dy, dc=0):
        return at(c=cslot((x + dx) % 4, (yh + dy) % 2, (core + dc) % 2))

    def tgt_dev(dz, dy):
        return at(r=tgt_slot(dz, dy))

    source = (src_slot, src_dev, True)
    target = (tgt_slot, tgt_dev, False)
    streams = {
        "q": (q_part, recv_q, source),
        "f": (f_part, recv_f, source),
        "k": (k_part, recv_k, target),
        "b": (b_part, recv_b, target),
    }

    def push(kind, slot, peer, half=None):
        part, recv, _ = streams[kind]
        ref = part(slot, half)
        sends.start(ref, ref, recv.at[slot, 0 if half is None else half], peer)

    def arrived(kind, slot, half=None):
        part, recv, _ = streams[kind]
        ref = part(slot, half)
        remote(ref, ref, send.at[0], recv.at[slot, 0 if half is None else half], at()).wait_recv()

    def first(kind):
        slot_of, dev_of, pair = streams[kind][2]
        mine = slot_of(0, 0)
        push(kind, mine, dev_of(0, 1))
        push(kind, mine, dev_of(1, 0))
        push(kind, mine, dev_of(3, 0))
        if pair:
            push(kind, mine, dev_of(0, 0, 1))

    def second(kind):
        slot_of, dev_of, pair = streams[kind][2]
        other = slot_of(0, 1)
        arrived(kind, other)
        push(kind, other, dev_of(1, 0))
        push(kind, other, dev_of(3, 0))
        if pair:
            push(kind, other, dev_of(0, 0, 1))

    def relay(kind, dy):
        slot_of, dev_of, pair = streams[kind][2]
        for step, half in ((3, 0), (1, 1)):
            slot = slot_of(step, dy)
            arrived(kind, slot)
            push(kind, slot, dev_of(4 - step, 0), half)
            if pair:
                push(kind, slot, dev_of(0, 0, 1))

    def last(kind, dy):
        slot_of, dev_of, pair = streams[kind][2]
        slot = slot_of(2, dy)
        arrived(kind, slot, 0)
        arrived(kind, slot, 1)
        if pair:
            push(kind, slot, dev_of(0, 0, 1))

    local[0].wait()
    local[1].wait()
    first("q")
    first("k")
    local[2].wait()
    for d in range(1, 8):
        frm = (row + d) % 8
        ref = fa.at[:, col, frm]
        remote(ref, ref, send.at[0], in_f.at[frm], at()).wait_recv()
    first("f")
    local[3].wait()
    for d in range(1, 16):
        frm = (col + d) % 16
        ref = ba.at[:, frm, row]
        remote(ref, ref, send.at[0], in_b.at[frm], at()).wait_recv()
    first("b")
    relay("k", 0)
    relay("q", 0)
    second("k")
    second("q")
    relay("b", 0)
    relay("f", 0)
    second("b")
    second("f")
    relay("k", 1)
    relay("q", 1)
    relay("b", 1)
    relay("f", 1)
    for dy in range(2):
        for kind in ("k", "q", "b", "f"):
            last(kind, dy)
    for kind in ("q", "f"):
        for dx in range(4):
            for dy in range(2):
                arrived(kind, src_slot(dx, dy, 1 - core))
    sends.drain()


def gather(q, k, fwd, bwd, weight):
    bf = jnp.bfloat16
    return pl.pallas_call(
        gather_kernel,
        in_specs=[HB] * 4 + [SM],
        out_specs=[VM] * 4,
        out_shape=[
            jax.ShapeDtypeStruct((16, 128, 512), bf),
            jax.ShapeDtypeStruct((8, 128, 512), bf),
            jax.ShapeDtypeStruct((16, 16, 8, 2, 128), bf),
            jax.ShapeDtypeStruct((8, 16, 8, 2, 128), bf),
        ],
        scratch_shapes=[
            pltpu.VMEM((2, 16384), bf),
            pltpu.VMEM((2, 16384), bf),
            pltpu.VMEM((8, 16, 2, 128), bf),
            pltpu.VMEM((8, 16, 2, 128), bf),
            pltpu.SemaphoreType.DMA((100,)),
            pltpu.SemaphoreType.DMA((16, 2)),
            pltpu.SemaphoreType.DMA((16, 2)),
            pltpu.SemaphoreType.DMA((8, 2)),
            pltpu.SemaphoreType.DMA((8, 2)),
            pltpu.SemaphoreType.DMA((8,)),
            pltpu.SemaphoreType.DMA((16,)),
            pltpu.SemaphoreType.DMA((6,)),
        ],
        compiler_params=pltpu.CompilerParams(
            collective_id=0, has_side_effects=True, vmem_limit_bytes=16 << 20
        ),
        name="gather",
    )(q, k, fwd, bwd, weight)


def merge_kernel(part, ks, out, kt, landed, mine, send, recv, recv2, own):
    row, col = lax.axis_index("row"), lax.axis_index("col")
    peers = [{"row": row, "col": (col + d) % 16} for d in range(1, 16)]
    enter(peers)
    sends = Sends(send)
    keep = pltpu.make_async_copy(part.at[col], landed.at[col], own.at[0])
    keep.start()
    for d, peer in enumerate(peers):
        sends.start(part.at[peer["col"]], landed.at[col], recv.at[col], peer)
    for block in range(8):
        rows = slice(block * 128, (block + 1) * 128)
        kt[:, rows] = ks[rows, :].T
    keep.wait()
    for peer in peers:
        ref = landed.at[peer["col"]]
        remote(ref, ref, send.at[0], recv.at[peer["col"]], peer).wait_recv()
    logs = landed[:, 0:8]
    top = jnp.max(logs, axis=0)
    weight = jnp.exp(logs - top[None])
    total = jnp.sum(weight, axis=0)
    mean = jnp.sum(weight * landed[:, 8:16], axis=0) / total
    mine[0:8, :] = top + jnp.log(total) + LOG_HEADS
    mine[8:16, :] = mean
    keep = pltpu.make_async_copy(mine, out.at[col], own.at[1])
    keep.start()
    for peer in peers:
        sends.start(mine, out.at[col], recv2.at[col], peer)
    keep.wait()
    for peer in peers:
        ref = out.at[peer["col"]]
        remote(ref, ref, send.at[0], recv2.at[peer["col"]], peer).wait_recv()
    sends.drain()


def merge(part, ks):
    return pl.pallas_call(
        merge_kernel,
        in_specs=[VM] * 2,
        out_specs=[VM] * 2,
        out_shape=[
            jax.ShapeDtypeStruct((16, 16, 128), jnp.float32),
            jax.ShapeDtypeStruct((512, 1024), jnp.bfloat16),
        ],
        scratch_shapes=[
            pltpu.VMEM((16, 16, 128), jnp.float32),
            pltpu.VMEM((16, 128), jnp.float32),
            pltpu.SemaphoreType.DMA((30,)),
            pltpu.SemaphoreType.DMA((16,)),
            pltpu.SemaphoreType.DMA((16,)),
            pltpu.SemaphoreType.DMA((2,)),
        ],
        compiler_params=pltpu.CompilerParams(
            collective_id=1, has_side_effects=True, vmem_limit_bytes=4 << 20
        ),
        name="merge",
    )(part, ks)


def reduce_kernel(
    qp, kp, own, last, pair_in, pair_sum, hop_q, acc_q, fin_q, hop_k, acc_k, fin_k, out_q, out_k, send, recv
):
    row, col = lax.axis_index("row"), lax.axis_index("col")
    x, yh, core = col // 4, (col // 2) % 2, col % 2
    yl, z = row // 4, row % 4
    f32 = jnp.float32
    qo, ko, last_q, last_k = own.at[0], own.at[1], last.at[0], last.at[1]

    def q_dev(xx, yy, cc):
        return {"row": row, "col": xx * 4 + yy * 2 + cc}

    def k_dev(yy, zz):
        return {"row": yy * 4 + zz, "col": col}

    sibling = q_dev(x, yh, 1 - core)
    pair_y = q_dev(x, 1 - yh, core)
    pair_r = k_dev(1 - yl, z)
    sides_q = (q_dev((x + 1) % 4, yh, core), q_dev((x + 3) % 4, yh, core))
    sides_k = (k_dev(yl, (z + 1) % 4), k_dev(yl, (z + 3) % 4))
    enter([sibling, pair_y, pair_r, *sides_q, *sides_k])
    sends = Sends(send)
    parts = [pl.ds(n * 64, 64) for n in range(2)]

    def landed(ref, sem):
        remote(ref, ref, send.at[0], sem, sibling).wait_recv()
        return ref

    class Ring:
        def __init__(self, block, me, sides, hop, acc, fin, which):
            self.block, self.me, self.sides = block, me, sides
            self.hop, self.acc, self.fin, self.which = hop, acc, fin, which

        def at(self, step, half):
            return self.block((self.me + step) % 4, half)

        def far(self):
            for half in range(2):
                sends.start(
                    self.at(2, half), self.hop.at[half], recv.at[self.which, half], self.sides[half]
                )

        def near(self):
            for side, step in ((0, 1), (1, 3)):
                sends.start(
                    self.at(step, 1 - side),
                    self.fin.at[side],
                    recv.at[self.which, 2 + side],
                    self.sides[side],
                )

        def turn(self):
            for side, step in ((0, 1), (1, 3)):
                came = landed(self.hop.at[side], recv.at[self.which, side])[...].astype(f32)
                self.acc[side] = (came + self.at(step, side)[...].astype(f32)).astype(jnp.bfloat16)
                for n, rows in enumerate(parts):
                    sends.start(
                        self.acc.at[side, rows],
                        self.fin.at[2 + side, rows],
                        recv.at[self.which, 4 + 2 * side + n],
                        self.sides[side],
                    )

        def near_arrive(self):
            for slot in range(2):
                landed(self.fin.at[slot], recv.at[self.which, 2 + slot])

        def arrive(self, n):
            for side in range(2):
                landed(self.fin.at[2 + side, parts[n]], recv.at[self.which, 4 + 2 * side + n])

        def total(self, half, rows):
            return (
                self.at(0, half)[rows, :].astype(f32)
                + self.fin[1 - half, rows, :].astype(f32)
                + self.fin[2 + half, rows, :].astype(f32)
            )

    ring_q = Ring(lambda xx, half: pair_sum.at[xx, half], x, sides_q, hop_q, acc_q, fin_q, 1)
    ring_k = Ring(lambda zz, half: kp.at[half, zz], z, sides_k, hop_k, acc_k, fin_k, 2)
    order_x = [(x + d) % 4 for d in (2, 1, 3, 0)]
    for xx in order_x:
        sends.start(qp.at[xx, :, 1 - core], pair_in.at[xx], recv.at[0, xx], sibling)
    ring_k.far()
    ring_k.near()
    for n, xx in enumerate(order_x):
        came = landed(pair_in.at[xx], recv.at[0, xx])[...].astype(f32)
        pair_sum[xx] = (qp[xx, :, core].astype(f32) + came).astype(jnp.bfloat16)
        if n == 0:
            ring_q.far()
        elif n == 2:
            ring_q.near()
    ring_k.turn()
    ring_q.turn()

    def across(ring, pos, stage, last, out, peer, slot, n):
        rows = parts[n]
        ring.arrive(n)
        for half in range(2):

            @pl.when(pos != half)
            def _():
                stage[rows, :] = ring.total(half, rows).astype(jnp.bfloat16)

            @pl.when(pos == half)
            def _():
                out[rows, :] = ring.total(half, rows)

        sends.start(stage.at[rows], last.at[rows], recv.at[3, 2 * slot + n], peer)

    ring_k.near_arrive()
    ring_q.near_arrive()
    for n in range(2):
        across(ring_k, yl, out_k, last_k, ko, pair_r, 0, n)
        across(ring_q, yh, out_q, last_q, qo, pair_y, 1, n)
    for n in range(2):
        landed(last_k.at[parts[n]], recv.at[3, n])
        landed(last_q.at[parts[n]], recv.at[3, 2 + n])
    sends.drain()


def reduce(qp, kp):
    bf = jnp.bfloat16
    block = (128, 512)
    return pl.pallas_call(
        reduce_kernel,
        in_specs=[VM] * 2,
        out_specs=[VM] * 2,
        out_shape=[
            jax.ShapeDtypeStruct((2, *block), jnp.float32),
            jax.ShapeDtypeStruct((2, *block), bf),
        ],
        scratch_shapes=[
            pltpu.VMEM((4, 2, *block), bf),
            pltpu.VMEM((4, 2, *block), bf),
            pltpu.VMEM((2, *block), bf),
            pltpu.VMEM((2, *block), bf),
            pltpu.VMEM((4, *block), bf),
            pltpu.VMEM((2, *block), bf),
            pltpu.VMEM((2, *block), bf),
            pltpu.VMEM((4, *block), bf),
            pltpu.VMEM(block, bf),
            pltpu.VMEM(block, bf),
            pltpu.SemaphoreType.DMA((24,)),
            pltpu.SemaphoreType.DMA((4, 8)),
        ],
        compiler_params=pltpu.CompilerParams(
            collective_id=2, has_side_effects=True, vmem_limit_bytes=16 << 20
        ),
        name="reduce",
    )(qp, kp)


def mask_keys(ks, km):
    half = lax.broadcasted_iota(jnp.int32, (128, 128), 1) < HEAD
    for block in range(8):
        rows = slice(block * 128, (block + 1) * 128)
        for h in range(HEADS):
            kk = ks[rows, (h // 2) * 128 : (h // 2 + 1) * 128]
            keep = half if h % 2 == 0 else jnp.logical_not(half)
            km[h, rows, :] = jnp.where(keep, kk, jnp.zeros_like(kk))


def order_of(meta, which, g):
    return meta[which * NU + g]


def place_of(meta, which, g):
    return meta[NU + NV + which * NU + g]


def rows_of(g):
    return pl.ds(pl.multiple_of(g * GRAIN, GRAIN), GRAIN)


def chunk_bounds(meta, i):
    low = place_of(meta, 0, i * (UB // GRAIN))
    high = place_of(meta, 0, (i + 1) * (UB // GRAIN) - 1)
    per = VC // GRAIN
    first = jnp.int32(0)
    full = jnp.int32(0)
    for j in range(NV // per):
        first += (place_of(meta, 1, (j + 1) * per - 1) < low).astype(jnp.int32)
        full += (place_of(meta, 1, j * per) <= high).astype(jnp.int32)
    return first, full


def source_places(meta, i):
    lane = lax.broadcasted_iota(jnp.int32, (1, UB), 1)
    pu = lane % GRAIN
    for t in range(UB // GRAIN):
        place = GRAIN * place_of(meta, 0, i * (UB // GRAIN) + t)
        pu += jnp.where(lane // GRAIN == t, place, 0)
    return pu


def chunk_valid(meta, pu, j, width):
    off = lax.broadcasted_iota(jnp.int32, (GRAIN, UB), 0)
    per = VC // GRAIN
    pv = jnp.concatenate(
        [off + GRAIN * place_of(meta, 1, j * per + t) for t in range(width * per)], axis=0
    )
    return pv >= pu


def largest_norm(ref, n):
    width = HEADS * HEAD
    head = lax.broadcasted_iota(jnp.int32, (16, width), 1) // HEAD
    pick = (head == lax.broadcasted_iota(jnp.int32, (16, width), 0)).astype(jnp.bfloat16)
    best = jnp.zeros((16, 256), jnp.float32)
    for block in range(n // 256):
        rows = ref[block * 256 : (block + 1) * 256, :]
        best = jnp.maximum(best, nt(pick, rows * rows))
    return jnp.max(best) * 1.02


def stats_kernel(
    q_ref, k_ref, f_ref, b_ref, meta, out, qs, ks, ws, ms, cs, fs, bs, km, ft, bt, run_m, run_t, run_e, held, sem
):
    def flush(n):
        slot = n % SLOTS
        return pltpu.make_async_copy(held.at[slot], ws.at[n], sem.at[slot])

    for block in range(16):
        ft[block * 128 : (block + 1) * 128, :] = f_ref[block].T
    for block in range(8):
        bt[block * 128 : (block + 1) * 128, :] = b_ref[block].T

    def sort_sources(g, _):
        frm = rows_of(order_of(meta, 0, g))
        qs[rows_of(g), :] = q_ref[frm, :] * jnp.bfloat16(SCALE)
        fs[rows_of(g), :] = ft[frm, :]
        return 0

    def sort_targets(g, _):
        frm = rows_of(order_of(meta, 1, g))
        ks[rows_of(g), :] = k_ref[frm, :]
        bs[rows_of(g), :] = bt[frm, :]
        return 0

    lax.fori_loop(0, NU, sort_sources, 0, unroll=8)
    lax.fori_loop(0, NV, sort_targets, 0, unroll=8)
    mask_keys(ks, km)
    plain = largest_norm(qs, 2048) * largest_norm(ks, 1024) < SAFE * SAFE
    start = jnp.where(plain, 0.0, TOP)

    def sources(i, tile):
        us = pl.ds(pl.multiple_of(i * UB, UB), UB)
        first, full = chunk_bounds(meta, i)
        odd = first % 2
        mixed = jnp.maximum(full - first - odd + 1, 0) // 2
        pairs = (1024 // VC - first) // 2
        run_m[...] = jnp.full(run_m.shape, start, jnp.float32)
        run_t[...] = jnp.zeros_like(run_t)
        run_e[...] = jnp.zeros_like(run_e)

        def targets(j, width, masked, shift):
            rows = width * VC
            vs = pl.ds(pl.multiple_of(j * VC, VC), rows)
            n = tile + j - first
            for t in range(width):

                @pl.when(n + t >= SLOTS)
                def _():
                    flush(n + t - SLOTS).wait()

            counts = nt(bs[vs, :], fs[us, :])
            if masked:
                valid = chunk_valid(meta, source_places(meta, i), j, width)
            for h in range(HEADS):
                scores = nt(km[h, vs, :], qs[us, (h // 2) * 128 : (h // 2 + 1) * 128])
                if masked:
                    scores = jnp.where(valid, scores, NEG)
                for t in range(rows // SUB):
                    part = slice(t * SUB, (t + 1) * SUB)
                    s = scores[part].reshape(SUB // 8, 8, UB)
                    c = counts[part].reshape(SUB // 8, 8, UB)
                    if shift:
                        old = run_m[h]
                        new = jnp.maximum(old, jnp.max(s, axis=0))
                        w = jnp.exp(s - new[None])
                        shrink = jnp.exp(old - new)
                        run_m[h] = new
                        run_t[h] = run_t[h] * shrink + jnp.sum(w, axis=0)
                        run_e[h] = run_e[h] * shrink + jnp.sum(w * c, axis=0)
                    else:
                        new = jnp.zeros((8, UB), jnp.float32)
                        w = jnp.exp(s)
                        run_t[h] += jnp.sum(w, axis=0)
                        run_e[h] += jnp.sum(w * c, axis=0)
                    at = t * SUB // VC
                    inner = t % (VC // SUB)
                    held[(n + at) % SLOTS, h, inner * SUB : (inner + 1) * SUB, :] = w.reshape(
                        SUB, UB
                    ).astype(jnp.bfloat16)
                    ms[n + at, h, inner] = new
            for t in range(width):
                cs[n + t] = counts[t * VC : (t + 1) * VC]
                flush(n + t).start()

        def sweep(shift):
            def single(j, _):
                targets(first, 1, True, shift)
                return 0

            def mixed_pair(j, _):
                targets(first + odd + 2 * j, 2, True, shift)
                return 0

            def open_pair(j, _):
                targets(first + odd + 2 * j, 2, False, shift)
                return 0

            lax.fori_loop(0, odd, single, 0)
            lax.fori_loop(0, mixed, mixed_pair, 0)
            lax.fori_loop(mixed, pairs, open_pair, 0)

        @pl.when(plain)
        def _():
            sweep(False)

        @pl.when(jnp.logical_not(plain))
        def _():
            sweep(True)

        for h in range(HEADS):
            part_m = run_m[h]
            top = jnp.max(part_m, axis=0, keepdims=True)
            weight = jnp.exp(part_m - top)
            total = jnp.sum(run_t[h] * weight, axis=0, keepdims=True)
            expect = jnp.sum(run_e[h] * weight, axis=0, keepdims=True)
            some = total > 0.0
            safe = jnp.where(some, total, 1.0)
            log = jnp.where(some, top + jnp.log(safe), NEG)
            mean = expect / safe
            for t in range(UB // 128):
                at = i * (UB // 128) + t
                out[at, h : h + 1, :] = log[:, t * 128 : (t + 1) * 128]
                out[at, HEADS + h : HEADS + h + 1, :] = mean[:, t * 128 : (t + 1) * 128]
        return tile + 1024 // VC - first

    count = lax.fori_loop(0, 2048 // UB, sources, jnp.int32(0))
    for back in range(1, SLOTS + 1):

        @pl.when(count >= back)
        def _():
            flush(count - back).wait()


def stats(q, k, f, b, meta):
    bf = jnp.bfloat16
    return pl.pallas_call(
        stats_kernel,
        in_specs=[VM] * 4 + [SM],
        out_specs=[VM] * 3 + [pl.BlockSpec(memory_space=pl.ANY), VM, VM],
        out_shape=[
            jax.ShapeDtypeStruct((16, 16, 128), jnp.float32),
            jax.ShapeDtypeStruct((2048, 512), bf),
            jax.ShapeDtypeStruct((1024, 512), bf),
            jax.ShapeDtypeStruct((TILES, HEADS, VC, UB), bf),
            jax.ShapeDtypeStruct((TILES, HEADS, VC // SUB, 8, UB), jnp.float32),
            jax.ShapeDtypeStruct((TILES, VC, UB), jnp.float32),
        ],
        scratch_shapes=[
            pltpu.VMEM((2048, 256), bf),
            pltpu.VMEM((1024, 256), bf),
            pltpu.VMEM((HEADS, 1024, 128), bf),
            pltpu.VMEM((2048, 256), bf),
            pltpu.VMEM((1024, 256), bf),
            pltpu.VMEM((HEADS, 8, UB), jnp.float32),
            pltpu.VMEM((HEADS, 8, UB), jnp.float32),
            pltpu.VMEM((HEADS, 8, UB), jnp.float32),
            pltpu.VMEM((SLOTS, HEADS, VC, UB), bf),
            pltpu.SemaphoreType.DMA((SLOTS,)),
        ],
        compiler_params=pltpu.CompilerParams(vmem_limit_bytes=12 << 20),
        name="stats",
    )(q, k, f, b, meta)


def grads_kernel(qs, kt, ws, ms, cs, meta, st, qg, kg, qacc, kacc, held, sem):
    def fetch(n):
        slot = n % SLOTS
        return pltpu.make_async_copy(ws.at[n], held.at[slot], sem.at[slot])

    count = jnp.int32(0)
    for i in range(2048 // UB):
        count += 1024 // VC - chunk_bounds(meta, i)[0]
    for n in range(SLOTS):

        @pl.when(count > n)
        def _():
            fetch(n).start()

    kacc[...] = jnp.zeros_like(kacc)

    def sources(i, tile):
        us = pl.ds(pl.multiple_of(i * UB, UB), UB)
        first, _ = chunk_bounds(meta, i)
        both = jnp.concatenate([st[i * (UB // 128) + t] for t in range(UB // 128)], axis=1)
        qacc[...] = jnp.zeros_like(qacc)

        def targets(j, width):
            rows = width * VC
            vs = pl.ds(pl.multiple_of(j * VC, VC), rows)
            n = tile + j - first
            for t in range(width):
                fetch(n + t).wait()
            low = lax.broadcasted_iota(jnp.int32, (rows, 128), 1) < HEAD
            pair = []
            for h in range(HEADS):
                log = both[h : h + 1]
                mean = both[HEADS + h : HEADS + h + 1]
                parts = []
                for t in range(rows // SUB):
                    at = t * SUB // VC
                    inner = t % (VC // SUB)
                    w = held[(n + at) % SLOTS, h, inner * SUB : (inner + 1) * SUB, :].astype(
                        jnp.float32
                    )
                    scale = jnp.exp(ms[n + at, h, inner] - log)
                    w = (w.reshape(SUB // 8, 8, UB) * scale[None]).reshape(SUB, UB)
                    counts = cs[n + at, inner * SUB : (inner + 1) * SUB, :]
                    parts.append((w * (mean - counts)).astype(jnp.bfloat16))
                g = jnp.concatenate(parts, axis=0)
                hs = slice(h * HEAD, (h + 1) * HEAD)
                qacc[hs, :] += nn(kt[hs, vs], g)
                pair.append(nn(g, qs[us, (h // 2) * 128 : (h // 2 + 1) * 128]))
                if h % 2:
                    cols = slice((h // 2) * 128, (h // 2 + 1) * 128)
                    kacc[vs, cols] += jnp.where(low, pair[-2], pair[-1])
            for t in range(width):

                @pl.when(n + t + SLOTS < count)
                def _():
                    fetch(n + t + SLOTS).start()

        odd = first % 2

        def single(j, _):
            targets(first, 1)
            return 0

        def double(j, _):
            targets(first + odd + 2 * j, 2)
            return 0

        lax.fori_loop(0, odd, single, 0)
        lax.fori_loop(0, (1024 // VC - first) // 2, double, 0)
        turned = (qacc[...] * SCALE).T.astype(jnp.bfloat16)
        for t in range(UB // GRAIN):
            to = order_of(meta, 0, i * (UB // GRAIN) + t)
            qg[rows_of(to), :] = turned[t * GRAIN : (t + 1) * GRAIN]
        return tile + 1024 // VC - first

    lax.fori_loop(0, 2048 // UB, sources, jnp.int32(0))

    def unsort(g, _):
        kg[rows_of(order_of(meta, 1, g)), :] = kacc[rows_of(g), :].astype(jnp.bfloat16)
        return 0

    lax.fori_loop(0, NV, unsort, 0, unroll=4)


def grads(qs, kt, ws, ms, cs, meta, st):
    bf = jnp.bfloat16
    return pl.pallas_call(
        grads_kernel,
        in_specs=[VM] * 2 + [pl.BlockSpec(memory_space=pl.ANY), VM, VM, SM, VM],
        out_specs=[VM] * 2,
        out_shape=[
            jax.ShapeDtypeStruct((2048, 512), bf),
            jax.ShapeDtypeStruct((1024, 512), bf),
        ],
        scratch_shapes=[
            pltpu.VMEM((512, UB), jnp.float32),
            pltpu.VMEM((1024, 512), jnp.float32),
            pltpu.VMEM((SLOTS, HEADS, VC, UB), bf),
            pltpu.SemaphoreType.DMA((SLOTS,)),
        ],
        compiler_params=pltpu.CompilerParams(vmem_limit_bytes=12 << 20),
        name="grads",
    )(qs, kt, ws, ms, cs, meta, st)


def in_order(places, index):
    n = places.shape[0]
    rank = jnp.sum((places[None, :] < places[:, None]).astype(jnp.int32), axis=1)
    hit = rank[None, :] == jnp.arange(n, dtype=jnp.int32)[:, None]
    return (
        jnp.sum(jnp.where(hit, index[None, :], 0), axis=1),
        jnp.sum(jnp.where(hit, places[None, :], 0), axis=1),
    )


def local(queries, keys, fwd_table, bwd_table, step_weight, block_order):
    row_id = lax.axis_index("row")
    col_id = lax.axis_index("col")
    block_order = lax.optimization_barrier(jnp.maximum(block_order, 0))
    line = lax.dynamic_slice_in_dim(block_order, row_id * NU, NU)
    pairs = block_order.reshape(4, 128)
    column = jnp.concatenate(
        [
            lax.dynamic_slice_in_dim(pairs, NU * odd + 4 * col_id, 4, axis=1).reshape(16)
            for odd in range(2)
        ]
    )
    at = jnp.arange(NV, dtype=jnp.int32)
    order_u, place_u = in_order(line, jnp.arange(NU, dtype=jnp.int32))
    order_v, place_v = in_order(column, at % 16 // 4 * 8 + at // 16 * 4 + at % 4)
    meta = jnp.concatenate([order_u, order_v, place_u, place_v])
    here = [
        pltpu.with_memory_space_constraint(a, pltpu.MemorySpace.HBM)
        for a in (queries, keys, fwd_table, bwd_table, step_weight)
    ]
    q, k, f, b = gather(*here)
    part, qs, ks, ws, ms, cs = stats(
        q.reshape(2048, 512),
        k.reshape(1024, 512),
        f.reshape(16, 256, 128),
        b.reshape(8, 256, 128),
        meta,
    )
    st, kt = merge(part, ks)
    qg, kg = grads(qs, kt, ws, ms, cs, meta, st)
    own, last = reduce(qg.reshape(4, 2, 2, 128, 512), kg.reshape(2, 4, 128, 512))
    return own[0] + last[0].astype(jnp.float32), own[1] + last[1].astype(jnp.float32)


def solution(mesh):
    return jax.shard_map(
        local,
        mesh=mesh,
        in_specs=(
            P(("row", "col"), None),
            P(("row", "col"), None),
            P(("row", "col"), None),
            P(("row", "col"), None),
            P(("row", "col")),
            P(),
        ),
        out_specs=(P(("row", "col"), None), P(("row", "col"), None)),
        check_vma=False,
    )
```
